128 devices in a mesh: segment: 8 (over z, core), blk: 16 (over x, y).
Axes of the slice: x: 4, y: 4, z: 4, core: 2. Of those that a mesh axis runs over, the one named last changes fastest.
Arguments:
- layer_inputs: bfloat16 [8, 6, 2048, 256], P('segment', None, 'blk'), may hold values from -6 to 6
- final_cot: bfloat16 [6, 2048, 256], P(None, 'blk'), may hold values from -6 to 6
- attn_weights: bfloat16 [8, 4, 256, 256], P('segment'), may hold values from -0.375 to 0.375
- norm_gain: float32 [8, 256], P('segment'), may hold values from 0.5 to 1.5
- pair_list: int32 [16, 8], replicated, may hold values from 0 to 15, as said below
- pair_count: int32 [16], replicated, may hold values from 2 to 8, as said below
Outputs:
- layer_cots: bfloat16 [8, 6, 2048, 256], P('segment', None, 'blk')
- weight_grads: float32 [8, 4, 256, 256], P('segment')
- gain_grads: float32 [8, 256], P('segment')
The draws below stay inside these ranges and needn't reach their ends.
Inputs may be any that keep to these rules, and one draw needn't show every extreme that they name: `pair_list`: each row holds 8 distinct blocks and its first entry is the row's own block. `pair_count`: some row uses all 8 slots.
All inputs are finite; a program needn't handle non-finite values.
Results may differ from the reference program's by a relative error of at most 0.038.
Values may be sent and summed in bfloat16 or wider, within the bound.
A program may use at most 64 MiB of HBM per device.

```python
import jax
import jax.numpy as jnp
from jax import lax

D = 256
HEADS = 16
BLK_ATOMS = 128
WALKERS = 6
NBLK = 16
ATOMS = 2048
MAXN = 8
LAYERS = 8


def block_lists(key):
    row_ids = jnp.arange(NBLK, dtype=jnp.int32)
    noise_bits = jax.random.randint(jax.random.fold_in(key, 11), (NBLK, NBLK), 0, 2 ** 20, dtype=jnp.int32)
    ranked = noise_bits * NBLK + row_ids[None, :]
    ranked = jnp.where(row_ids[None, :] == row_ids[:, None], -1, ranked)
    slot_order = jnp.argsort(ranked, axis=1, stable=True)[:, :MAXN].astype(jnp.int32)
    counts = jax.random.randint(jax.random.fold_in(key, 12), (NBLK,), 2, MAXN + 1, dtype=jnp.int32)
    full_row = jax.random.randint(jax.random.fold_in(key, 13), (), 0, NBLK, dtype=jnp.int32)
    counts = jnp.where(row_ids == full_row, MAXN, counts).astype(jnp.int32)
    return (slot_order, counts)


def draw_pair_list(key, part):
    return block_lists(key)[0]


def draw_pair_count(key, part):
    return block_lists(key)[1]


def block_levels(stream_key, dims, split, low, high):
    def one(dim, blocks):
        draws = jax.random.uniform(jax.random.fold_in(jax.random.fold_in(stream_key, 6), dim), (blocks,), jnp.float32, low / len(split), high / len(split))
        return jnp.repeat(jnp.exp(draws), dims[dim] // blocks).reshape((-1,) + (1,) * (len(dims) - dim - 1))

    loudness = one(*split[0])
    for cut in split[1:]:
        loudness = loudness * one(*cut)
    return loudness


def bell_draw(own_key, dims, scale, reach, pieces=(), kind=jnp.bfloat16):
    gain = block_levels(own_key, dims, pieces, -0.22, 0.18) if pieces else 1.0
    entries = jax.random.normal(own_key, dims, jnp.float32) * scale * gain
    return jnp.minimum(jnp.maximum(entries, -reach), reach).astype(kind)


def setup_inputs(seed: int = 0) -> dict:
    key_of = jax.random.split(jax.random.key(seed), 7)
    return {
        "layer_inputs": bell_draw(key_of[0], (LAYERS, WALKERS, ATOMS, D), 1.0, 6.0, ((0, 8), (2, 16))),
        "final_cot": bell_draw(key_of[1], (WALKERS, ATOMS, D), 1.0, 6.0, ((1, 16),)),
        "attn_weights": bell_draw(key_of[2], (LAYERS, 4, D, D), D ** -0.5, 0.375, ((0, 8),)),
        "norm_gain": jnp.clip(1.0 + 0.1 * jax.random.normal(key_of[3], (LAYERS, D), jnp.float32), 0.5, 1.5),
        "pair_list": draw_pair_list(jax.random.fold_in(key_of[6], 71), 0),
        "pair_count": draw_pair_count(jax.random.fold_in(key_of[6], 71), 0),
    }


eps = 1e-05

def rounded(values):
    return lax.optimization_barrier(values.astype(jnp.bfloat16)).astype(jnp.float32)

def rms_parts(inputs, gain_row):
    feats = inputs.astype(jnp.float32)
    inv_rms = lax.rsqrt(lax.optimization_barrier(jnp.mean(feats * feats, axis=-1, keepdims=True)) + eps)
    unit_feat = feats * inv_rms
    normed = (unit_feat * gain_row).astype(jnp.bfloat16)
    return (unit_feat, inv_rms, normed)

def norm_back(normed_grad, unit_feat, inv_rms, gain_row):
    unit_grad = normed_grad * gain_row
    centre = lax.optimization_barrier(jnp.mean(unit_grad * unit_feat, axis=-1, keepdims=True))
    return inv_rms * (unit_grad - unit_feat * centre)

def layer_back(inputs, cotangent, weights, gain_row, pair_list, pair_count):
    block_count = ATOMS // BLK_ATOMS
    head_size = D // HEADS
    score_scale = head_size ** (-0.5)
    unit_feat, inv_rms, normed = rms_parts(inputs, gain_row)
    queries = jnp.dot(normed, weights[0], preferred_element_type=jnp.float32).astype(jnp.bfloat16)
    keys_all = jnp.dot(normed, weights[1], preferred_element_type=jnp.float32).astype(jnp.bfloat16)
    values_all = jnp.dot(normed, weights[2], preferred_element_type=jnp.float32).astype(jnp.bfloat16)
    shape_heads = (block_count, BLK_ATOMS, HEADS, head_size)
    wide_shape = (block_count, MAXN * BLK_ATOMS, HEADS, head_size)
    query_h = queries.reshape(shape_heads).astype(jnp.float32)
    key_h = keys_all.reshape(shape_heads)[pair_list].reshape(wide_shape).astype(jnp.float32)
    value_h = values_all.reshape(shape_heads)[pair_list].reshape(wide_shape).astype(jnp.float32)
    slot_ok = jnp.arange(MAXN)[None, :] < pair_count[:, None]
    column_ok = jnp.repeat(slot_ok, BLK_ATOMS, axis=1)
    scores = jnp.einsum('aqhd,akhd->ahqk', query_h, key_h) * score_scale
    scores = jnp.where(column_ok[:, None, None, :], scores, -1e+30)
    expos = jnp.exp(scores)
    probs = expos / lax.optimization_barrier(jnp.sum(expos, axis=3, keepdims=True))
    probs_b = rounded(probs)
    attended = rounded(jnp.einsum('ahqk,akhd->aqhd', probs_b, value_h))
    out_grad = rounded(jnp.dot(cotangent, weights[3].T, preferred_element_type=jnp.float32)).reshape(shape_heads)
    delta = jnp.moveaxis(lax.optimization_barrier(jnp.sum(out_grad * attended, axis=3)), 2, 1)
    prob_grad = jnp.einsum('aqhd,akhd->ahqk', out_grad, value_h)
    score_grad = rounded(probs * (prob_grad - delta[..., None]) * score_scale)
    query_grad = jnp.einsum('ahqk,akhd->aqhd', score_grad, key_h).reshape(ATOMS, D).astype(jnp.bfloat16)
    part_shape = (block_count, MAXN, BLK_ATOMS, D)
    key_part = rounded(jnp.einsum('ahqk,aqhd->akhd', score_grad, query_h)).reshape(part_shape)
    value_part = rounded(jnp.einsum('ahqk,aqhd->akhd', probs_b, out_grad)).reshape(part_shape)
    zero_blocks = jnp.zeros((block_count, BLK_ATOMS, D), jnp.float32)
    key_grad = zero_blocks.at[pair_list].add(key_part).reshape(ATOMS, D).astype(jnp.bfloat16)
    value_grad = zero_blocks.at[pair_list].add(value_part).reshape(ATOMS, D).astype(jnp.bfloat16)
    normed_grad = jnp.dot(query_grad, weights[0].T, preferred_element_type=jnp.float32) + jnp.dot(key_grad, weights[1].T, preferred_element_type=jnp.float32) + jnp.dot(value_grad, weights[2].T, preferred_element_type=jnp.float32)
    gain_grad = lax.optimization_barrier(jnp.sum(normed_grad * unit_feat, axis=0))
    input_grad = (cotangent.astype(jnp.float32) + norm_back(normed_grad, unit_feat, inv_rms, gain_row)).astype(jnp.bfloat16)
    attended_b = attended.reshape(ATOMS, D).astype(jnp.bfloat16)
    weight_grad = jnp.stack([jnp.dot(normed.T, query_grad, preferred_element_type=jnp.float32), jnp.dot(normed.T, key_grad, preferred_element_type=jnp.float32), jnp.dot(normed.T, value_grad, preferred_element_type=jnp.float32), jnp.dot(attended_b.T, cotangent, preferred_element_type=jnp.float32)])
    return (input_grad, weight_grad, gain_grad)

def reference(layer_inputs, final_cot, attn_weights, norm_gain, pair_list, pair_count):
    cotangent = final_cot
    cot_list = []
    grad_list = []
    gain_list = []
    for layer_no in range(LAYERS - 1, -1, -1):

        def per_walker(walker_pair, layer_no=layer_no):
            return layer_back(walker_pair[0], walker_pair[1], attn_weights[layer_no], norm_gain[layer_no], pair_list, pair_count)
        input_grads, walker_grads, walker_gains = lax.map(per_walker, (layer_inputs[layer_no], cotangent))
        cot_list.insert(0, input_grads)
        grad_list.insert(0, lax.optimization_barrier(jnp.sum(walker_grads, axis=0)))
        gain_list.insert(0, lax.optimization_barrier(jnp.sum(walker_gains, axis=0)))
        cotangent = input_grads
    return (jnp.stack(cot_list), jnp.stack(grad_list), jnp.stack(gain_list))
```

```python
from functools import partial

import jax
import jax.numpy as jnp
from jax import lax
from jax.experimental import pallas as pl
from jax.experimental.pallas import tpu as pltpu
from jax.sharding import PartitionSpec as P

HEADS = 16
DH = 16
BLKS = 16
SEGS = 8
ROWS = 128
WIDTH = 256
GROUP = 8
DUMMY = BLKS
eps = 1e-05
F32, BF16 = jnp.float32, jnp.bfloat16
VMEM_SPEC = pl.BlockSpec(memory_space=pltpu.VMEM)
SMEM_SPEC = pl.BlockSpec(memory_space=pltpu.SMEM)


def mm(a, b):
    return jnp.dot(a, b, preferred_element_type=F32)


def mm_nt(a, b):
    return lax.dot_general(a, b, (((1,), (1,)), ((), ())), preferred_element_type=F32)


def peers(me):
    return [lax.rem(me + k, BLKS) for k in range(1, BLKS)]


def greet(me, more=()):
    barrier = pltpu.get_barrier_semaphore()
    for peer in peers(me):
        pl.semaphore_signal(
            barrier, inc=1, device_id={"blk": peer}, device_id_type=pl.DeviceIdType.MESH
        )
    for seg in more:
        pl.semaphore_signal(
            barrier, inc=1, device_id={"segment": seg}, device_id_type=pl.DeviceIdType.MESH
        )
    pl.semaphore_wait(barrier, BLKS - 1 + len(more))


def copy_to(src, dst, send, recv, where):
    return pltpu.make_async_remote_copy(
        src_ref=src,
        dst_ref=dst,
        send_sem=send,
        recv_sem=recv,
        device_id=where,
        device_id_type=pl.DeviceIdType.MESH,
    )


def swap_kernel(in_ref, out_ref, send, recv):
    me = lax.axis_index("blk")
    greet(me)
    copies = [
        copy_to(in_ref.at[:, peer], out_ref.at[:, me], send.at[k], recv.at[k], {"blk": peer})
        for k, peer in enumerate(peers(me))
    ]
    for c in copies:
        c.start()
    out_ref[:, me] = in_ref[:, me]
    for c in copies:
        c.wait()


def swap(values, collective_id):
    return pl.pallas_call(
        swap_kernel,
        out_shape=jax.ShapeDtypeStruct(values.shape, values.dtype),
        in_specs=[VMEM_SPEC],
        out_specs=VMEM_SPEC,
        scratch_shapes=[
            pltpu.SemaphoreType.DMA((BLKS - 1,)),
            pltpu.SemaphoreType.DMA((BLKS - 1,)),
        ],
        compiler_params=pltpu.CompilerParams(
            collective_id=collective_id, has_side_effects=True, vmem_limit_bytes=16 << 20
        ),
        name="swap",
    )(values)


def total_kernel(in_ref, out_ref, got, own, send1, recv1, send2, recv2):
    me = lax.axis_index("blk")
    greet(me)
    first = [
        copy_to(in_ref.at[peer], got.at[me], send1.at[k], recv1.at[k], {"blk": peer})
        for k, peer in enumerate(peers(me))
    ]
    for c in first:
        c.start()
    got[me] = in_ref[me]
    for c in first:
        c.wait()
    acc = got[0].astype(F32)
    for b in range(1, BLKS):
        acc = acc + got[b].astype(F32)
    own[...] = acc.astype(BF16)
    second = [
        copy_to(own, out_ref.at[me], send2.at[k], recv2.at[k], {"blk": peer})
        for k, peer in enumerate(peers(me))
    ]
    for c in second:
        c.start()
    out_ref[me] = own[...]
    for c in second:
        c.wait()


def total(values, collective_id):
    sems = pltpu.SemaphoreType.DMA((BLKS - 1,))
    return pl.pallas_call(
        total_kernel,
        out_shape=jax.ShapeDtypeStruct(values.shape, BF16),
        in_specs=[VMEM_SPEC],
        out_specs=VMEM_SPEC,
        scratch_shapes=[
            pltpu.VMEM(values.shape, BF16),
            pltpu.VMEM(values.shape[1:], BF16),
            sems,
            sems,
            sems,
            sems,
        ],
        compiler_params=pltpu.CompilerParams(
            collective_id=collective_id, has_side_effects=True, vmem_limit_bytes=16 << 20
        ),
        name="total",
    )(values)


def step_kernel(
    walker_ref, dqkv_ref, x_ref, gain_ref, g_ref, fc_ref, wc_ref, wo_ref,
    cot_ref, gnext_ref, dout_ref, stash_ref,
    hop_in, dout_own, send1, recv1, hop_send, hop_recv, send2, recv2,
):
    me = lax.axis_index("blk")
    seg = lax.axis_index("segment")
    above, below = lax.rem(seg + 1, SEGS), lax.rem(seg + SEGS - 1, SEGS)
    greet(me, (above,))
    first = [
        copy_to(dqkv_ref.at[peer], stash_ref.at[me], send1.at[k], recv1.at[k], {"blk": peer})
        for k, peer in enumerate(peers(me))
    ]
    for c in first:
        c.start()
    stash_ref[me] = dqkv_ref[me]
    x = x_ref[walker_ref[0]].astype(F32)
    inv = lax.rsqrt(jnp.mean(x * x, axis=0, keepdims=True) + eps)
    unit = x * inv
    g = g_ref[...].astype(F32)
    for c in first:
        c.wait_recv()
    grads = stash_ref[...].reshape(HEADS * 3 * DH, ROWS)
    unit_grad = mm(wc_ref[...], grads) * gain_ref[...]
    centre = jnp.mean(unit_grad * unit, axis=0, keepdims=True)
    cot_ref[...] = (g + inv * (unit_grad - unit * centre)).astype(BF16)
    hop = copy_to(cot_ref, hop_in, hop_send, hop_recv, {"segment": below})
    hop.start()
    last_g = fc_ref[walker_ref[1]].astype(F32)
    hop.wait_recv()
    gnext = jnp.where(seg == SEGS - 1, last_g, hop_in[...].astype(F32)).astype(BF16)
    gnext_ref[...] = gnext
    dout_own[...] = mm(wo_ref[...], gnext).astype(BF16).reshape(HEADS, DH, ROWS)
    second = [
        copy_to(dout_own.at[peer], dout_ref.at[me], send2.at[k], recv2.at[k], {"blk": peer})
        for k, peer in enumerate(peers(me))
    ]
    for c in second:
        c.start()
    dout_ref[me] = dout_own[me]
    for c in second:
        c.wait_recv()
    for c in first:
        c.wait_send()
    hop.wait_send()
    for c in second:
        c.wait_send()


def step(walker_pair, dqkv, x_t, gain_col, g, fc_t, w_cat, w_out):
    sems = pltpu.SemaphoreType.DMA((BLKS - 1,))
    tile = jax.ShapeDtypeStruct((WIDTH, ROWS), BF16)
    return pl.pallas_call(
        step_kernel,
        out_shape=(
            tile,
            tile,
            jax.ShapeDtypeStruct((BLKS, DH, ROWS), BF16),
            jax.ShapeDtypeStruct((HEADS, 3 * DH, ROWS), BF16),
        ),
        in_specs=[SMEM_SPEC] + [VMEM_SPEC] * 7,
        out_specs=[VMEM_SPEC] * 4,
        scratch_shapes=[
            pltpu.VMEM((WIDTH, ROWS), BF16),
            pltpu.VMEM((HEADS, DH, ROWS), BF16),
            sems,
            sems,
            pltpu.SemaphoreType.DMA,
            pltpu.SemaphoreType.DMA,
            sems,
            sems,
        ],
        compiler_params=pltpu.CompilerParams(
            collective_id=2, has_side_effects=True, vmem_limit_bytes=16 << 20
        ),
        name="step",
    )(walker_pair, dqkv, x_t, gain_col, g, fc_t, w_cat, w_out)


def turned(tile):
    return jnp.transpose(tile.astype(F32)).astype(BF16)


def forward_kernel(info_ref, qkv_ref, att_ref, lse_ref, k_nat, q_all, sums, lse, att):
    for b in range(BLKS):
        k_nat[b] = turned(qkv_ref[0, b, DH : 2 * DH, :])
        q_all[b] = qkv_ref[0, b, 0:DH, :]
    q_all[DUMMY] = jnp.zeros((DH, ROWS), BF16)
    sums[...] = jnp.zeros_like(sums)
    att[...] = jnp.zeros_like(att)
    groups = info_ref[2 * BLKS * 8]

    def pair(n):
        return info_ref[n], info_ref[BLKS * 8 + n]

    def add_up(n, carry):
        for u in range(GROUP):
            a, j = pair(n * GROUP + u)
            expo = jnp.exp(mm(k_nat[j], q_all[a]))
            sums[a] += jnp.sum(expo.reshape(ROWS // 8, 8, ROWS), axis=0)
        return carry

    lax.fori_loop(0, groups, add_up, 0)
    for b in range(BLKS):
        lse[b] = jnp.log(jnp.sum(sums[b], axis=0, keepdims=True))
        lse_ref[0, b] = lse[b]
    lse[DUMMY] = jnp.full((1, ROWS), 1e30, F32)

    def attend(n, carry):
        for u in range(GROUP):
            a, j = pair(n * GROUP + u)
            prob = jnp.exp(mm(k_nat[j], q_all[a]) - lse[a]).astype(BF16)
            att[a] += mm(qkv_ref[0, j, 2 * DH : 3 * DH, :], prob)
        return carry

    lax.fori_loop(0, groups, attend, 0)
    for b in range(BLKS):
        att_ref[0, b] = att[b].astype(BF16)


def forward(info, qkv, walkers):
    def spec(*tail):
        return pl.BlockSpec((1, BLKS) + tail, lambda w, s: (w, 0, 0, 0))

    return pl.pallas_call(
        forward_kernel,
        grid_spec=pltpu.PrefetchScalarGridSpec(
            num_scalar_prefetch=1,
            grid=(walkers,),
            in_specs=[spec(3 * DH, ROWS)],
            out_specs=[spec(DH, ROWS), spec(1, ROWS)],
            scratch_shapes=[
                pltpu.VMEM((BLKS, ROWS, DH), BF16),
                pltpu.VMEM((BLKS + 1, DH, ROWS), BF16),
                pltpu.VMEM((BLKS + 1, 8, ROWS), F32),
                pltpu.VMEM((BLKS + 1, 1, ROWS), F32),
                pltpu.VMEM((BLKS + 1, DH, ROWS), F32),
            ],
        ),
        out_shape=(
            jax.ShapeDtypeStruct((walkers, BLKS, DH, ROWS), BF16),
            jax.ShapeDtypeStruct((walkers, BLKS, 1, ROWS), F32),
        ),
        compiler_params=pltpu.CompilerParams(vmem_limit_bytes=24 << 20),
        name="forward",
    )(info, qkv)


def backward_kernel(
    info_ref, walker_ref, qkv_ref, att_ref, lse_ref, dout_ref, out_ref,
    kv_nat, q_dout, lse, delta, dq, dkv,
):
    nothing = jnp.zeros((DH, ROWS), BF16)
    for b in range(BLKS):
        kv_nat[b] = turned(qkv_ref[0, b, DH : 3 * DH, :])
        q_dout[b, 0:DH, 0:ROWS] = qkv_ref[0, b, 0:DH, :]
        q_dout[b, 0:DH, ROWS : 2 * ROWS] = nothing
        q_dout[b, DH : 2 * DH, 0:ROWS] = nothing
        q_dout[b, DH : 2 * DH, ROWS : 2 * ROWS] = dout_ref[b]
        lse[b] = lse_ref[0, b]
        delta[b] = jnp.sum(
            dout_ref[b].astype(F32) * att_ref[0, b].astype(F32), axis=0, keepdims=True
        )
    q_dout[DUMMY] = jnp.zeros((2 * DH, 2 * ROWS), BF16)
    lse[DUMMY] = jnp.full((1, ROWS), 1e30, F32)
    delta[DUMMY] = jnp.zeros((1, ROWS), F32)
    dq[...] = jnp.zeros_like(dq)
    dkv[...] = jnp.zeros_like(dkv)

    def body(n, carry):
        for u in range(GROUP):
            a = info_ref[n * GROUP + u]
            j = info_ref[BLKS * 8 + n * GROUP + u]
            both = mm(kv_nat[j], q_dout[a])
            prob = jnp.exp(both[:, 0:ROWS] - lse[a])
            score_grad = (prob * (both[:, ROWS : 2 * ROWS] - delta[a])).astype(BF16)
            side = jnp.concatenate([score_grad, prob.astype(BF16)], axis=1)
            dkv[j] += mm_nt(q_dout[a], side)
            dq[a] += mm(qkv_ref[0, j, DH : 2 * DH, :], score_grad)
        return carry

    lax.fori_loop(0, info_ref[2 * BLKS * 8], body, 0)
    for b in range(BLKS):
        out_ref[b, 0:DH] = (dq[b] * 0.25).astype(BF16)
        out_ref[b, DH : 3 * DH] = dkv[b].astype(BF16)


def backward(info, walker_pair, qkv, att, lse, dout):
    def spec(*tail):
        return pl.BlockSpec((1, BLKS) + tail, lambda i, s, w: (w[0], 0, 0, 0))

    def whole(*dims):
        return pl.BlockSpec(dims, lambda i, s, w: (0,) * len(dims))

    return pl.pallas_call(
        backward_kernel,
        grid_spec=pltpu.PrefetchScalarGridSpec(
            num_scalar_prefetch=2,
            grid=(1,),
            in_specs=[
                spec(3 * DH, ROWS),
                spec(DH, ROWS),
                spec(1, ROWS),
                whole(BLKS, DH, ROWS),
            ],
            out_specs=whole(BLKS, 3 * DH, ROWS),
            scratch_shapes=[
                pltpu.VMEM((BLKS, ROWS, 2 * DH), BF16),
                pltpu.VMEM((BLKS + 1, 2 * DH, 2 * ROWS), BF16),
                pltpu.VMEM((BLKS + 1, 1, ROWS), F32),
                pltpu.VMEM((BLKS + 1, 1, ROWS), F32),
                pltpu.VMEM((BLKS + 1, DH, ROWS), F32),
                pltpu.VMEM((BLKS, 2 * DH, ROWS), F32),
            ],
        ),
        out_shape=jax.ShapeDtypeStruct((BLKS, 3 * DH, ROWS), BF16),
        compiler_params=pltpu.CompilerParams(vmem_limit_bytes=16 << 20),
        name="backward",
    )(info, walker_pair, qkv, att, lse, dout)


def pair_table(pair_list, pair_count):
    blocks, slots = pair_list.shape
    pairs = blocks * slots
    keys = pair_list.T.reshape(-1)
    queries = jnp.tile(jnp.arange(blocks, dtype=jnp.int32), slots)
    used = (jnp.arange(slots)[:, None] < pair_count[None, :]).reshape(-1)
    order = jnp.arange(pairs)
    place = jnp.sum((order[None, :] < order[:, None]) & used[None, :], axis=1)
    chosen = (place[None, :] == order[:, None]) & used[None, :]
    count = jnp.sum(used.astype(jnp.int32))
    key_of = jnp.sum(jnp.where(chosen, keys[None, :], 0), axis=1)
    query_of = jnp.sum(jnp.where(chosen, queries[None, :], 0), axis=1)
    query_of = jnp.where(order < count, query_of, DUMMY)
    groups = (count + GROUP - 1) // GROUP
    return jnp.concatenate([query_of, key_of, groups[None]]).astype(jnp.int32)


def per_device(layer_inputs, final_cot, attn_weights, norm_gain, pair_list, pair_count):
    seg = lax.axis_index("segment")
    walkers = layer_inputs.shape[1]
    weights = attn_weights[0]
    gain_col = norm_gain[0][:, None]
    info = pair_table(pair_list, pair_count)
    x_t = jnp.swapaxes(layer_inputs[0], 1, 2)
    fc_t = jnp.swapaxes(final_cot, 1, 2)
    w_cat = (
        weights[:3]
        .reshape(3, WIDTH, HEADS, DH)
        .transpose(1, 2, 0, 3)
        .reshape(WIDTH, 3 * WIDTH)
    )
    w_out = weights[3]

    feats = x_t.astype(F32)
    inv_rms = lax.rsqrt(jnp.mean(feats * feats, axis=1, keepdims=True) + eps)
    unit = feats * inv_rms
    normed = (unit * gain_col).astype(BF16)
    qkv = jnp.einsum("fc,wfi->wci", w_cat, normed, preferred_element_type=F32).astype(BF16)
    qkv = qkv.reshape(walkers, HEADS, 3 * DH, ROWS)
    part = jnp.arange(3 * DH)[:, None] < DH
    qkv = jnp.where(part, qkv * jnp.asarray(0.25, BF16), qkv)

    g = jnp.where(seg == SEGS - 1, fc_t[0], jnp.zeros_like(fc_t[0]))
    dout = mm(w_out, g).astype(BF16).reshape(1, HEADS, DH, ROWS)
    dout = jnp.pad(dout, ((0, 0), (0, 0), (0, 2 * DH), (0, 0)))
    swapped = swap(jnp.concatenate([qkv, dout], axis=0), 0)
    dout = swapped[walkers, :, 0:DH]
    att, lse = forward(info, swapped, walkers)

    ticks = walkers + SEGS - 1
    cots, gs, stashes = [], [], []
    for tick in range(ticks):
        now = jnp.clip(tick - (SEGS - 1 - seg), 0, walkers - 1)
        later = jnp.clip(tick + 1 - (SEGS - 1 - seg), 0, walkers - 1)
        walker_pair = jnp.stack([now, later]).astype(jnp.int32)
        dqkv = backward(info, walker_pair, swapped, att, lse, dout)
        gs.append(g)
        cot, g, dout, stash = step(walker_pair, dqkv, x_t, gain_col, g, fc_t, w_cat, w_out)
        cots.append(cot)
        stashes.append(stash)

    def mine(values):
        return lax.dynamic_slice_in_dim(jnp.stack(values), SEGS - 1 - seg, walkers, 0)

    cots, gs, stashes = lax.optimization_barrier((cots, gs, stashes))
    cot_all, g_all, grads = mine(cots), mine(gs), mine(stashes)
    att_own = swap(att, 1).reshape(walkers, WIDTH, ROWS)
    dw = jnp.einsum(
        "wfi,whtdi->tfhd",
        normed,
        grads.reshape(walkers, HEADS, 3, DH, ROWS),
        preferred_element_type=F32,
    ).reshape(3, WIDTH, WIDTH)
    dwo = jnp.einsum("wci,wfi->cf", att_own, g_all, preferred_element_type=F32)
    normed_grad = jnp.einsum(
        "fc,wci->wfi",
        w_cat,
        grads.reshape(walkers, 3 * WIDTH, ROWS),
        preferred_element_type=F32,
    )
    gain_part = jnp.sum(normed_grad * unit, axis=(0, 2))

    own = jnp.concatenate([dw, dwo[None]], axis=0).reshape(BLKS, 4 * WIDTH // BLKS, WIDTH)
    extra = jnp.zeros((BLKS, 16, WIDTH), F32).at[0, 0].set(gain_part)
    summed = total(jnp.concatenate([own, extra], axis=1).astype(BF16), 3).astype(F32)
    grad_total = summed[:, : 4 * WIDTH // BLKS].reshape(4, WIDTH, WIDTH)
    gain_total = summed[0, 4 * WIDTH // BLKS]
    return (jnp.swapaxes(cot_all, 1, 2)[None], grad_total[None], gain_total[None])


def solution(mesh):
    return jax.shard_map(
        per_device,
        mesh=mesh,
        in_specs=(
            P("segment", None, "blk", None),
            P(None, "blk", None),
            P("segment", None, None, None),
            P("segment", None),
            P(),
            P(),
        ),
        out_specs=(
            P("segment", None, "blk", None),
            P("segment", None, None, None),
            P("segment", None),
        ),
        check_vma=False,
    )
```

```python
from functools import partial

import jax
import jax.numpy as jnp
from jax import lax
from jax.experimental import pallas as pl
from jax.experimental.pallas import tpu as pltpu
from jax.sharding import PartitionSpec as P

HEADS = 16
DH = 16
BLKS = 16
SEGS = 8
ROWS = 128
WIDTH = 256
GROUP = 16
DUMMY = BLKS
eps = 1e-05
F32, BF16 = jnp.float32, jnp.bfloat16
VMEM_SPEC = pl.BlockSpec(memory_space=pltpu.VMEM)
SMEM_SPEC = pl.BlockSpec(memory_space=pltpu.SMEM)


def mm(a, b):
    return jnp.dot(a, b, preferred_element_type=F32)


def mm_nt(a, b):
    return lax.dot_general(a, b, (((1,), (1,)), ((), ())), preferred_element_type=F32)


def peers(me):
    return [lax.rem(me + k, BLKS) for k in range(1, BLKS)]


def greet(me, more=()):
    barrier = pltpu.get_barrier_semaphore()
    for peer in peers(me):
        pl.semaphore_signal(
            barrier, inc=1, device_id={"blk": peer}, device_id_type=pl.DeviceIdType.MESH
        )
    for seg in more:
        pl.semaphore_signal(
            barrier, inc=1, device_id={"segment": seg}, device_id_type=pl.DeviceIdType.MESH
        )
    pl.semaphore_wait(barrier, BLKS - 1 + len(more))


def copy_to(src, dst, send, recv, where):
    return pltpu.make_async_remote_copy(
        src_ref=src,
        dst_ref=dst,
        send_sem=send,
        recv_sem=recv,
        device_id=where,
        device_id_type=pl.DeviceIdType.MESH,
    )


def swap_kernel(in_ref, out_ref, send, recv):
    me = lax.axis_index("blk")
    greet(me)
    copies = [
        copy_to(in_ref.at[:, peer], out_ref.at[:, me], send.at[k], recv.at[k], {"blk": peer})
        for k, peer in enumerate(peers(me))
    ]
    for c in copies:
        c.start()
    out_ref[:, me] = in_ref[:, me]
    for c in copies:
        c.wait()


def swap(values, collective_id):
    return pl.pallas_call(
        swap_kernel,
        out_shape=jax.ShapeDtypeStruct(values.shape, values.dtype),
        in_specs=[VMEM_SPEC],
        out_specs=VMEM_SPEC,
        scratch_shapes=[
            pltpu.SemaphoreType.DMA((BLKS - 1,)),
            pltpu.SemaphoreType.DMA((BLKS - 1,)),
        ],
        compiler_params=pltpu.CompilerParams(
            collective_id=collective_id, has_side_effects=True, vmem_limit_bytes=16 << 20
        ),
        name="swap",
    )(values)


def total_kernel(in_ref, out_ref, got, own, send1, recv1, send2, recv2):
    me = lax.axis_index("blk")
    greet(me)
    first = [
        copy_to(in_ref.at[peer], got.at[me], send1.at[k], recv1.at[k], {"blk": peer})
        for k, peer in enumerate(peers(me))
    ]
    for c in first:
        c.start()
    got[me] = in_ref[me]
    for c in first:
        c.wait()
    acc = got[0].astype(F32)
    for b in range(1, BLKS):
        acc = acc + got[b].astype(F32)
    own[...] = acc.astype(BF16)
    second = [
        copy_to(own, out_ref.at[me], send2.at[k], recv2.at[k], {"blk": peer})
        for k, peer in enumerate(peers(me))
    ]
    for c in second:
        c.start()
    out_ref[me] = own[...]
    for c in second:
        c.wait()


def total(values, collective_id):
    sems = pltpu.SemaphoreType.DMA((BLKS - 1,))
    return pl.pallas_call(
        total_kernel,
        out_shape=jax.ShapeDtypeStruct(values.shape, BF16),
        in_specs=[VMEM_SPEC],
        out_specs=VMEM_SPEC,
        scratch_shapes=[
            pltpu.VMEM(values.shape, BF16),
            pltpu.VMEM(values.shape[1:], BF16),
            sems,
            sems,
            sems,
            sems,
        ],
        compiler_params=pltpu.CompilerParams(
            collective_id=collective_id, has_side_effects=True, vmem_limit_bytes=16 << 20
        ),
        name="total",
    )(values)


def step_kernel(
    walker_ref, dqkv_ref, x_ref, gain_ref, g_ref, fc_ref, wc_ref, wo_ref,
    cot_ref, gnext_ref, dout_ref, stash_ref,
    hop_in, dout_own, send1, recv1, hop_send, hop_recv, send2, recv2,
):
    me = lax.axis_index("blk")
    seg = lax.axis_index("segment")
    above, below = lax.rem(seg + 1, SEGS), lax.rem(seg + SEGS - 1, SEGS)
    greet(me, (above,))
    first = [
        copy_to(dqkv_ref.at[peer], stash_ref.at[me], send1.at[k], recv1.at[k], {"blk": peer})
        for k, peer in enumerate(peers(me))
    ]
    for c in first:
        c.start()
    stash_ref[me] = dqkv_ref[me]
    x = x_ref[walker_ref[0]].astype(F32)
    inv = lax.rsqrt(jnp.mean(x * x, axis=0, keepdims=True) + eps)
    unit = x * inv
    g = g_ref[...].astype(F32)
    for c in first:
        c.wait_recv()
    grads = stash_ref[...].reshape(HEADS * 3 * DH, ROWS)
    unit_grad = mm(wc_ref[...], grads) * gain_ref[...]
    centre = jnp.mean(unit_grad * unit, axis=0, keepdims=True)
    cot_ref[...] = (g + inv * (unit_grad - unit * centre)).astype(BF16)
    hop = copy_to(cot_ref, hop_in, hop_send, hop_recv, {"segment": below})
    hop.start()
    last_g = fc_ref[walker_ref[1]].astype(F32)
    hop.wait_recv()
    gnext = jnp.where(seg == SEGS - 1, last_g, hop_in[...].astype(F32)).astype(BF16)
    gnext_ref[...] = gnext
    dout_own[...] = mm(wo_ref[...], gnext).astype(BF16).reshape(HEADS, DH, ROWS)
    second = [
        copy_to(dout_own.at[peer], dout_ref.at[me], send2.at[k], recv2.at[k], {"blk": peer})
        for k, peer in enumerate(peers(me))
    ]
    for c in second:
        c.start()
    dout_ref[me] = dout_own[me]
    for c in second:
        c.wait_recv()
    for c in first:
        c.wait_send()
    hop.wait_send()
    for c in second:
        c.wait_send()


def step(walker_pair, dqkv, x_t, gain_col, g, fc_t, w_cat, w_out):
    sems = pltpu.SemaphoreType.DMA((BLKS - 1,))
    tile = jax.ShapeDtypeStruct((WIDTH, ROWS), BF16)
    return pl.pallas_call(
        step_kernel,
        out_shape=(
            tile,
            tile,
            jax.ShapeDtypeStruct((BLKS, DH, ROWS), BF16),
            jax.ShapeDtypeStruct((HEADS, 3 * DH, ROWS), BF16),
        ),
        in_specs=[SMEM_SPEC] + [VMEM_SPEC] * 7,
        out_specs=[VMEM_SPEC] * 4,
        scratch_shapes=[
            pltpu.VMEM((WIDTH, ROWS), BF16),
            pltpu.VMEM((HEADS, DH, ROWS), BF16),
            sems,
            sems,
            pltpu.SemaphoreType.DMA,
            pltpu.SemaphoreType.DMA,
            sems,
            sems,
        ],
        compiler_params=pltpu.CompilerParams(
            collective_id=2, has_side_effects=True, vmem_limit_bytes=16 << 20
        ),
        name="step",
    )(walker_pair, dqkv, x_t, gain_col, g, fc_t, w_cat, w_out)


def turned(tile):
    return jnp.transpose(tile.astype(F32)).astype(BF16)


def forward_kernel(info_ref, qkv_ref, att_ref, lse_ref, k_nat, q_all, sums, lse, att):
    for b in range(BLKS):
        k_nat[b] = turned(qkv_ref[0, b, DH : 2 * DH, :])
        q_all[b] = qkv_ref[0, b, 0:DH, :]
    q_all[DUMMY] = jnp.zeros((DH, ROWS), BF16)
    sums[...] = jnp.zeros_like(sums)
    att[...] = jnp.zeros_like(att)
    groups = info_ref[2 * BLKS * 8]

    def group(n):
        return [(info_ref[n * GROUP + u], info_ref[BLKS * 8 + n * GROUP + u]) for u in range(GROUP)]

    def add_up(n, carry):
        pairs = group(n)
        scores = [mm(k_nat[j], q_all[a]) for a, j in pairs]
        parts = [jnp.sum(jnp.exp(s).reshape(ROWS // 8, 8, ROWS), axis=0) for s in scores]
        for (a, _), part in zip(pairs, parts):
            sums[a] += part
        return carry

    lax.fori_loop(0, groups, add_up, 0)
    for b in range(BLKS):
        lse[b] = jnp.log(jnp.sum(sums[b], axis=0, keepdims=True))
        lse_ref[0, b] = lse[b]
    lse[DUMMY] = jnp.full((1, ROWS), 1e30, F32)

    def attend(n, carry):
        pairs = group(n)
        scores = [mm(k_nat[j], q_all[a]) for a, j in pairs]
        probs = [jnp.exp(s - lse[a]).astype(BF16) for s, (a, _) in zip(scores, pairs)]
        parts = [mm(qkv_ref[0, j, 2 * DH : 3 * DH, :], p) for p, (_, j) in zip(probs, pairs)]
        for (a, _), part in zip(pairs, parts):
            att[a] += part
        return carry

    lax.fori_loop(0, groups, attend, 0)
    for b in range(BLKS):
        att_ref[0, b] = att[b].astype(BF16)


def forward(info, qkv, walkers):
    def spec(*tail):
        return pl.BlockSpec((1, BLKS) + tail, lambda w, s: (w, 0, 0, 0))

    return pl.pallas_call(
        forward_kernel,
        grid_spec=pltpu.PrefetchScalarGridSpec(
            num_scalar_prefetch=1,
            grid=(walkers,),
            in_specs=[spec(3 * DH, ROWS)],
            out_specs=[spec(DH, ROWS), spec(1, ROWS)],
            scratch_shapes=[
                pltpu.VMEM((BLKS, ROWS, DH), BF16),
                pltpu.VMEM((BLKS + 1, DH, ROWS), BF16),
                pltpu.VMEM((BLKS + 1, 8, ROWS), F32),
                pltpu.VMEM((BLKS + 1, 1, ROWS), F32),
                pltpu.VMEM((BLKS + 1, DH, ROWS), F32),
            ],
        ),
        out_shape=(
            jax.ShapeDtypeStruct((walkers, BLKS, DH, ROWS), BF16),
            jax.ShapeDtypeStruct((walkers, BLKS, 1, ROWS), F32),
        ),
        compiler_params=pltpu.CompilerParams(vmem_limit_bytes=24 << 20),
        name="forward",
    )(info, qkv)


def backward_kernel(
    info_ref, walker_ref, qkv_ref, att_ref, lse_ref, dout_ref, out_ref,
    kv_nat, q_dout, lse, delta, dq, dkv,
):
    nothing = jnp.zeros((DH, ROWS), BF16)
    for b in range(BLKS):
        kv_nat[b] = turned(qkv_ref[0, b, DH : 3 * DH, :])
        q_dout[b, 0:DH, 0:ROWS] = qkv_ref[0, b, 0:DH, :]
        q_dout[b, 0:DH, ROWS : 2 * ROWS] = nothing
        q_dout[b, DH : 2 * DH, 0:ROWS] = nothing
        q_dout[b, DH : 2 * DH, ROWS : 2 * ROWS] = dout_ref[b]
        lse[b] = lse_ref[0, b]
        delta[b] = jnp.sum(
            dout_ref[b].astype(F32) * att_ref[0, b].astype(F32), axis=0, keepdims=True
        )
    q_dout[DUMMY] = jnp.zeros((2 * DH, 2 * ROWS), BF16)
    lse[DUMMY] = jnp.full((1, ROWS), 1e30, F32)
    delta[DUMMY] = jnp.zeros((1, ROWS), F32)
    dq[...] = jnp.zeros_like(dq)
    dkv[...] = jnp.zeros_like(dkv)

    def body(n, carry):
        pairs = [(info_ref[n * GROUP + u], info_ref[BLKS * 8 + n * GROUP + u]) for u in range(GROUP)]
        sides = [q_dout[a] for a, _ in pairs]
        boths = [mm(kv_nat[j], side) for (_, j), side in zip(pairs, sides)]
        probs = [jnp.exp(both[:, 0:ROWS] - lse[a]) for both, (a, _) in zip(boths, pairs)]
        score_grads = [
            (prob * (both[:, ROWS : 2 * ROWS] - delta[a])).astype(BF16)
            for prob, both, (a, _) in zip(probs, boths, pairs)
        ]
        kv_parts = [
            mm_nt(side, jnp.concatenate([score_grad, prob.astype(BF16)], axis=1))
            for side, score_grad, prob in zip(sides, score_grads, probs)
        ]
        q_parts = [
            mm(qkv_ref[0, j, DH : 2 * DH, :], score_grad)
            for (_, j), score_grad in zip(pairs, score_grads)
        ]
        for (a, j), kv_part, q_part in zip(pairs, kv_parts, q_parts):
            dkv[j] += kv_part
            dq[a] += q_part
        return carry

    lax.fori_loop(0, info_ref[2 * BLKS * 8], body, 0)
    for b in range(BLKS):
        out_ref[b, 0:DH] = (dq[b] * 0.25).astype(BF16)
        out_ref[b, DH : 3 * DH] = dkv[b].astype(BF16)


def backward(info, walker_pair, qkv, att, lse, dout):
    def spec(*tail):
        return pl.BlockSpec((1, BLKS) + tail, lambda i, s, w: (w[0], 0, 0, 0))

    def whole(*dims):
        return pl.BlockSpec(dims, lambda i, s, w: (0,) * len(dims))

    return pl.pallas_call(
        backward_kernel,
        grid_spec=pltpu.PrefetchScalarGridSpec(
            num_scalar_prefetch=2,
            grid=(1,),
            in_specs=[
                spec(3 * DH, ROWS),
                spec(DH, ROWS),
                spec(1, ROWS),
                whole(BLKS, DH, ROWS),
            ],
            out_specs=whole(BLKS, 3 * DH, ROWS),
            scratch_shapes=[
                pltpu.VMEM((BLKS, ROWS, 2 * DH), BF16),
                pltpu.VMEM((BLKS + 1, 2 * DH, 2 * ROWS), BF16),
                pltpu.VMEM((BLKS + 1, 1, ROWS), F32),
                pltpu.VMEM((BLKS + 1, 1, ROWS), F32),
                pltpu.VMEM((BLKS + 1, DH, ROWS), F32),
                pltpu.VMEM((BLKS, 2 * DH, ROWS), F32),
            ],
        ),
        out_shape=jax.ShapeDtypeStruct((BLKS, 3 * DH, ROWS), BF16),
        compiler_params=pltpu.CompilerParams(vmem_limit_bytes=16 << 20),
        name="backward",
    )(info, walker_pair, qkv, att, lse, dout)


def pair_table(pair_list, pair_count):
    blocks, slots = pair_list.shape
    pairs = blocks * slots
    keys = pair_list.T.reshape(-1)
    queries = jnp.tile(jnp.arange(blocks, dtype=jnp.int32), slots)
    used = (jnp.arange(slots)[:, None] < pair_count[None, :]).reshape(-1)
    order = jnp.arange(pairs)
    place = jnp.sum((order[None, :] < order[:, None]) & used[None, :], axis=1)
    chosen = (place[None, :] == order[:, None]) & used[None, :]
    count = jnp.sum(used.astype(jnp.int32))
    key_of = jnp.sum(jnp.where(chosen, keys[None, :], 0), axis=1)
    query_of = jnp.sum(jnp.where(chosen, queries[None, :], 0), axis=1)
    query_of = jnp.where(order < count, query_of, DUMMY)
    groups = (count + GROUP - 1) // GROUP
    return jnp.concatenate([query_of, key_of, groups[None]]).astype(jnp.int32)


def per_device(layer_inputs, final_cot, attn_weights, norm_gain, pair_list, pair_count):
    seg = lax.axis_index("segment")
    walkers = layer_inputs.shape[1]
    weights = attn_weights[0]
    gain_col = norm_gain[0][:, None]
    info = pair_table(pair_list, pair_count)
    x_t = jnp.swapaxes(layer_inputs[0], 1, 2)
    fc_t = jnp.swapaxes(final_cot, 1, 2)
    w_cat = (
        weights[:3]
        .reshape(3, WIDTH, HEADS, DH)
        .transpose(1, 2, 0, 3)
        .reshape(WIDTH, 3 * WIDTH)
    )
    w_out = weights[3]

    feats = x_t.astype(F32)
    inv_rms = lax.rsqrt(jnp.mean(feats * feats, axis=1, keepdims=True) + eps)
    unit = feats * inv_rms
    normed = (unit * gain_col).astype(BF16)
    qkv = jnp.einsum("fc,wfi->wci", w_cat, normed, preferred_element_type=F32).astype(BF16)
    qkv = qkv.reshape(walkers, HEADS, 3 * DH, ROWS)
    part = jnp.arange(3 * DH)[:, None] < DH
    qkv = jnp.where(part, qkv * jnp.asarray(0.25, BF16), qkv)

    g = jnp.where(seg == SEGS - 1, fc_t[0], jnp.zeros_like(fc_t[0]))
    dout = mm(w_out, g).astype(BF16).reshape(1, HEADS, DH, ROWS)
    dout = jnp.pad(dout, ((0, 0), (0, 0), (0, 2 * DH), (0, 0)))
    swapped = swap(jnp.concatenate([qkv, dout], axis=0), 0)
    dout = swapped[walkers, :, 0:DH]
    att, lse = forward(info, swapped, walkers)

    ticks = walkers + SEGS - 1
    cots, gs, stashes = [], [], []
    for tick in range(ticks):
        now = jnp.clip(tick - (SEGS - 1 - seg), 0, walkers - 1)
        later = jnp.clip(tick + 1 - (SEGS - 1 - seg), 0, walkers - 1)
        walker_pair = jnp.stack([now, later]).astype(jnp.int32)
        dqkv = backward(info, walker_pair, swapped, att, lse, dout)
        gs.append(g)
        cot, g, dout, stash = step(walker_pair, dqkv, x_t, gain_col, g, fc_t, w_cat, w_out)
        cots.append(cot)
        stashes.append(stash)

    def mine(values):
        return lax.dynamic_slice_in_dim(jnp.stack(values), SEGS - 1 - seg, walkers, 0)

    cots, gs, stashes = lax.optimization_barrier((cots, gs, stashes))
    cot_all, g_all, grads = mine(cots), mine(gs), mine(stashes)
    att_own = swap(att, 1).reshape(walkers, WIDTH, ROWS)
    dw = jnp.einsum(
        "wfi,whtdi->tfhd",
        normed,
        grads.reshape(walkers, HEADS, 3, DH, ROWS),
        preferred_element_type=F32,
    ).reshape(3, WIDTH, WIDTH)
    dwo = jnp.einsum("wci,wfi->cf", att_own, g_all, preferred_element_type=F32)
    normed_grad = jnp.einsum(
        "fc,wci->wfi",
        w_cat,
        grads.reshape(walkers, 3 * WIDTH, ROWS),
        preferred_element_type=F32,
    )
    gain_part = jnp.sum(normed_grad * unit, axis=(0, 2))

    own = jnp.concatenate([dw, dwo[None]], axis=0).reshape(BLKS, 4 * WIDTH // BLKS, WIDTH)
    extra = jnp.zeros((BLKS, 16, WIDTH), F32).at[0, 0].set(gain_part)
    summed = total(jnp.concatenate([own, extra], axis=1).astype(BF16), 3).astype(F32)
    grad_total = summed[:, : 4 * WIDTH // BLKS].reshape(4, WIDTH, WIDTH)
    gain_total = summed[0, 4 * WIDTH // BLKS]
    return (jnp.swapaxes(cot_all, 1, 2)[None], grad_total[None], gain_total[None])


def solution(mesh):
    return jax.shard_map(
        per_device,
        mesh=mesh,
        in_specs=(
            P("segment", None, "blk", None),
            P(None, "blk", None),
            P("segment", None, None, None),
            P("segment", None),
            P(),
            P(),
        ),
        out_specs=(
            P("segment", None, "blk", None),
            P("segment", None, None, None),
            P("segment", None),
        ),
        check_vma=False,
    )
```

```python
from functools import partial

import jax
import jax.numpy as jnp
from jax import lax
from jax.experimental import pallas as pl
from jax.experimental.pallas import tpu as pltpu
from jax.sharding import PartitionSpec as P

HEADS = 16
DH = 16
BLKS = 16
SEGS = 8
ROWS = 128
WIDTH = 256
GROUP = 16
DUMMY = BLKS
eps = 1e-05
F32, BF16 = jnp.float32, jnp.bfloat16
VMEM_SPEC = pl.BlockSpec(memory_space=pltpu.VMEM)
SMEM_SPEC = pl.BlockSpec(memory_space=pltpu.SMEM)


def mm(a, b):
    return jnp.dot(a, b, preferred_element_type=F32)


def mm_nt(a, b):
    return lax.dot_general(a, b, (((1,), (1,)), ((), ())), preferred_element_type=F32)


def peers(me):
    return [lax.rem(me + k, BLKS) for k in range(1, BLKS)]


def signal(semaphore, where):
    pl.semaphore_signal(semaphore, inc=1, device_id=where, device_id_type=pl.DeviceIdType.MESH)


def greet(me, more=()):
    barrier = pltpu.get_barrier_semaphore()
    for peer in peers(me):
        signal(barrier, {"blk": peer})
    for seg in more:
        signal(barrier, {"segment": seg})


def all_in(more=()):
    pl.semaphore_wait(pltpu.get_barrier_semaphore(), BLKS - 1 + len(more))


def copy_to(src, dst, send, recv, where):
    return pltpu.make_async_remote_copy(
        src_ref=src,
        dst_ref=dst,
        send_sem=send,
        recv_sem=recv,
        device_id=where,
        device_id_type=pl.DeviceIdType.MESH,
    )


def swap_kernel(in_ref, out_ref, send, recv):
    me = lax.axis_index("blk")
    rows = out_ref.shape[0]
    greet(me)
    all_in()
    copies = [
        copy_to(
            in_ref.at[pl.ds(0, rows), peer], out_ref.at[:, me], send.at[k], recv.at[k], {"blk": peer}
        )
        for k, peer in enumerate(peers(me))
    ]
    for c in copies:
        c.start()
    out_ref[:, me] = in_ref[pl.ds(0, rows), me]
    for c in copies:
        c.wait()


def swap(values, rows):
    return pl.pallas_call(
        swap_kernel,
        out_shape=jax.ShapeDtypeStruct((rows,) + values.shape[1:], values.dtype),
        in_specs=[VMEM_SPEC],
        out_specs=VMEM_SPEC,
        scratch_shapes=[
            pltpu.SemaphoreType.DMA((BLKS - 1,)),
            pltpu.SemaphoreType.DMA((BLKS - 1,)),
        ],
        compiler_params=pltpu.CompilerParams(
            collective_id=0, has_side_effects=True, vmem_limit_bytes=16 << 20
        ),
        name="swap",
    )(values)


def total_kernel(in_ref, out_ref, got, own, send1, recv1, send2, recv2):
    me = lax.axis_index("blk")
    greet(me)
    all_in()
    first = [
        copy_to(in_ref.at[peer], got.at[me], send1.at[k], recv1.at[k], {"blk": peer})
        for k, peer in enumerate(peers(me))
    ]
    for c in first:
        c.start()
    got[me] = in_ref[me]
    for c in first:
        c.wait()
    acc = got[0].astype(F32)
    for b in range(1, BLKS):
        acc = acc + got[b].astype(F32)
    own[...] = acc.astype(BF16)
    second = [
        copy_to(own, out_ref.at[me], send2.at[k], recv2.at[k], {"blk": peer})
        for k, peer in enumerate(peers(me))
    ]
    for c in second:
        c.start()
    out_ref[me] = own[...]
    for c in second:
        c.wait()


def total(values, collective_id):
    sems = pltpu.SemaphoreType.DMA((BLKS - 1,))
    return pl.pallas_call(
        total_kernel,
        out_shape=jax.ShapeDtypeStruct(values.shape, BF16),
        in_specs=[VMEM_SPEC],
        out_specs=VMEM_SPEC,
        scratch_shapes=[
            pltpu.VMEM(values.shape, BF16),
            pltpu.VMEM(values.shape[1:], BF16),
            sems,
            sems,
            sems,
            sems,
        ],
        compiler_params=pltpu.CompilerParams(
            collective_id=collective_id, has_side_effects=True, vmem_limit_bytes=16 << 20
        ),
        name="total",
    )(values)


def step_kernel(
    last, walker_ref, parts_ref, x_ref, gain_ref, g_ref, fc_ref, w_ref, w_below_ref,
    cot_ref, gnext_ref, dout_ref, stash_ref,
    g_own, dout_own, ready, send1, recv1, hop_send, hop_recv, send2, recv2,
):
    me = lax.axis_index("blk")
    seg = lax.axis_index("segment")
    above, below = lax.rem(seg + 1, SEGS), lax.rem(seg + SEGS - 1, SEGS)
    near = () if last else (above, below)
    greet(me, near)
    x = x_ref[walker_ref[0]].astype(F32)
    inv = lax.rsqrt(jnp.mean(x * x, axis=0, keepdims=True) + eps)
    unit = x * inv
    all_in(near)
    first = [
        copy_to(parts_ref.at[:, peer], stash_ref.at[:, me], send1.at[k], recv1.at[k], {"blk": peer})
        for k, peer in enumerate(peers(me))
    ]
    for c in first:
        c.start()
    stash_ref[:, me] = parts_ref[:, me]
    g = g_ref[...].astype(F32)
    for c in first:
        c.wait_recv()
    if not last:
        signal(ready, {"segment": above})
    normed_grad = mm(w_ref[0], stash_ref[0].reshape(WIDTH, ROWS))
    for t in range(1, 3):
        normed_grad += mm(w_ref[t], stash_ref[t].reshape(WIDTH, ROWS))
    unit_grad = normed_grad * gain_ref[...]
    centre = jnp.mean(unit_grad * unit, axis=0, keepdims=True)
    cot = (g + inv * (unit_grad - unit * centre)).astype(BF16)
    cot_ref[...] = cot
    if last:
        gnext_ref[...] = cot
        dout_ref[...] = jnp.zeros_like(dout_ref)
    else:
        last_g = fc_ref[walker_ref[1]].astype(F32)
        g_below = jnp.where(seg == 0, last_g, cot.astype(F32)).astype(BF16)
        g_own[...] = g_below
        dout_own[...] = mm(w_below_ref[...], g_below).astype(BF16).reshape(HEADS, DH, ROWS)
        pl.semaphore_wait(ready, 1)
        second = []
        for k in range(BLKS):
            peer = lax.rem(me + k, BLKS)
            second.append(
                copy_to(
                    dout_own.at[peer], dout_ref.at[me], send2.at[k], recv2.at[k],
                    {"segment": below, "blk": peer},
                )
            )
        hop = copy_to(g_own, gnext_ref, hop_send, hop_recv, {"segment": below})
        for c in second:
            c.start()
        hop.start()
        for c in second:
            c.wait()
        hop.wait()
    for c in first:
        c.wait_send()


def step(last, walker_pair, parts, x_t, gain_col, g, fc_t, weights, w_below):
    sems = pltpu.SemaphoreType.DMA((BLKS - 1,))
    more = pltpu.SemaphoreType.DMA((BLKS,))
    tile = jax.ShapeDtypeStruct((WIDTH, ROWS), BF16)
    return pl.pallas_call(
        partial(step_kernel, last),
        out_shape=(
            tile,
            tile,
            jax.ShapeDtypeStruct((BLKS, DH, ROWS), BF16),
            jax.ShapeDtypeStruct((4, HEADS, DH, ROWS), BF16),
        ),
        in_specs=[SMEM_SPEC] + [VMEM_SPEC] * 7,
        out_specs=[VMEM_SPEC] * 4,
        scratch_shapes=[
            pltpu.VMEM((WIDTH, ROWS), BF16),
            pltpu.VMEM((HEADS, DH, ROWS), BF16),
            pltpu.SemaphoreType.REGULAR,
            sems,
            sems,
            pltpu.SemaphoreType.DMA,
            pltpu.SemaphoreType.DMA,
            more,
            more,
        ],
        compiler_params=pltpu.CompilerParams(
            collective_id=1 if last else 2, has_side_effects=True, vmem_limit_bytes=16 << 20
        ),
        name="last_step" if last else "step",
    )(walker_pair, parts, x_t, gain_col, g, fc_t, weights, w_below)


def prepare_kernel(x_ref, fc_ref, w_ref, gain_ref, x_out, fc_out, normed_out, qkv_out, turned_w):
    walker = pl.program_id(0)

    @pl.when(walker == 0)
    def _():
        for t in range(3):
            turned_w[t] = turned(w_ref[t])

    x = x_ref[0].astype(F32)
    inv = lax.rsqrt(jnp.mean(x * x, axis=1, keepdims=True) + eps)
    normed = jnp.transpose(x * inv * gain_ref[...]).astype(BF16)
    x_out[0] = jnp.transpose(x).astype(BF16)
    fc = turned(fc_ref[0])
    fc_out[0] = fc
    normed_out[0] = normed

    @pl.when(walker < pl.num_programs(0) - 1)
    def _():
        query = mm(turned_w[0], normed).astype(BF16) * jnp.asarray(0.25, BF16)
        qkv_out[0] = query.reshape(HEADS, DH, ROWS)
        for t in range(1, 3):
            qkv_out[t] = mm(turned_w[t], normed).astype(BF16).reshape(HEADS, DH, ROWS)

    @pl.when(walker == pl.num_programs(0) - 1)
    def _():
        first_g = turned(fc_ref[0])
        qkv_out[0] = mm(w_ref[3], first_g).astype(BF16).reshape(HEADS, DH, ROWS)
        qkv_out[1] = jnp.zeros((HEADS, DH, ROWS), BF16)
        qkv_out[2] = jnp.zeros((HEADS, DH, ROWS), BF16)


def prepare(x, fc, weights, gain):
    walkers = x.shape[0]

    def own(w):
        return (lax.rem(w, walkers), 0, 0)

    def tile():
        return pl.BlockSpec((1, WIDTH, ROWS), own)

    flat = jax.ShapeDtypeStruct((walkers, WIDTH, ROWS), BF16)
    return pl.pallas_call(
        prepare_kernel,
        grid=(walkers + 1,),
        in_specs=[
            pl.BlockSpec((1, ROWS, WIDTH), own),
            pl.BlockSpec((1, ROWS, WIDTH), own),
            pl.BlockSpec((4, WIDTH, WIDTH), lambda w: (0, 0, 0)),
            pl.BlockSpec((1, WIDTH), lambda w: (0, 0)),
        ],
        out_specs=[
            tile(),
            tile(),
            tile(),
            pl.BlockSpec((3, HEADS, DH, ROWS), lambda w: (w, 0, 0, 0)),
        ],
        out_shape=(
            flat,
            flat,
            flat,
            jax.ShapeDtypeStruct((3 * (walkers + 1), HEADS, DH, ROWS), BF16),
        ),
        scratch_shapes=[pltpu.VMEM((3, WIDTH, WIDTH), BF16)],
        compiler_params=pltpu.CompilerParams(vmem_limit_bytes=16 << 20),
        name="prepare",
    )(x, fc, weights, gain)


def turned(tile):
    return jnp.transpose(tile.astype(F32)).astype(BF16)


def forward_kernel(info_ref, qkv_ref, att_ref, lse_ref, k_nat, q_all, sums, lse, att):
    for b in range(BLKS):
        k_nat[b] = turned(qkv_ref[1, b])
        q_all[b] = qkv_ref[0, b]
    q_all[DUMMY] = jnp.zeros((DH, ROWS), BF16)
    sums[...] = jnp.zeros_like(sums)
    att[...] = jnp.zeros_like(att)
    groups = info_ref[2 * BLKS * 8]

    def group(n):
        return [(info_ref[n * GROUP + u], info_ref[BLKS * 8 + n * GROUP + u]) for u in range(GROUP)]

    def add_up(n, carry):
        pairs = group(n)
        scores = [mm(k_nat[j], q_all[a]) for a, j in pairs]
        parts = [jnp.sum(jnp.exp(s).reshape(ROWS // 8, 8, ROWS), axis=0) for s in scores]
        for (a, _), part in zip(pairs, parts):
            sums[a] += part
        return carry

    lax.fori_loop(0, groups, add_up, 0)
    for b in range(BLKS):
        lse[b] = jnp.log(jnp.sum(sums[b], axis=0, keepdims=True))
        lse_ref[0, b] = lse[b]
    lse[DUMMY] = jnp.full((1, ROWS), 1e30, F32)

    def attend(n, carry):
        pairs = group(n)
        scores = [mm(k_nat[j], q_all[a]) for a, j in pairs]
        probs = [jnp.exp(s - lse[a]).astype(BF16) for s, (a, _) in zip(scores, pairs)]
        parts = [mm(qkv_ref[2, j], p) for p, (_, j) in zip(probs, pairs)]
        for (a, _), part in zip(pairs, parts):
            att[a] += part
        return carry

    lax.fori_loop(0, groups, attend, 0)
    for b in range(BLKS):
        att_ref[0, b] = att[b].astype(BF16)


def forward(info, qkv, walkers):
    def spec(*tail):
        return pl.BlockSpec((1, BLKS) + tail, lambda w, s: (w, 0, 0, 0))

    return pl.pallas_call(
        forward_kernel,
        grid_spec=pltpu.PrefetchScalarGridSpec(
            num_scalar_prefetch=1,
            grid=(walkers,),
            in_specs=[pl.BlockSpec((3, BLKS, DH, ROWS), lambda w, s: (w, 0, 0, 0))],
            out_specs=[spec(DH, ROWS), spec(1, ROWS)],
            scratch_shapes=[
                pltpu.VMEM((BLKS, ROWS, DH), BF16),
                pltpu.VMEM((BLKS + 1, DH, ROWS), BF16),
                pltpu.VMEM((BLKS + 1, 8, ROWS), F32),
                pltpu.VMEM((BLKS + 1, 1, ROWS), F32),
                pltpu.VMEM((BLKS + 1, DH, ROWS), F32),
            ],
        ),
        out_shape=(
            jax.ShapeDtypeStruct((walkers, BLKS, DH, ROWS), BF16),
            jax.ShapeDtypeStruct((walkers, BLKS, 1, ROWS), F32),
        ),
        compiler_params=pltpu.CompilerParams(vmem_limit_bytes=24 << 20),
        name="forward",
    )(info, qkv)


def backward_kernel(
    info_ref, walker_ref, qkv_ref, att_ref, lse_ref, dout_ref, out_ref,
    kv_nat, q_dout, lse, delta, dq, dkv,
):
    nothing = jnp.zeros((DH, ROWS), BF16)
    for b in range(BLKS):
        kv_nat[b] = turned(jnp.concatenate([qkv_ref[1, b], qkv_ref[2, b]], axis=0))
        q_dout[b, 0:DH, 0:ROWS] = qkv_ref[0, b]
        q_dout[b, 0:DH, ROWS : 2 * ROWS] = nothing
        q_dout[b, DH : 2 * DH, 0:ROWS] = nothing
        q_dout[b, DH : 2 * DH, ROWS : 2 * ROWS] = dout_ref[b]
        lse[b] = lse_ref[0, b]
        delta[b] = jnp.sum(
            dout_ref[b].astype(F32) * att_ref[0, b].astype(F32), axis=0, keepdims=True
        )
    q_dout[DUMMY] = jnp.zeros((2 * DH, 2 * ROWS), BF16)
    lse[DUMMY] = jnp.full((1, ROWS), 1e30, F32)
    delta[DUMMY] = jnp.zeros((1, ROWS), F32)
    dq[...] = jnp.zeros_like(dq)
    dkv[...] = jnp.zeros_like(dkv)

    def body(n, carry):
        pairs = [(info_ref[n * GROUP + u], info_ref[BLKS * 8 + n * GROUP + u]) for u in range(GROUP)]
        sides = [q_dout[a] for a, _ in pairs]
        boths = [mm(kv_nat[j], side) for (_, j), side in zip(pairs, sides)]
        probs = [jnp.exp(both[:, 0:ROWS] - lse[a]) for both, (a, _) in zip(boths, pairs)]
        score_grads = [
            (prob * (both[:, ROWS : 2 * ROWS] - delta[a])).astype(BF16)
            for prob, both, (a, _) in zip(probs, boths, pairs)
        ]
        kv_parts = [
            mm_nt(side, jnp.concatenate([score_grad, prob.astype(BF16)], axis=1))
            for side, score_grad, prob in zip(sides, score_grads, probs)
        ]
        q_parts = [
            mm(qkv_ref[1, j], score_grad)
            for (_, j), score_grad in zip(pairs, score_grads)
        ]
        for (a, j), kv_part, q_part in zip(pairs, kv_parts, q_parts):
            dkv[j] += kv_part
            dq[a] += q_part
        return carry

    lax.fori_loop(0, info_ref[2 * BLKS * 8], body, 0)
    for b in range(BLKS):
        out_ref[0, b] = (dq[b] * 0.25).astype(BF16)
        out_ref[1, b] = dkv[b, 0:DH].astype(BF16)
        out_ref[2, b] = dkv[b, DH : 2 * DH].astype(BF16)
        out_ref[3, b] = att_ref[0, b]


def backward(info, walker_pair, qkv, att, lse, dout):
    def spec(*tail):
        return pl.BlockSpec((1, BLKS) + tail, lambda i, s, w: (w[0], 0, 0, 0))

    def whole(*dims):
        return pl.BlockSpec(dims, lambda i, s, w: (0,) * len(dims))

    return pl.pallas_call(
        backward_kernel,
        grid_spec=pltpu.PrefetchScalarGridSpec(
            num_scalar_prefetch=2,
            grid=(1,),
            in_specs=[
                pl.BlockSpec((3, BLKS, DH, ROWS), lambda i, s, w: (w[0], 0, 0, 0)),
                spec(DH, ROWS),
                spec(1, ROWS),
                whole(BLKS, DH, ROWS),
            ],
            out_specs=whole(4, BLKS, DH, ROWS),
            scratch_shapes=[
                pltpu.VMEM((BLKS, ROWS, 2 * DH), BF16),
                pltpu.VMEM((BLKS + 1, 2 * DH, 2 * ROWS), BF16),
                pltpu.VMEM((BLKS + 1, 1, ROWS), F32),
                pltpu.VMEM((BLKS + 1, 1, ROWS), F32),
                pltpu.VMEM((BLKS + 1, DH, ROWS), F32),
                pltpu.VMEM((BLKS, 2 * DH, ROWS), F32),
            ],
        ),
        out_shape=jax.ShapeDtypeStruct((4, BLKS, DH, ROWS), BF16),
        compiler_params=pltpu.CompilerParams(vmem_limit_bytes=16 << 20),
        name="backward",
    )(info, walker_pair, qkv, att, lse, dout)


def pair_table(pair_list, pair_count):
    blocks, slots = pair_list.shape
    pairs = blocks * slots
    keys = pair_list.T.reshape(-1)
    queries = jnp.tile(jnp.arange(blocks, dtype=jnp.int32), slots)
    used = (jnp.arange(slots)[:, None] < pair_count[None, :]).reshape(-1)
    order = jnp.arange(pairs)
    place = jnp.sum((order[None, :] < order[:, None]) & used[None, :], axis=1)
    chosen = (place[None, :] == order[:, None]) & used[None, :]
    count = jnp.sum(used.astype(jnp.int32))
    key_of = jnp.sum(jnp.where(chosen, keys[None, :], 0), axis=1)
    query_of = jnp.sum(jnp.where(chosen, queries[None, :], 0), axis=1)
    query_of = jnp.where(order < count, query_of, DUMMY)
    groups = (count + GROUP - 1) // GROUP
    return jnp.concatenate([query_of, key_of, groups[None]]).astype(jnp.int32)


def per_device(layer_inputs, final_cot, attn_weights, norm_gain, pair_list, pair_count):
    seg = lax.axis_index("segment")
    walkers = layer_inputs.shape[1]
    weights = attn_weights[0]
    gain_col = norm_gain[0][:, None]
    info = pair_table(pair_list, pair_count)
    w_below = lax.ppermute(weights[3], "segment", [(s, (s + 1) % SEGS) for s in range(SEGS)])
    x_t, fc_t, normed, qkv = prepare(layer_inputs[0], final_cot, weights, norm_gain)
    swapped = swap(qkv, 3 * walkers + 1)
    dout = swapped[3 * walkers]
    g = fc_t[0]
    att, lse = forward(info, swapped, walkers)

    ticks = walkers + SEGS - 1
    cots, gs, stashes = [], [], []
    for tick in range(ticks):
        now = jnp.clip(tick - (SEGS - 1 - seg), 0, walkers - 1)
        walker_pair = jnp.stack([now, min(tick + 1, walkers - 1)]).astype(jnp.int32)
        parts = backward(info, walker_pair, swapped, att, lse, dout)
        gs.append(g)
        cot, g, dout, stash = step(
            tick == ticks - 1, walker_pair, parts, x_t, gain_col, g, fc_t, weights, w_below
        )
        cots.append(cot)
        stashes.append(stash)

    def mine(values):
        return lax.dynamic_slice_in_dim(jnp.stack(values), SEGS - 1 - seg, walkers, 0)

    cots, gs, stashes = lax.optimization_barrier((cots, gs, stashes))
    cot_all, g_all = mine(cots), mine(gs)
    grads = mine(stashes).reshape(walkers, 4, WIDTH, ROWS)
    dw = jnp.einsum("wfi,wtci->tfc", normed, grads[:, :3], preferred_element_type=F32)
    dwo = jnp.einsum("wci,wfi->cf", grads[:, 3], g_all, preferred_element_type=F32)
    normed_grad = jnp.einsum("tfc,wtci->wfi", weights[:3], grads[:, :3], preferred_element_type=F32)
    feats = x_t.astype(F32)
    unit = feats * lax.rsqrt(jnp.mean(feats * feats, axis=1, keepdims=True) + eps)
    gain_part = jnp.sum(normed_grad * unit, axis=(0, 2))

    own = jnp.concatenate([dw, dwo[None]], axis=0).reshape(BLKS, 4 * WIDTH // BLKS, WIDTH)
    extra = jnp.zeros((BLKS, 16, WIDTH), F32).at[0, 0].set(gain_part)
    summed = total(jnp.concatenate([own, extra], axis=1).astype(BF16), 3).astype(F32)
    grad_total = summed[:, : 4 * WIDTH // BLKS].reshape(4, WIDTH, WIDTH)
    gain_total = summed[0, 4 * WIDTH // BLKS]
    return (jnp.swapaxes(cot_all, 1, 2)[None], grad_total[None], gain_total[None])


def solution(mesh):
    return jax.shard_map(
        per_device,
        mesh=mesh,
        in_specs=(
            P("segment", None, "blk", None),
            P(None, "blk", None),
            P("segment", None, None, None),
            P("segment", None),
            P(),
            P(),
        ),
        out_specs=(
            P("segment", None, "blk", None),
            P("segment", None, None, None),
            P("segment", None),
        ),
        check_vma=False,
    )
```

```python
from functools import partial

import jax
import jax.numpy as jnp
from jax import lax
from jax.experimental import pallas as pl
from jax.experimental.pallas import tpu as pltpu
from jax.sharding import PartitionSpec as P

HEADS = 16
DH = 16
BLKS = 16
SEGS = 8
ROWS = 128
WIDTH = 256
GROUP = 16
MAXN = 8
PAIRS = BLKS * MAXN + GROUP
DUMMY = BLKS
eps = 1e-05
F32, BF16 = jnp.float32, jnp.bfloat16
VMEM_SPEC = pl.BlockSpec(memory_space=pltpu.VMEM)
SMEM_SPEC = pl.BlockSpec(memory_space=pltpu.SMEM)


def mm(a, b):
    return jnp.dot(a, b, preferred_element_type=F32)


def mm_nt(a, b):
    return lax.dot_general(a, b, (((1,), (1,)), ((), ())), preferred_element_type=F32)


SIDE = 4
SHIFTS = sorted(
    [(dx, dy) for dx in range(SIDE) for dy in range(SIDE)],
    key=lambda s: -min(s[0], SIDE - s[0]) - min(s[1], SIDE - s[1]),
)


def blocks_from(me):
    x, y = me // SIDE, lax.rem(me, SIDE)
    return [lax.rem(x + dx, SIDE) * SIDE + lax.rem(y + dy, SIDE) for dx, dy in SHIFTS]


def peers(me):
    return blocks_from(me)[: BLKS - 1]


def signal(semaphore, where):
    pl.semaphore_signal(semaphore, inc=1, device_id=where, device_id_type=pl.DeviceIdType.MESH)


def greet(me, more=()):
    barrier = pltpu.get_barrier_semaphore()
    for peer in peers(me):
        signal(barrier, {"blk": peer})
    for seg in more:
        signal(barrier, {"segment": seg})


def all_in(more=()):
    pl.semaphore_wait(pltpu.get_barrier_semaphore(), BLKS - 1 + len(more))


def copy_to(src, dst, send, recv, where):
    return pltpu.make_async_remote_copy(
        src_ref=src,
        dst_ref=dst,
        send_sem=send,
        recv_sem=recv,
        device_id=where,
        device_id_type=pl.DeviceIdType.MESH,
    )


def swap_kernel(in_ref, w_ref, out_ref, below_ref, send, recv, w_send, w_recv):
    me = lax.axis_index("blk")
    seg = lax.axis_index("segment")
    above, below = lax.rem(seg + 1, SEGS), lax.rem(seg + SEGS - 1, SEGS)
    greet(me, (below,))
    all_in((above,))
    copies = [
        copy_to(in_ref.at[peer], out_ref.at[me], send.at[k], recv.at[k], {"blk": peer})
        for k, peer in enumerate(peers(me))
    ]
    copies.append(copy_to(w_ref, below_ref, w_send, w_recv, {"segment": above}))
    for c in copies:
        c.start()
    out_ref[me] = in_ref[me]
    for c in copies:
        c.wait()


def swap(values, w_out):
    sems = pltpu.SemaphoreType.DMA((BLKS - 1,))
    return pl.pallas_call(
        swap_kernel,
        out_shape=(
            jax.ShapeDtypeStruct(values.shape, values.dtype),
            jax.ShapeDtypeStruct(w_out.shape, w_out.dtype),
        ),
        in_specs=[VMEM_SPEC] * 2,
        out_specs=[VMEM_SPEC] * 2,
        scratch_shapes=[sems, sems, pltpu.SemaphoreType.DMA, pltpu.SemaphoreType.DMA],
        compiler_params=pltpu.CompilerParams(
            collective_id=0, has_side_effects=True, vmem_limit_bytes=16 << 20
        ),
        name="swap",
    )(values, w_out)


def total_kernel(
    in_ref, gain_ref, out_ref, gain_out, got, own, got_gain, send1, recv1, send2, recv2, send3, recv3
):
    me = lax.axis_index("blk")
    greet(me)
    all_in()
    first = [
        copy_to(in_ref.at[peer], got.at[me], send1.at[k], recv1.at[k], {"blk": peer})
        for k, peer in enumerate(peers(me))
    ]
    gains = [
        copy_to(gain_ref, got_gain.at[me], send3.at[k], recv3.at[k], {"blk": peer})
        for k, peer in enumerate(peers(me))
    ]
    for c in first:
        c.start()
    for c in gains:
        c.start()
    got[me] = in_ref[me]
    got_gain[me] = gain_ref[...]
    for c in first:
        c.wait_recv()
    acc = got[0].astype(F32)
    for b in range(1, BLKS):
        acc = acc + got[b].astype(F32)
    own[...] = acc.astype(BF16)
    second = [
        copy_to(own, out_ref.at[me], send2.at[k], recv2.at[k], {"blk": peer})
        for k, peer in enumerate(peers(me))
    ]
    for c in second:
        c.start()
    out_ref[me] = own[...]
    for c in gains:
        c.wait()
    gain_out[...] = jnp.sum(got_gain[...], axis=0)
    for c in first:
        c.wait_send()
    for c in second:
        c.wait()


def total(values, gains, collective_id):
    sems = pltpu.SemaphoreType.DMA((BLKS - 1,))
    return pl.pallas_call(
        total_kernel,
        out_shape=(
            jax.ShapeDtypeStruct(values.shape, BF16),
            jax.ShapeDtypeStruct(gains.shape, F32),
        ),
        in_specs=[VMEM_SPEC] * 2,
        out_specs=[VMEM_SPEC] * 2,
        scratch_shapes=[
            pltpu.VMEM(values.shape, BF16),
            pltpu.VMEM(values.shape[1:], BF16),
            pltpu.VMEM((BLKS,) + gains.shape, F32),
        ]
        + [sems] * 6,
        compiler_params=pltpu.CompilerParams(
            collective_id=collective_id, has_side_effects=True, vmem_limit_bytes=16 << 20
        ),
        name="total",
    )(values, gains)


def local_grads(walker_ref, x_ref, gain_ref, g_ref, w_ref):
    x = x_ref[walker_ref[0]].astype(F32)
    inv = lax.rsqrt(jnp.mean(x * x, axis=0, keepdims=True) + eps)
    unit = x * inv
    g = g_ref[...].astype(F32)

    def finish(stash_ref):
        normed_grad = mm(w_ref[0], stash_ref[:, 0].reshape(WIDTH, ROWS))
        for t in range(1, 3):
            normed_grad += mm(w_ref[t], stash_ref[:, t].reshape(WIDTH, ROWS))
        unit_grad = normed_grad * gain_ref[...]
        centre = jnp.mean(unit_grad * unit, axis=0, keepdims=True)
        return (g + inv * (unit_grad - unit * centre)).astype(BF16)

    return finish


def send_parts(me, parts_ref, stash_ref, send, recv):
    copies = [
        copy_to(parts_ref.at[peer], stash_ref.at[me], send.at[k], recv.at[k], {"blk": peer})
        for k, peer in enumerate(peers(me))
    ]
    for c in copies:
        c.start()
    stash_ref[me] = parts_ref[me]
    return copies


def step_kernel(
    walker_ref, list_ref, count_ref, parts_ref, x_ref, gain_ref, g_ref, fc_ref, w_ref, w_below_ref, qkv_ref,
    cot_ref, stash_ref, gnext_ref, dout_ref, att_ref, lse_ref,
    k_nat, q_all, v_all, g_own, dout_own, ready, send1, recv1, hop_send, hop_recv, send2, recv2,
):
    me = lax.axis_index("blk")
    seg = lax.axis_index("segment")
    above, below = lax.rem(seg + 1, SEGS), lax.rem(seg + SEGS - 1, SEGS)
    near = (above, below)
    greet(me, near)
    grads = local_grads(walker_ref, x_ref, gain_ref, g_ref, w_ref)
    head_tiles(lambda t, b: qkv_ref[b, 3 * walker_ref[2] + t], k_nat, q_all, v_all)
    all_in(near)
    first = send_parts(me, parts_ref, stash_ref, send1, recv1)
    row_sums(list_ref, count_ref, k_nat, q_all, lse_ref)
    for c in first:
        c.wait_recv()
    signal(ready, {"segment": above})
    cot = grads(stash_ref)
    cot_ref[...] = cot
    last_g = fc_ref[walker_ref[1]].astype(F32)
    g_below = jnp.where(seg == 0, last_g, cot.astype(F32)).astype(BF16)
    g_own[...] = g_below
    dout_own[...] = mm(w_below_ref[...], g_below).astype(BF16).reshape(HEADS, DH, ROWS)
    pl.semaphore_wait(ready, 1)
    second = [
        copy_to(
            dout_own.at[peer], dout_ref.at[me], send2.at[k], recv2.at[k],
            {"segment": below, "blk": peer},
        )
        for k, peer in enumerate(blocks_from(me))
    ]
    second.append(copy_to(g_own, gnext_ref, hop_send, hop_recv, {"segment": below}))
    for c in second:
        c.start()
    attend_rows(list_ref, count_ref, k_nat, q_all, v_all, lse_ref, att_ref)
    for c in second:
        c.wait()
    for c in first:
        c.wait_send()


def last_step_kernel(
    walker_ref, parts_ref, x_ref, gain_ref, g_ref, w_ref, cot_ref, stash_ref, send1, recv1
):
    me = lax.axis_index("blk")
    greet(me)
    grads = local_grads(walker_ref, x_ref, gain_ref, g_ref, w_ref)
    all_in()
    first = send_parts(me, parts_ref, stash_ref, send1, recv1)
    for c in first:
        c.wait()
    cot_ref[...] = grads(stash_ref)


TILE = jax.ShapeDtypeStruct((WIDTH, ROWS), BF16)
STASH = jax.ShapeDtypeStruct((HEADS, 4, DH, ROWS), BF16)
ATTENDED = jax.ShapeDtypeStruct((BLKS, DH, ROWS), BF16)
LOG_SUMS = jax.ShapeDtypeStruct((BLKS, 1, ROWS), F32)
HEAD_TILES = [
    pltpu.VMEM((BLKS, ROWS, DH), BF16),
    pltpu.VMEM((BLKS, DH, ROWS), BF16),
    pltpu.VMEM((BLKS, DH, ROWS), BF16),
]


def step(picks, pair_list, pair_count, parts, x_t, gain_col, g, fc_t, weights, w_below, qkv):
    sems = pltpu.SemaphoreType.DMA((BLKS - 1,))
    more = pltpu.SemaphoreType.DMA((BLKS,))
    return pl.pallas_call(
        step_kernel,
        out_shape=(TILE, STASH, TILE, ATTENDED, ATTENDED, LOG_SUMS),
        in_specs=[SMEM_SPEC] * 3 + [VMEM_SPEC] * 8,
        out_specs=[VMEM_SPEC] * 6,
        scratch_shapes=HEAD_TILES
        + [
            pltpu.VMEM((WIDTH, ROWS), BF16),
            pltpu.VMEM((HEADS, DH, ROWS), BF16),
            pltpu.SemaphoreType.REGULAR,
            sems,
            sems,
            pltpu.SemaphoreType.DMA,
            pltpu.SemaphoreType.DMA,
            more,
            more,
        ],
        compiler_params=pltpu.CompilerParams(
            collective_id=2, has_side_effects=True, vmem_limit_bytes=24 << 20
        ),
        name="step",
    )(picks, pair_list, pair_count, parts, x_t, gain_col, g, fc_t, weights, w_below, qkv)


def last_step(picks, parts, x_t, gain_col, g, weights):
    sems = pltpu.SemaphoreType.DMA((BLKS - 1,))
    return pl.pallas_call(
        last_step_kernel,
        out_shape=(TILE, STASH),
        in_specs=[SMEM_SPEC] + [VMEM_SPEC] * 5,
        out_specs=[VMEM_SPEC] * 2,
        scratch_shapes=[sems, sems],
        compiler_params=pltpu.CompilerParams(
            collective_id=1, has_side_effects=True, vmem_limit_bytes=16 << 20
        ),
        name="last_step",
    )(picks, parts, x_t, gain_col, g, weights)


def prepare_kernel(x_ref, fc_ref, w_ref, gain_ref, x_out, fc_out, normed_out, qkv_out, turned_w):
    walker = pl.program_id(0)

    @pl.when(walker == 0)
    def _():
        for t in range(3):
            turned_w[t] = turned(w_ref[t])

    x = x_ref[0].astype(F32)
    inv = lax.rsqrt(jnp.mean(x * x, axis=1, keepdims=True) + eps)
    normed = jnp.transpose(x * inv * gain_ref[...]).astype(BF16)
    x_out[0] = jnp.transpose(x).astype(BF16)
    fc = turned(fc_ref[0])
    fc_out[0] = fc
    normed_out[0] = normed

    @pl.when(walker < pl.num_programs(0) - 1)
    def _():
        query = mm(turned_w[0], normed).astype(BF16) * jnp.asarray(0.25, BF16)
        qkv_out[:, 0] = query.reshape(HEADS, DH, ROWS)
        for t in range(1, 3):
            qkv_out[:, t] = mm(turned_w[t], normed).astype(BF16).reshape(HEADS, DH, ROWS)

    @pl.when(walker == pl.num_programs(0) - 1)
    def _():
        first_g = turned(fc_ref[0])
        qkv_out[:, 0] = mm(w_ref[3], first_g).astype(BF16).reshape(HEADS, DH, ROWS)


def prepare(x, fc, weights, gain):
    walkers = x.shape[0]

    def own(w):
        return (lax.rem(w, walkers), 0, 0)

    def tile():
        return pl.BlockSpec((1, WIDTH, ROWS), own)

    flat = jax.ShapeDtypeStruct((walkers, WIDTH, ROWS), BF16)
    return pl.pallas_call(
        prepare_kernel,
        grid=(walkers + 1,),
        in_specs=[
            pl.BlockSpec((1, ROWS, WIDTH), own),
            pl.BlockSpec((1, ROWS, WIDTH), own),
            pl.BlockSpec((4, WIDTH, WIDTH), lambda w: (0, 0, 0)),
            pl.BlockSpec((1, WIDTH), lambda w: (0, 0)),
        ],
        out_specs=[
            tile(),
            tile(),
            tile(),
            pl.BlockSpec((HEADS, 3, DH, ROWS), lambda w: (0, w, 0, 0)),
        ],
        out_shape=(
            flat,
            flat,
            flat,
            jax.ShapeDtypeStruct((HEADS, 3 * walkers + 1, DH, ROWS), BF16),
        ),
        scratch_shapes=[pltpu.VMEM((3, WIDTH, WIDTH), BF16)],
        compiler_params=pltpu.CompilerParams(vmem_limit_bytes=48 << 20),
        name="prepare",
    )(x, fc, weights, gain)


def turned(tile):
    return jnp.transpose(tile.astype(F32)).astype(BF16)


def head_tiles(tile, k_nat, q_all, v_all):
    for b in range(BLKS):
        k_nat[b] = turned(tile(1, b))
        q_all[b] = tile(0, b)
        v_all[b] = tile(2, b)


def slots(n, list_ref):
    a = [2 * n + c // MAXN for c in range(2 * MAXN)]
    return [(a[c], c % MAXN, list_ref[a[c], c % MAXN]) for c in range(2 * MAXN)]


def row_sums(list_ref, count_ref, k_nat, q_all, lse_ref):
    def body(n, carry):
        some = slots(n, list_ref)
        scores = [mm(k_nat[j], q_all[a]) for a, _, j in some]
        parts = [jnp.sum(jnp.exp(s).reshape(ROWS // 8, 8, ROWS), axis=0) for s in scores]
        parts = [
            jnp.where(c < count_ref[a], part, 0.0) for part, (a, c, _) in zip(parts, some)
        ]
        for u in range(2):
            row = parts[u * MAXN]
            for part in parts[u * MAXN + 1 : (u + 1) * MAXN]:
                row = row + part
            lse_ref[2 * n + u] = jnp.log(jnp.sum(row, axis=0, keepdims=True))
        return carry

    lax.fori_loop(0, BLKS // 2, body, 0)


def attend_rows(list_ref, count_ref, k_nat, q_all, v_all, lse_ref, att_ref):
    def body(n, carry):
        some = slots(n, list_ref)
        scores = [mm(k_nat[j], q_all[a]) for a, _, j in some]
        shifts = [lse_ref[a] + jnp.where(c < count_ref[a], 0.0, 1e30) for a, c, _ in some]
        probs = [jnp.exp(s - shift).astype(BF16) for s, shift in zip(scores, shifts)]
        parts = [mm(v_all[j], p) for p, (_, _, j) in zip(probs, some)]
        for u in range(2):
            row = parts[u * MAXN]
            for part in parts[u * MAXN + 1 : (u + 1) * MAXN]:
                row = row + part
            att_ref[2 * n + u] = row.astype(BF16)
        return carry

    lax.fori_loop(0, BLKS // 2, body, 0)


def forward_kernel(list_ref, count_ref, qkv_ref, att_ref, lse_ref, info_ref, k_nat, q_all, v_all):
    def note(n, place):
        c, a = n // BLKS, lax.rem(n, BLKS)
        info_ref[place] = a
        info_ref[PAIRS + place] = list_ref[a, c]
        return place + jnp.where(c < count_ref[a], 1, 0)

    used = lax.fori_loop(0, BLKS * MAXN, note, 0)
    for k in range(GROUP):
        info_ref[used + k] = DUMMY
        info_ref[PAIRS + used + k] = 0
    info_ref[2 * PAIRS] = (used + GROUP - 1) // GROUP
    head_tiles(lambda t, b: qkv_ref[b, t], k_nat, q_all, v_all)
    row_sums(list_ref, count_ref, k_nat, q_all, lse_ref)
    attend_rows(list_ref, count_ref, k_nat, q_all, v_all, lse_ref, att_ref)


def forward(pair_list, pair_count, qkv):
    return pl.pallas_call(
        forward_kernel,
        grid=(1,),
        in_specs=[
            SMEM_SPEC,
            SMEM_SPEC,
            pl.BlockSpec((BLKS, 3, DH, ROWS), lambda i: (0, 0, 0, 0)),
        ],
        out_specs=[
            pl.BlockSpec((BLKS, DH, ROWS), lambda i: (0, 0, 0)),
            pl.BlockSpec((BLKS, 1, ROWS), lambda i: (0, 0, 0)),
            SMEM_SPEC,
        ],
        out_shape=(ATTENDED, LOG_SUMS, jax.ShapeDtypeStruct((2 * PAIRS + 1,), jnp.int32)),
        scratch_shapes=HEAD_TILES,
        compiler_params=pltpu.CompilerParams(vmem_limit_bytes=24 << 20),
        name="forward",
    )(pair_list, pair_count, qkv)


def backward_kernel(
    info_ref, walker_ref, qkv_ref, att_ref, lse_ref, dout_ref, out_ref,
    kv_nat, q_dout, lse, delta, dq, dkv,
):
    nothing = jnp.zeros((DH, ROWS), BF16)
    for b in range(BLKS):
        kv_nat[b] = turned(jnp.concatenate([qkv_ref[b, 1], qkv_ref[b, 2]], axis=0))
        q_dout[b, 0:DH, 0:ROWS] = qkv_ref[b, 0]
        q_dout[b, 0:DH, ROWS : 2 * ROWS] = nothing
        q_dout[b, DH : 2 * DH, 0:ROWS] = nothing
        q_dout[b, DH : 2 * DH, ROWS : 2 * ROWS] = dout_ref[b]
        lse[b] = lse_ref[b]
        delta[b] = jnp.sum(
            dout_ref[b].astype(F32) * att_ref[b].astype(F32), axis=0, keepdims=True
        )
    q_dout[DUMMY] = jnp.zeros((2 * DH, 2 * ROWS), BF16)
    lse[DUMMY] = jnp.full((1, ROWS), 1e30, F32)
    delta[DUMMY] = jnp.zeros((1, ROWS), F32)
    dq[...] = jnp.zeros_like(dq)
    dkv[...] = jnp.zeros_like(dkv)

    def body(n, carry):
        pairs = [(info_ref[n * GROUP + u], info_ref[PAIRS + n * GROUP + u]) for u in range(GROUP)]
        sides = [q_dout[a] for a, _ in pairs]
        boths = [mm(kv_nat[j], side) for (_, j), side in zip(pairs, sides)]
        probs = [jnp.exp(both[:, 0:ROWS] - lse[a]) for both, (a, _) in zip(boths, pairs)]
        score_grads = [
            (prob * (both[:, ROWS : 2 * ROWS] - delta[a])).astype(BF16)
            for prob, both, (a, _) in zip(probs, boths, pairs)
        ]
        kv_parts = [
            mm_nt(side, jnp.concatenate([score_grad, prob.astype(BF16)], axis=1))
            for side, score_grad, prob in zip(sides, score_grads, probs)
        ]
        q_parts = [
            mm(qkv_ref[j, 1], score_grad)
            for (_, j), score_grad in zip(pairs, score_grads)
        ]
        for (a, j), kv_part, q_part in zip(pairs, kv_parts, q_parts):
            dkv[j] += kv_part
            dq[a] += q_part
        return carry

    lax.fori_loop(0, info_ref[2 * PAIRS], body, 0)
    for b in range(BLKS):
        out_ref[b, 0] = (dq[b] * 0.25).astype(BF16)
        out_ref[b, 1] = dkv[b, 0:DH].astype(BF16)
        out_ref[b, 2] = dkv[b, DH : 2 * DH].astype(BF16)
        out_ref[b, 3] = att_ref[b]


def backward(info, walker_pair, qkv, att, lse, dout):
    def whole(*dims):
        return pl.BlockSpec(dims, lambda i, s, w: (0,) * len(dims))

    return pl.pallas_call(
        backward_kernel,
        grid_spec=pltpu.PrefetchScalarGridSpec(
            num_scalar_prefetch=2,
            grid=(1,),
            in_specs=[
                pl.BlockSpec((BLKS, 3, DH, ROWS), lambda i, s, w: (0, w[0], 0, 0)),
                whole(BLKS, DH, ROWS),
                whole(BLKS, 1, ROWS),
                whole(BLKS, DH, ROWS),
            ],
            out_specs=whole(BLKS, 4, DH, ROWS),
            scratch_shapes=[
                pltpu.VMEM((BLKS, ROWS, 2 * DH), BF16),
                pltpu.VMEM((BLKS + 1, 2 * DH, 2 * ROWS), BF16),
                pltpu.VMEM((BLKS + 1, 1, ROWS), F32),
                pltpu.VMEM((BLKS + 1, 1, ROWS), F32),
                pltpu.VMEM((BLKS + 1, DH, ROWS), F32),
                pltpu.VMEM((BLKS, 2 * DH, ROWS), F32),
            ],
        ),
        out_shape=STASH,
        compiler_params=pltpu.CompilerParams(vmem_limit_bytes=16 << 20),
        name="backward",
    )(info, walker_pair, qkv, att, lse, dout)


def per_device(layer_inputs, final_cot, attn_weights, norm_gain, pair_list, pair_count):
    seg = lax.axis_index("segment")
    walkers = layer_inputs.shape[1]
    weights = attn_weights[0]
    gain_col = norm_gain[0][:, None]
    x_t, fc_t, normed, qkv = prepare(layer_inputs[0], final_cot, weights, norm_gain)
    qkv, w_below = swap(qkv, weights[3])
    dout = qkv[:, 3 * walkers]
    g = fc_t[0]
    att, lse, info = forward(pair_list, pair_count, qkv)

    ticks = walkers + SEGS - 1
    cots, gs, stashes = [], [], []
    for tick in range(ticks):
        first = tick - (SEGS - 1 - seg)
        picks = jnp.stack([first, jnp.int32(tick + 1), first + 1])
        picks = jnp.clip(picks, 0, walkers - 1).astype(jnp.int32)
        parts = backward(info, picks, qkv, att, lse, dout)
        gs.append(g)
        if tick < ticks - 1:
            cot, stash, g, dout, att, lse = step(
                picks, pair_list, pair_count, parts, x_t, gain_col, g, fc_t, weights, w_below, qkv
            )
        else:
            cot, stash = last_step(picks, parts, x_t, gain_col, g, weights)
        cots.append(cot)
        stashes.append(stash)

    def mine(values):
        return lax.dynamic_slice_in_dim(jnp.stack(values), SEGS - 1 - seg, walkers, 0)

    cots, gs, stashes = lax.optimization_barrier((cots, gs, stashes))
    cot_all, g_all = mine(cots), mine(gs)
    grads = jnp.swapaxes(mine(stashes), 1, 2).reshape(walkers, 4, WIDTH, ROWS)
    dw = jnp.einsum("wfi,wtci->tfc", normed, grads[:, :3], preferred_element_type=F32)
    dwo = jnp.einsum("wci,wfi->cf", grads[:, 3], g_all, preferred_element_type=F32)
    normed_grad = jnp.einsum("tfc,wtci->wfi", weights[:3], grads[:, :3], preferred_element_type=F32)
    feats = x_t.astype(F32)
    unit = feats * lax.rsqrt(jnp.mean(feats * feats, axis=1, keepdims=True) + eps)
    gain_part = jnp.sum(normed_grad * unit, axis=(0, 2))

    own = jnp.concatenate([dw, dwo[None]], axis=0).reshape(BLKS, 4 * WIDTH // BLKS, WIDTH)
    gains = jnp.pad(gain_part.reshape(2, ROWS), ((0, 6), (0, 0)))
    summed, gain_sum = total(own.astype(BF16), gains, 3)
    grad_total = summed.reshape(4, WIDTH, WIDTH).astype(F32)
    gain_total = gain_sum[:2].reshape(WIDTH)
    return (jnp.swapaxes(cot_all, 1, 2)[None], grad_total[None], gain_total[None])


def solution(mesh):
    return jax.shard_map(
        per_device,
        mesh=mesh,
        in_specs=(
            P("segment", None, "blk", None),
            P(None, "blk", None),
            P("segment", None, None, None),
            P("segment", None),
            P(),
            P(),
        ),
        out_specs=(
            P("segment", None, "blk", None),
            P("segment", None, None, None),
            P("segment", None),
        ),
        check_vma=False,
    )
```

```python
from functools import partial

import jax
import jax.numpy as jnp
from jax import lax
from jax.experimental import pallas as pl
from jax.experimental.pallas import tpu as pltpu
from jax.sharding import PartitionSpec as P

HEADS = 16
DH = 16
BLKS = 16
SEGS = 8
ROWS = 128
WIDTH = 256
GROUP = 16
MAXN = 8
PAIRS = BLKS * MAXN + GROUP
DUMMY = BLKS
eps = 1e-05
F32, BF16 = jnp.float32, jnp.bfloat16
VMEM_SPEC = pl.BlockSpec(memory_space=pltpu.VMEM)
SMEM_SPEC = pl.BlockSpec(memory_space=pltpu.SMEM)


def mm(a, b):
    return jnp.dot(a, b, preferred_element_type=F32)


def mm_nt(a, b):
    return lax.dot_general(a, b, (((1,), (1,)), ((), ())), preferred_element_type=F32)


SIDE = 4
SHIFTS = sorted(
    [(dx, dy) for dx in range(SIDE) for dy in range(SIDE)],
    key=lambda s: -min(s[0], SIDE - s[0]) - min(s[1], SIDE - s[1]),
)


def blocks_from(me):
    x, y = me // SIDE, lax.rem(me, SIDE)
    return [lax.rem(x + dx, SIDE) * SIDE + lax.rem(y + dy, SIDE) for dx, dy in SHIFTS]


def peers(me):
    return blocks_from(me)[: BLKS - 1]


def signal(semaphore, where):
    pl.semaphore_signal(semaphore, inc=1, device_id=where, device_id_type=pl.DeviceIdType.MESH)


def greet(me, more=()):
    barrier = pltpu.get_barrier_semaphore()
    for peer in peers(me):
        signal(barrier, {"blk": peer})
    for seg in more:
        signal(barrier, {"segment": seg})


def all_in(more=()):
    pl.semaphore_wait(pltpu.get_barrier_semaphore(), BLKS - 1 + len(more))


def copy_to(src, dst, send, recv, where):
    return pltpu.make_async_remote_copy(
        src_ref=src,
        dst_ref=dst,
        send_sem=send,
        recv_sem=recv,
        device_id=where,
        device_id_type=pl.DeviceIdType.MESH,
    )


def swap_kernel(in_ref, w_ref, out_ref, below_ref, send, recv, w_send, w_recv):
    me = lax.axis_index("blk")
    seg = lax.axis_index("segment")
    above, below = lax.rem(seg + 1, SEGS), lax.rem(seg + SEGS - 1, SEGS)
    greet(me, (below,))
    all_in((above,))
    copies = [
        copy_to(in_ref.at[peer], out_ref.at[me], send.at[k], recv.at[k], {"blk": peer})
        for k, peer in enumerate(peers(me))
    ]
    copies.append(copy_to(w_ref, below_ref, w_send, w_recv, {"segment": above}))
    for c in copies:
        c.start()
    out_ref[me] = in_ref[me]
    for c in copies:
        c.wait()


def swap(values, w_out):
    sems = pltpu.SemaphoreType.DMA((BLKS - 1,))
    return pl.pallas_call(
        swap_kernel,
        out_shape=(
            jax.ShapeDtypeStruct(values.shape, values.dtype),
            jax.ShapeDtypeStruct(w_out.shape, w_out.dtype),
        ),
        in_specs=[VMEM_SPEC] * 2,
        out_specs=[VMEM_SPEC] * 2,
        scratch_shapes=[sems, sems, pltpu.SemaphoreType.DMA, pltpu.SemaphoreType.DMA],
        compiler_params=pltpu.CompilerParams(
            collective_id=0, has_side_effects=True, vmem_limit_bytes=16 << 20
        ),
        name="swap",
    )(values, w_out)


def total_kernel(
    in_ref, gain_ref, out_ref, gain_out, got, own, got_gain, send1, recv1, send2, recv2, send3, recv3
):
    me = lax.axis_index("blk")
    greet(me)
    all_in()
    first = [
        copy_to(in_ref.at[peer], got.at[me], send1.at[k], recv1.at[k], {"blk": peer})
        for k, peer in enumerate(peers(me))
    ]
    gains = [
        copy_to(gain_ref, got_gain.at[me], send3.at[k], recv3.at[k], {"blk": peer})
        for k, peer in enumerate(peers(me))
    ]
    for c in first:
        c.start()
    for c in gains:
        c.start()
    got[me] = in_ref[me]
    got_gain[me] = gain_ref[...]
    for c in first:
        c.wait_recv()
    acc = got[0].astype(F32)
    for b in range(1, BLKS):
        acc = acc + got[b].astype(F32)
    own[...] = acc.astype(BF16)
    second = [
        copy_to(own, out_ref.at[me], send2.at[k], recv2.at[k], {"blk": peer})
        for k, peer in enumerate(peers(me))
    ]
    for c in second:
        c.start()
    out_ref[me] = own[...]
    for c in gains:
        c.wait()
    gain_out[...] = jnp.sum(got_gain[...], axis=0)
    for c in first:
        c.wait_send()
    for c in second:
        c.wait()


def total(values, gains, collective_id):
    sems = pltpu.SemaphoreType.DMA((BLKS - 1,))
    return pl.pallas_call(
        total_kernel,
        out_shape=(
            jax.ShapeDtypeStruct(values.shape, BF16),
            jax.ShapeDtypeStruct(gains.shape, F32),
        ),
        in_specs=[VMEM_SPEC] * 2,
        out_specs=[VMEM_SPEC] * 2,
        scratch_shapes=[
            pltpu.VMEM(values.shape, BF16),
            pltpu.VMEM(values.shape[1:], BF16),
            pltpu.VMEM((BLKS,) + gains.shape, F32),
        ]
        + [sems] * 6,
        compiler_params=pltpu.CompilerParams(
            collective_id=collective_id, has_side_effects=True, vmem_limit_bytes=16 << 20
        ),
        name="total",
    )(values, gains)


def local_grads(walker_ref, x_ref, gain_ref, g_ref, w_ref):
    x = x_ref[walker_ref[0]].astype(F32)
    inv = lax.rsqrt(jnp.mean(x * x, axis=0, keepdims=True) + eps)
    unit = x * inv
    g = g_ref[...].astype(F32)

    def finish(stash_ref):
        normed_grad = mm(w_ref[0], stash_ref[:, 0].reshape(WIDTH, ROWS))
        for t in range(1, 3):
            normed_grad += mm(w_ref[t], stash_ref[:, t].reshape(WIDTH, ROWS))
        unit_grad = normed_grad * gain_ref[...]
        centre = jnp.mean(unit_grad * unit, axis=0, keepdims=True)
        return (g + inv * (unit_grad - unit * centre)).astype(BF16)

    return finish


def send_parts(me, parts_ref, stash_ref, send, recv):
    copies = [
        copy_to(parts_ref.at[peer], stash_ref.at[me], send.at[k], recv.at[k], {"blk": peer})
        for k, peer in enumerate(peers(me))
    ]
    for c in copies:
        c.start()
    stash_ref[me] = parts_ref[me]
    return copies


def step_kernel(
    walker_ref, list_ref, count_ref, parts_ref, x_ref, gain_ref, g_ref, fc_ref, w_ref, w_below_ref, qkv_ref,
    cot_ref, stash_ref, gnext_ref, dout_ref, att_ref, lse_ref,
    k_nat, q_all, v_all, g_own, dout_own, ready, send1, recv1, hop_send, hop_recv, send2, recv2,
):
    me = lax.axis_index("blk")
    seg = lax.axis_index("segment")
    above, below = lax.rem(seg + 1, SEGS), lax.rem(seg + SEGS - 1, SEGS)
    near = (above, below)
    greet(me, near)
    grads = local_grads(walker_ref, x_ref, gain_ref, g_ref, w_ref)
    head_tiles(lambda t, b: qkv_ref[b, 3 * walker_ref[2] + t], k_nat, q_all, v_all)
    all_in(near)
    first = send_parts(me, parts_ref, stash_ref, send1, recv1)
    row_sums(list_ref, count_ref, k_nat, q_all, lse_ref)
    for c in first:
        c.wait_recv()
    signal(ready, {"segment": above})
    cot = grads(stash_ref)
    cot_ref[...] = cot
    last_g = fc_ref[walker_ref[1]].astype(F32)
    g_below = jnp.where(seg == 0, last_g, cot.astype(F32)).astype(BF16)
    g_own[...] = g_below
    dout_own[...] = mm(w_below_ref[...], g_below).astype(BF16).reshape(HEADS, DH, ROWS)
    pl.semaphore_wait(ready, 1)
    second = [
        copy_to(
            dout_own.at[peer], dout_ref.at[me], send2.at[k], recv2.at[k],
            {"segment": below, "blk": peer},
        )
        for k, peer in enumerate(blocks_from(me))
    ]
    second.append(copy_to(g_own, gnext_ref, hop_send, hop_recv, {"segment": below}))
    for c in second:
        c.start()
    attend_rows(list_ref, count_ref, k_nat, q_all, v_all, lse_ref, att_ref)
    for c in second:
        c.wait()
    for c in first:
        c.wait_send()


def last_step_kernel(
    walker_ref, parts_ref, x_ref, gain_ref, g_ref, w_ref, cot_ref, stash_ref, send1, recv1
):
    me = lax.axis_index("blk")
    greet(me)
    grads = local_grads(walker_ref, x_ref, gain_ref, g_ref, w_ref)
    all_in()
    first = send_parts(me, parts_ref, stash_ref, send1, recv1)
    for c in first:
        c.wait()
    cot_ref[...] = grads(stash_ref)


TILE = jax.ShapeDtypeStruct((WIDTH, ROWS), BF16)
STASH = jax.ShapeDtypeStruct((HEADS, 4, DH, ROWS), BF16)
ATTENDED = jax.ShapeDtypeStruct((BLKS, DH, ROWS), BF16)
LOG_SUMS = jax.ShapeDtypeStruct((BLKS, 1, ROWS), F32)
HEAD_TILES = [
    pltpu.VMEM((BLKS, ROWS, DH), BF16),
    pltpu.VMEM((BLKS, DH, ROWS), BF16),
    pltpu.VMEM((BLKS, DH, ROWS), BF16),
]


def step(picks, pair_list, pair_count, parts, x_t, gain_col, g, fc_t, weights, w_below, qkv):
    sems = pltpu.SemaphoreType.DMA((BLKS - 1,))
    more = pltpu.SemaphoreType.DMA((BLKS,))
    return pl.pallas_call(
        step_kernel,
        out_shape=(TILE, STASH, TILE, ATTENDED, ATTENDED, LOG_SUMS),
        in_specs=[SMEM_SPEC] * 3 + [VMEM_SPEC] * 8,
        out_specs=[VMEM_SPEC] * 6,
        scratch_shapes=HEAD_TILES
        + [
            pltpu.VMEM((WIDTH, ROWS), BF16),
            pltpu.VMEM((HEADS, DH, ROWS), BF16),
            pltpu.SemaphoreType.REGULAR,
            sems,
            sems,
            pltpu.SemaphoreType.DMA,
            pltpu.SemaphoreType.DMA,
            more,
            more,
        ],
        compiler_params=pltpu.CompilerParams(
            collective_id=2, has_side_effects=True, vmem_limit_bytes=24 << 20
        ),
        name="step",
    )(picks, pair_list, pair_count, parts, x_t, gain_col, g, fc_t, weights, w_below, qkv)


def last_step(picks, parts, x_t, gain_col, g, weights):
    sems = pltpu.SemaphoreType.DMA((BLKS - 1,))
    return pl.pallas_call(
        last_step_kernel,
        out_shape=(TILE, STASH),
        in_specs=[SMEM_SPEC] + [VMEM_SPEC] * 5,
        out_specs=[VMEM_SPEC] * 2,
        scratch_shapes=[sems, sems],
        compiler_params=pltpu.CompilerParams(
            collective_id=1, has_side_effects=True, vmem_limit_bytes=16 << 20
        ),
        name="last_step",
    )(picks, parts, x_t, gain_col, g, weights)


def prepare_kernel(x_ref, fc_ref, w_ref, gain_ref, x_out, fc_out, normed_out, qkv_out, turned_w):
    walker = pl.program_id(0)

    @pl.when(walker == 0)
    def _():
        for t in range(3):
            turned_w[t] = turned(w_ref[t])

    x = x_ref[0].astype(F32)
    inv = lax.rsqrt(jnp.mean(x * x, axis=1, keepdims=True) + eps)
    normed = jnp.transpose(x * inv * gain_ref[...]).astype(BF16)
    x_out[0] = jnp.transpose(x).astype(BF16)
    fc = turned(fc_ref[0])
    fc_out[0] = fc
    normed_out[0] = normed

    @pl.when(walker < pl.num_programs(0) - 1)
    def _():
        query = mm(turned_w[0], normed).astype(BF16) * jnp.asarray(0.25, BF16)
        qkv_out[:, 0] = query.reshape(HEADS, DH, ROWS)
        for t in range(1, 3):
            qkv_out[:, t] = mm(turned_w[t], normed).astype(BF16).reshape(HEADS, DH, ROWS)

    @pl.when(walker == pl.num_programs(0) - 1)
    def _():
        first_g = turned(fc_ref[0])
        qkv_out[:, 0] = mm(w_ref[3], first_g).astype(BF16).reshape(HEADS, DH, ROWS)


def prepare(x, fc, weights, gain):
    walkers = x.shape[0]

    def own(w):
        return (lax.rem(w, walkers), 0, 0)

    def tile():
        return pl.BlockSpec((1, WIDTH, ROWS), own)

    flat = jax.ShapeDtypeStruct((walkers, WIDTH, ROWS), BF16)
    return pl.pallas_call(
        prepare_kernel,
        grid=(walkers + 1,),
        in_specs=[
            pl.BlockSpec((1, ROWS, WIDTH), own),
            pl.BlockSpec((1, ROWS, WIDTH), own),
            pl.BlockSpec((4, WIDTH, WIDTH), lambda w: (0, 0, 0)),
            pl.BlockSpec((1, WIDTH), lambda w: (0, 0)),
        ],
        out_specs=[
            tile(),
            tile(),
            tile(),
            pl.BlockSpec((HEADS, 3, DH, ROWS), lambda w: (0, w, 0, 0)),
        ],
        out_shape=(
            flat,
            flat,
            flat,
            jax.ShapeDtypeStruct((HEADS, 3 * walkers + 1, DH, ROWS), BF16),
        ),
        scratch_shapes=[pltpu.VMEM((3, WIDTH, WIDTH), BF16)],
        compiler_params=pltpu.CompilerParams(vmem_limit_bytes=48 << 20),
        name="prepare",
    )(x, fc, weights, gain)


def turned(tile):
    return jnp.transpose(tile.astype(F32)).astype(BF16)


def head_tiles(tile, k_nat, q_all, v_all):
    for b in range(BLKS):
        k_nat[b] = turned(tile(1, b))
        q_all[b] = tile(0, b)
        v_all[b] = tile(2, b)


def slots(n, list_ref):
    a = [2 * n + c // MAXN for c in range(2 * MAXN)]
    return [(a[c], c % MAXN, list_ref[a[c], c % MAXN]) for c in range(2 * MAXN)]


def row_sums(list_ref, count_ref, k_nat, q_all, lse_ref):
    def body(n, carry):
        some = slots(n, list_ref)
        scores = [mm(k_nat[j], q_all[a]) for a, _, j in some]
        parts = [jnp.sum(jnp.exp(s).reshape(ROWS // 8, 8, ROWS), axis=0) for s in scores]
        parts = [
            jnp.where(c < count_ref[a], part, 0.0) for part, (a, c, _) in zip(parts, some)
        ]
        for u in range(2):
            row = parts[u * MAXN]
            for part in parts[u * MAXN + 1 : (u + 1) * MAXN]:
                row = row + part
            lse_ref[2 * n + u] = jnp.log(jnp.sum(row, axis=0, keepdims=True))
        return carry

    lax.fori_loop(0, BLKS // 2, body, 0)


def attend_rows(list_ref, count_ref, k_nat, q_all, v_all, lse_ref, att_ref):
    def body(n, carry):
        some = slots(n, list_ref)
        scores = [mm(k_nat[j], q_all[a]) for a, _, j in some]
        shifts = [lse_ref[a] + jnp.where(c < count_ref[a], 0.0, 1e30) for a, c, _ in some]
        probs = [jnp.exp(s - shift).astype(BF16) for s, shift in zip(scores, shifts)]
        parts = [mm(v_all[j], p) for p, (_, _, j) in zip(probs, some)]
        for u in range(2):
            row = parts[u * MAXN]
            for part in parts[u * MAXN + 1 : (u + 1) * MAXN]:
                row = row + part
            att_ref[2 * n + u] = row.astype(BF16)
        return carry

    lax.fori_loop(0, BLKS // 2, body, 0)


def forward_kernel(list_ref, count_ref, qkv_ref, att_ref, lse_ref, info_ref, k_nat, q_all, v_all):
    def note(n, place):
        c, a = n // BLKS, lax.rem(n, BLKS)
        info_ref[place] = a
        info_ref[PAIRS + place] = list_ref[a, c]
        return place + jnp.where(c < count_ref[a], 1, 0)

    used = lax.fori_loop(0, BLKS * MAXN, note, 0)
    for k in range(GROUP):
        info_ref[used + k] = DUMMY
        info_ref[PAIRS + used + k] = 0
    info_ref[2 * PAIRS] = (used + GROUP - 1) // GROUP
    head_tiles(lambda t, b: qkv_ref[b, t], k_nat, q_all, v_all)
    row_sums(list_ref, count_ref, k_nat, q_all, lse_ref)
    attend_rows(list_ref, count_ref, k_nat, q_all, v_all, lse_ref, att_ref)


def forward(pair_list, pair_count, qkv):
    return pl.pallas_call(
        forward_kernel,
        grid=(1,),
        in_specs=[
            SMEM_SPEC,
            SMEM_SPEC,
            pl.BlockSpec((BLKS, 3, DH, ROWS), lambda i: (0, 0, 0, 0)),
        ],
        out_specs=[
            pl.BlockSpec((BLKS, DH, ROWS), lambda i: (0, 0, 0)),
            pl.BlockSpec((BLKS, 1, ROWS), lambda i: (0, 0, 0)),
            SMEM_SPEC,
        ],
        out_shape=(ATTENDED, LOG_SUMS, jax.ShapeDtypeStruct((2 * PAIRS + 1,), jnp.int32)),
        scratch_shapes=HEAD_TILES,
        compiler_params=pltpu.CompilerParams(vmem_limit_bytes=24 << 20),
        name="forward",
    )(pair_list, pair_count, qkv)


def filing(slot, tiles, shelves, sems):
    return [
        pltpu.make_async_copy(tile, shelf.at[slot], sems.at[k])
        for k, (tile, shelf) in enumerate(zip(tiles, shelves))
    ]


def backward_kernel(mode, info_ref, picks_ref, qkv_ref, att_ref, lse_ref, dout_ref, *refs):
    tiles, refs = (refs[:3], refs[3:]) if mode else ((), refs)
    refs = refs[3:] if mode == 2 else refs
    out_ref, refs = refs[0], refs[1:]
    shelves, refs = (refs[:3], refs[3:]) if mode else ((), refs)
    kv_nat, q_dout, lse, delta, dq, dkv, sems = refs
    copies = filing(picks_ref[3], tiles, shelves, sems)
    for c in copies:
        c.start()
    base = 3 * picks_ref[0]
    nothing = jnp.zeros((DH, ROWS), BF16)
    for b in range(BLKS):
        kv_nat[b] = turned(jnp.concatenate([qkv_ref[b, base + 1], qkv_ref[b, base + 2]], axis=0))
        q_dout[b, 0:DH, 0:ROWS] = qkv_ref[b, base]
        q_dout[b, 0:DH, ROWS : 2 * ROWS] = nothing
        q_dout[b, DH : 2 * DH, 0:ROWS] = nothing
        q_dout[b, DH : 2 * DH, ROWS : 2 * ROWS] = dout_ref[b]
        lse[b] = lse_ref[b]
        delta[b] = jnp.sum(
            dout_ref[b].astype(F32) * att_ref[b].astype(F32), axis=0, keepdims=True
        )
    q_dout[DUMMY] = jnp.zeros((2 * DH, 2 * ROWS), BF16)
    lse[DUMMY] = jnp.full((1, ROWS), 1e30, F32)
    delta[DUMMY] = jnp.zeros((1, ROWS), F32)
    dq[...] = jnp.zeros_like(dq)
    dkv[...] = jnp.zeros_like(dkv)

    def body(n, carry):
        pairs = [(info_ref[n * GROUP + u], info_ref[PAIRS + n * GROUP + u]) for u in range(GROUP)]
        sides = [q_dout[a] for a, _ in pairs]
        boths = [mm(kv_nat[j], side) for (_, j), side in zip(pairs, sides)]
        probs = [jnp.exp(both[:, 0:ROWS] - lse[a]) for both, (a, _) in zip(boths, pairs)]
        score_grads = [
            (prob * (both[:, ROWS : 2 * ROWS] - delta[a])).astype(BF16)
            for prob, both, (a, _) in zip(probs, boths, pairs)
        ]
        kv_parts = [
            mm_nt(side, jnp.concatenate([score_grad, prob.astype(BF16)], axis=1))
            for side, score_grad, prob in zip(sides, score_grads, probs)
        ]
        q_parts = [
            mm(qkv_ref[j, base + 1], score_grad)
            for (_, j), score_grad in zip(pairs, score_grads)
        ]
        for (a, j), kv_part, q_part in zip(pairs, kv_parts, q_parts):
            dkv[j] += kv_part
            dq[a] += q_part
        return carry

    lax.fori_loop(0, info_ref[2 * PAIRS], body, 0)
    for b in range(BLKS):
        out_ref[b, 0] = (dq[b] * 0.25).astype(BF16)
        out_ref[b, 1] = dkv[b, 0:DH].astype(BF16)
        out_ref[b, 2] = dkv[b, DH : 2 * DH].astype(BF16)
        out_ref[b, 3] = att_ref[b]
    for c in copies:
        c.wait()


SHELF_SPEC = pl.BlockSpec(memory_space=pl.ANY)


def shelf_shapes(walkers):
    return tuple(
        jax.ShapeDtypeStruct((walkers + 1,) + t.shape, t.dtype) for t in (TILE, TILE, STASH)
    )


def backward(info, picks, qkv, att, lse, dout, walkers, tiles=None, shelves=None):
    mode = 0 if tiles is None else 1 if shelves is None else 2
    outs = shelf_shapes(walkers) if mode else ()
    result = pl.pallas_call(
        partial(backward_kernel, mode),
        in_specs=[SMEM_SPEC] * 2
        + [VMEM_SPEC] * (7 if mode else 4)
        + [SHELF_SPEC] * (3 if mode == 2 else 0),
        out_specs=(VMEM_SPEC,) + (SHELF_SPEC,) * len(outs),
        out_shape=(STASH,) + outs,
        input_output_aliases={9: 1, 10: 2, 11: 3} if mode == 2 else {},
        scratch_shapes=[
            pltpu.VMEM((BLKS, ROWS, 2 * DH), BF16),
            pltpu.VMEM((BLKS + 1, 2 * DH, 2 * ROWS), BF16),
            pltpu.VMEM((BLKS + 1, 1, ROWS), F32),
            pltpu.VMEM((BLKS + 1, 1, ROWS), F32),
            pltpu.VMEM((BLKS + 1, DH, ROWS), F32),
            pltpu.VMEM((BLKS, 2 * DH, ROWS), F32),
            pltpu.SemaphoreType.DMA((3,)),
        ],
        compiler_params=pltpu.CompilerParams(vmem_limit_bytes=16 << 20),
        name="backward",
    )(info, picks, qkv, att, lse, dout, *(tiles or ()), *(shelves or ()))
    return result[0], result[1:]


def file_kernel(picks_ref, *refs):
    copies = filing(picks_ref[4], refs[:3], refs[6:9], refs[9])
    for c in copies:
        c.start()
    for c in copies:
        c.wait()


def file_last(picks, tiles, shelves, walkers):
    return pl.pallas_call(
        file_kernel,
        in_specs=[SMEM_SPEC] + [VMEM_SPEC] * 3 + [SHELF_SPEC] * 3,
        out_specs=(SHELF_SPEC,) * 3,
        out_shape=shelf_shapes(walkers),
        input_output_aliases={4: 0, 5: 1, 6: 2},
        scratch_shapes=[pltpu.SemaphoreType.DMA((3,))],
        name="file_last",
    )(picks, *tiles, *shelves)


def per_device(layer_inputs, final_cot, attn_weights, norm_gain, pair_list, pair_count):
    seg = lax.axis_index("segment")
    walkers = layer_inputs.shape[1]
    weights = attn_weights[0]
    gain_col = norm_gain[0][:, None]
    x_t, fc_t, normed, qkv = prepare(layer_inputs[0], final_cot, weights, norm_gain)
    qkv, w_below = swap(qkv, weights[3])
    dout = qkv[:, 3 * walkers]
    g = fc_t[0]
    att, lse, info = forward(pair_list, pair_count, qkv)

    ticks = walkers + SEGS - 1
    tiles = shelves = None
    for tick in range(ticks):
        first = tick - (SEGS - 1 - seg)
        picks = jnp.stack([first, jnp.int32(tick + 1), first + 1, first - 1, first])
        most = jnp.array([walkers - 1] * 3 + [walkers] * 2, jnp.int32)
        picks = jnp.minimum(jnp.maximum(picks, 0), most).astype(jnp.int32)
        parts, shelves = backward(info, picks, qkv, att, lse, dout, walkers, tiles, shelves or None)
        if tick < ticks - 1:
            cot, stash, gnext, dout, att, lse = step(
                picks, pair_list, pair_count, parts, x_t, gain_col, g, fc_t, weights, w_below, qkv
            )
        else:
            cot, stash = last_step(picks, parts, x_t, gain_col, g, weights)
        tiles = (cot, g, stash)
        g = gnext
    cot_all, g_all, stash_all = (
        shelf[:walkers] for shelf in file_last(picks, tiles, shelves, walkers)
    )
    grads = jnp.swapaxes(stash_all, 1, 2).reshape(walkers, 4, WIDTH, ROWS)
    dw = jnp.einsum("wfi,wtci->tfc", normed, grads[:, :3], preferred_element_type=F32)
    dwo = jnp.einsum("wci,wfi->cf", grads[:, 3], g_all, preferred_element_type=F32)
    normed_grad = jnp.einsum("tfc,wtci->wfi", weights[:3], grads[:, :3], preferred_element_type=F32)
    feats = x_t.astype(F32)
    unit = feats * lax.rsqrt(jnp.mean(feats * feats, axis=1, keepdims=True) + eps)
    gain_part = jnp.sum(normed_grad * unit, axis=(0, 2))

    own = jnp.concatenate([dw, dwo[None]], axis=0).reshape(BLKS, 4 * WIDTH // BLKS, WIDTH)
    gains = jnp.pad(gain_part.reshape(2, ROWS), ((0, 6), (0, 0)))
    summed, gain_sum = total(own.astype(BF16), gains, 3)
    grad_total = summed.reshape(4, WIDTH, WIDTH).astype(F32)
    gain_total = gain_sum[:2].reshape(WIDTH)
    return (jnp.swapaxes(cot_all, 1, 2)[None], grad_total[None], gain_total[None])


def solution(mesh):
    return jax.shard_map(
        per_device,
        mesh=mesh,
        in_specs=(
            P("segment", None, "blk", None),
            P(None, "blk", None),
            P("segment", None, None, None),
            P("segment", None),
            P(),
            P(),
        ),
        out_specs=(
            P("segment", None, "blk", None),
            P("segment", None, None, None),
            P("segment", None),
        ),
        check_vma=False,
    )
```

```python
from functools import partial

import jax
import jax.numpy as jnp
from jax import lax
from jax.experimental import pallas as pl
from jax.experimental.pallas import tpu as pltpu
from jax.sharding import PartitionSpec as P

HEADS = 16
DH = 16
BLKS = 16
SEGS = 8
ROWS = 128
WIDTH = 256
GROUP = 16
MAXN = 8
PAIRS = BLKS * MAXN + GROUP
DUMMY = BLKS
eps = 1e-05
F32, BF16 = jnp.float32, jnp.bfloat16
VMEM_SPEC = pl.BlockSpec(memory_space=pltpu.VMEM)
SMEM_SPEC = pl.BlockSpec(memory_space=pltpu.SMEM)


def mm(a, b):
    return jnp.dot(a, b, preferred_element_type=F32)


def mm_nt(a, b):
    return lax.dot_general(a, b, (((1,), (1,)), ((), ())), preferred_element_type=F32)


SIDE = 4
SHIFTS = sorted(
    [(dx, dy) for dx in range(SIDE) for dy in range(SIDE)],
    key=lambda s: -min(s[0], SIDE - s[0]) - min(s[1], SIDE - s[1]),
)


def blocks_from(me):
    x, y = me // SIDE, lax.rem(me, SIDE)
    return [lax.rem(x + dx, SIDE) * SIDE + lax.rem(y + dy, SIDE) for dx, dy in SHIFTS]


def peers(me):
    return blocks_from(me)[: BLKS - 1]


def signal(semaphore, where):
    pl.semaphore_signal(semaphore, inc=1, device_id=where, device_id_type=pl.DeviceIdType.MESH)


def greet(me, more=()):
    barrier = pltpu.get_barrier_semaphore()
    for peer in peers(me):
        signal(barrier, {"blk": peer})
    for seg in more:
        signal(barrier, {"segment": seg})


def all_in(more=()):
    pl.semaphore_wait(pltpu.get_barrier_semaphore(), BLKS - 1 + len(more))


def copy_to(src, dst, send, recv, where):
    return pltpu.make_async_remote_copy(
        src_ref=src,
        dst_ref=dst,
        send_sem=send,
        recv_sem=recv,
        device_id=where,
        device_id_type=pl.DeviceIdType.MESH,
    )


def swap_kernel(in_ref, w_ref, out_ref, below_ref, send, recv, w_send, w_recv):
    me = lax.axis_index("blk")
    seg = lax.axis_index("segment")
    above, below = lax.rem(seg + 1, SEGS), lax.rem(seg + SEGS - 1, SEGS)
    greet(me, (below,))
    all_in((above,))
    copies = [
        copy_to(in_ref.at[peer], out_ref.at[me], send.at[k], recv.at[k], {"blk": peer})
        for k, peer in enumerate(peers(me))
    ]
    copies.append(copy_to(w_ref, below_ref, w_send, w_recv, {"segment": above}))
    for c in copies:
        c.start()
    out_ref[me] = in_ref[me]
    for c in copies:
        c.wait()


def swap(values, w_out):
    sems = pltpu.SemaphoreType.DMA((BLKS - 1,))
    return pl.pallas_call(
        swap_kernel,
        out_shape=(
            jax.ShapeDtypeStruct(values.shape, values.dtype),
            jax.ShapeDtypeStruct(w_out.shape, w_out.dtype),
        ),
        in_specs=[VMEM_SPEC] * 2,
        out_specs=[VMEM_SPEC] * 2,
        scratch_shapes=[sems, sems, pltpu.SemaphoreType.DMA, pltpu.SemaphoreType.DMA],
        compiler_params=pltpu.CompilerParams(
            collective_id=0, has_side_effects=True, vmem_limit_bytes=52 << 20
        ),
        name="swap",
    )(values, w_out)


def close_kernel(
    normed_ref, x_ref, w_ref, cot_last, g_last, stash_last, cot_shelf, g_shelf, stash_shelf,
    cots_ref, out_ref, gain_out,
    cot_ref, g_ref, stash_ref, shelf_sems, mine, parts, got, own, gain_own, got_gain, send1, recv1, send2, recv2, send3, recv3,
):
    me = lax.axis_index("blk")
    seg = lax.axis_index("segment")
    walkers = normed_ref.shape[0]
    shelves = [
        pltpu.make_async_copy(shelf.at[pl.ds(0, walkers)], ref, shelf_sems.at[k])
        for k, (shelf, ref) in enumerate(
            [(cot_shelf, cot_ref), (g_shelf, g_ref), (stash_shelf, stash_ref)]
        )
    ]
    for c in shelves:
        c.start()
    greet(me)
    for c in shelves:
        c.wait()

    def newest(last_ref, shelf_ref):
        old = shelf_ref[walkers - 1].astype(F32)
        return jnp.where(seg == 0, last_ref[...].astype(F32), old).astype(BF16)

    mine[...] = newest(stash_last, stash_ref)
    g_new = newest(g_last, g_ref)

    def grads(w, t):
        tile = mine[:, t] if w == walkers - 1 else stash_ref[w, :, t]
        return tile.reshape(WIDTH, ROWS)

    for t in range(4):
        product = jnp.zeros((WIDTH, WIDTH), F32)
        for w in range(walkers):
            if t < 3:
                product += mm_nt(normed_ref[w], grads(w, t))
            else:
                product += mm_nt(grads(w, 3), g_new if w == walkers - 1 else g_ref[w])
        rows = WIDTH * 4 // BLKS
        parts[4 * t : 4 * t + 4] = product.astype(BF16).reshape(4, rows, WIDTH)
    gain = jnp.zeros((WIDTH, ROWS), F32)
    for w in range(walkers):
        x = x_ref[w].astype(F32)
        unit = x * lax.rsqrt(jnp.mean(x * x, axis=0, keepdims=True) + eps)
        normed_grad = mm(w_ref[0], grads(w, 0)) + mm(w_ref[1], grads(w, 1)) + mm(w_ref[2], grads(w, 2))
        gain += normed_grad * unit
    row = jnp.sum(jnp.transpose(gain), axis=0, keepdims=True)
    gain_own[...] = jnp.broadcast_to(row, gain_own.shape)

    all_in()
    first = [
        copy_to(parts.at[peer], got.at[me], send1.at[k], recv1.at[k], {"blk": peer})
        for k, peer in enumerate(peers(me))
    ]
    gains = [
        copy_to(gain_own, got_gain.at[me], send3.at[k], recv3.at[k], {"blk": peer})
        for k, peer in enumerate(peers(me))
    ]
    for c in first:
        c.start()
    for c in gains:
        c.start()
    got[me] = parts[me]
    got_gain[me] = gain_own[...]
    for w in range(walkers - 1):
        cots_ref[w] = turned(cot_ref[w])
    cots_ref[walkers - 1] = turned(newest(cot_last, cot_ref))
    for c in first:
        c.wait_recv()
    acc = got[0].astype(F32)
    for b in range(1, BLKS):
        acc = acc + got[b].astype(F32)
    own[...] = acc.astype(BF16)
    second = [
        copy_to(own, out_ref.at[me], send2.at[k], recv2.at[k], {"blk": peer})
        for k, peer in enumerate(peers(me))
    ]
    for c in second:
        c.start()
    out_ref[me] = own[...]
    for c in gains:
        c.wait()
    gain_out[...] = jnp.sum(got_gain[...], axis=0)
    for c in first:
        c.wait_send()
    for c in second:
        c.wait()


def close(normed, x_t, weights, tiles, shelves):
    sems = pltpu.SemaphoreType.DMA((BLKS - 1,))
    walkers = normed.shape[0]
    chunks = (BLKS, 4 * WIDTH // BLKS, WIDTH)
    return pl.pallas_call(
        close_kernel,
        out_shape=(
            jax.ShapeDtypeStruct((walkers, ROWS, WIDTH), BF16),
            jax.ShapeDtypeStruct(chunks, BF16),
            jax.ShapeDtypeStruct((8, WIDTH), F32),
        ),
        in_specs=[VMEM_SPEC] * 6 + [SHELF_SPEC] * 3,
        out_specs=[VMEM_SPEC] * 3,
        scratch_shapes=[
            *[pltpu.VMEM((walkers,) + t.shape, BF16) for t in (TILE, TILE, STASH)],
            pltpu.SemaphoreType.DMA((3,)),
            pltpu.VMEM((HEADS, 4, DH, ROWS), BF16),
            pltpu.VMEM(chunks, BF16),
            pltpu.VMEM(chunks, BF16),
            pltpu.VMEM(chunks[1:], BF16),
            pltpu.VMEM((8, WIDTH), F32),
            pltpu.VMEM((BLKS, 8, WIDTH), F32),
        ]
        + [sems] * 6,
        compiler_params=pltpu.CompilerParams(
            collective_id=3, has_side_effects=True, vmem_limit_bytes=52 << 20
        ),
        name="close",
    )(normed, x_t, weights, *tiles, *shelves)


def local_grads(walker_ref, x_ref, gain_ref, g_ref, w_ref):
    x = x_ref[walker_ref[0]].astype(F32)
    inv = lax.rsqrt(jnp.mean(x * x, axis=0, keepdims=True) + eps)
    unit = x * inv
    g = g_ref[...].astype(F32)

    def finish(stash_ref):
        normed_grad = mm(w_ref[0], stash_ref[:, 0].reshape(WIDTH, ROWS))
        for t in range(1, 3):
            normed_grad += mm(w_ref[t], stash_ref[:, t].reshape(WIDTH, ROWS))
        unit_grad = normed_grad * gain_ref[...]
        centre = jnp.mean(unit_grad * unit, axis=0, keepdims=True)
        return (g + inv * (unit_grad - unit * centre)).astype(BF16)

    return finish


def send_parts(me, parts_ref, stash_ref, send, recv):
    copies = [
        copy_to(parts_ref.at[peer], stash_ref.at[me], send.at[k], recv.at[k], {"blk": peer})
        for k, peer in enumerate(peers(me))
    ]
    for c in copies:
        c.start()
    stash_ref[me] = parts_ref[me]
    return copies


def step_kernel(
    walker_ref, list_ref, count_ref, parts_ref, x_ref, gain_ref, g_ref, fc_ref, w_ref, w_below_ref, qkv_ref,
    cot_ref, stash_ref, gnext_ref, dout_ref, att_ref, lse_ref,
    k_nat, q_all, v_all, g_own, dout_own, ready, send1, recv1, hop_send, hop_recv, send2, recv2,
):
    me = lax.axis_index("blk")
    seg = lax.axis_index("segment")
    above, below = lax.rem(seg + 1, SEGS), lax.rem(seg + SEGS - 1, SEGS)
    near = (above, below)
    greet(me, near)
    grads = local_grads(walker_ref, x_ref, gain_ref, g_ref, w_ref)
    head_tiles(lambda t, b: qkv_ref[b, 3 * walker_ref[2] + t], k_nat, q_all, v_all)
    all_in(near)
    first = send_parts(me, parts_ref, stash_ref, send1, recv1)
    row_sums(list_ref, count_ref, k_nat, q_all, lse_ref)
    for c in first:
        c.wait_recv()
    signal(ready, {"segment": above})
    cot = grads(stash_ref)
    cot_ref[...] = cot
    last_g = fc_ref[walker_ref[1]].astype(F32)
    g_below = jnp.where(seg == 0, last_g, cot.astype(F32)).astype(BF16)
    g_own[...] = g_below
    dout_own[...] = mm(w_below_ref[...], g_below).astype(BF16).reshape(HEADS, DH, ROWS)
    pl.semaphore_wait(ready, 1)
    second = [
        copy_to(
            dout_own.at[peer], dout_ref.at[me], send2.at[k], recv2.at[k],
            {"segment": below, "blk": peer},
        )
        for k, peer in enumerate(blocks_from(me))
    ]
    second.append(copy_to(g_own, gnext_ref, hop_send, hop_recv, {"segment": below}))
    for c in second:
        c.start()
    attend_rows(list_ref, count_ref, k_nat, q_all, v_all, lse_ref, att_ref)
    for c in second:
        c.wait()
    for c in first:
        c.wait_send()


def last_step_kernel(
    walker_ref, parts_ref, x_ref, gain_ref, g_ref, w_ref, cot_ref, stash_ref, send1, recv1
):
    me = lax.axis_index("blk")
    greet(me)
    grads = local_grads(walker_ref, x_ref, gain_ref, g_ref, w_ref)
    all_in()
    first = send_parts(me, parts_ref, stash_ref, send1, recv1)
    for c in first:
        c.wait()
    cot_ref[...] = grads(stash_ref)


TILE = jax.ShapeDtypeStruct((WIDTH, ROWS), BF16)
STASH = jax.ShapeDtypeStruct((HEADS, 4, DH, ROWS), BF16)
ATTENDED = jax.ShapeDtypeStruct((BLKS, DH, ROWS), BF16)
LOG_SUMS = jax.ShapeDtypeStruct((BLKS, 1, ROWS), F32)
HEAD_TILES = [
    pltpu.VMEM((BLKS, ROWS, DH), BF16),
    pltpu.VMEM((BLKS, DH, ROWS), BF16),
    pltpu.VMEM((BLKS, DH, ROWS), BF16),
]


def step(picks, pair_list, pair_count, parts, x_t, gain_col, g, fc_t, weights, w_below, qkv):
    sems = pltpu.SemaphoreType.DMA((BLKS - 1,))
    more = pltpu.SemaphoreType.DMA((BLKS,))
    return pl.pallas_call(
        step_kernel,
        out_shape=(TILE, STASH, TILE, ATTENDED, ATTENDED, LOG_SUMS),
        in_specs=[SMEM_SPEC] * 3 + [VMEM_SPEC] * 8,
        out_specs=[VMEM_SPEC] * 6,
        scratch_shapes=HEAD_TILES
        + [
            pltpu.VMEM((WIDTH, ROWS), BF16),
            pltpu.VMEM((HEADS, DH, ROWS), BF16),
            pltpu.SemaphoreType.REGULAR,
            sems,
            sems,
            pltpu.SemaphoreType.DMA,
            pltpu.SemaphoreType.DMA,
            more,
            more,
        ],
        compiler_params=pltpu.CompilerParams(
            collective_id=2, has_side_effects=True, vmem_limit_bytes=52 << 20
        ),
        name="step",
    )(picks, pair_list, pair_count, parts, x_t, gain_col, g, fc_t, weights, w_below, qkv)


def last_step(picks, parts, x_t, gain_col, g, weights):
    sems = pltpu.SemaphoreType.DMA((BLKS - 1,))
    return pl.pallas_call(
        last_step_kernel,
        out_shape=(TILE, STASH),
        in_specs=[SMEM_SPEC] + [VMEM_SPEC] * 5,
        out_specs=[VMEM_SPEC] * 2,
        scratch_shapes=[sems, sems],
        compiler_params=pltpu.CompilerParams(
            collective_id=1, has_side_effects=True, vmem_limit_bytes=52 << 20
        ),
        name="last_step",
    )(picks, parts, x_t, gain_col, g, weights)


def prepare_kernel(
    list_ref, count_ref, x_ref, fc_ref, w_ref, gain_ref,
    x_out, fc_out, normed_out, qkv_out, info_ref, turned_w,
):
    walker = pl.program_id(0)

    def note(n, place):
        c, a = n // BLKS, lax.rem(n, BLKS)
        info_ref[place] = a
        info_ref[PAIRS + place] = list_ref[a, c]
        return place + jnp.where(c < count_ref[a], 1, 0)

    @pl.when(walker == 0)
    def _():
        used = lax.fori_loop(0, BLKS * MAXN, note, 0)
        for k in range(GROUP):
            info_ref[used + k] = DUMMY
            info_ref[PAIRS + used + k] = 0
        info_ref[2 * PAIRS] = (used + GROUP - 1) // GROUP

    @pl.when(walker == 0)
    def _():
        for t in range(3):
            turned_w[t] = turned(w_ref[t])

    x = x_ref[0].astype(F32)
    inv = lax.rsqrt(jnp.mean(x * x, axis=1, keepdims=True) + eps)
    normed = jnp.transpose(x * inv * gain_ref[...]).astype(BF16)
    x_out[0] = jnp.transpose(x).astype(BF16)
    fc = turned(fc_ref[0])
    fc_out[0] = fc
    normed_out[0] = normed

    @pl.when(walker < pl.num_programs(0) - 1)
    def _():
        query = mm(turned_w[0], normed).astype(BF16) * jnp.asarray(0.25, BF16)
        qkv_out[:, 0] = query.reshape(HEADS, DH, ROWS)
        for t in range(1, 3):
            qkv_out[:, t] = mm(turned_w[t], normed).astype(BF16).reshape(HEADS, DH, ROWS)

    @pl.when(walker == pl.num_programs(0) - 1)
    def _():
        first_g = turned(fc_ref[0])
        qkv_out[:, 0] = mm(w_ref[3], first_g).astype(BF16).reshape(HEADS, DH, ROWS)


def prepare(x, fc, weights, gain, pair_list, pair_count):
    walkers = x.shape[0]

    def own(w):
        return (lax.rem(w, walkers), 0, 0)

    def tile():
        return pl.BlockSpec((1, WIDTH, ROWS), own)

    flat = jax.ShapeDtypeStruct((walkers, WIDTH, ROWS), BF16)
    return pl.pallas_call(
        prepare_kernel,
        grid=(walkers + 1,),
        in_specs=[
            SMEM_SPEC,
            SMEM_SPEC,
            pl.BlockSpec((1, ROWS, WIDTH), own),
            pl.BlockSpec((1, ROWS, WIDTH), own),
            pl.BlockSpec((4, WIDTH, WIDTH), lambda w: (0, 0, 0)),
            pl.BlockSpec((1, WIDTH), lambda w: (0, 0)),
        ],
        out_specs=[
            tile(),
            tile(),
            tile(),
            pl.BlockSpec((HEADS, 3, DH, ROWS), lambda w: (0, w, 0, 0)),
            SMEM_SPEC,
        ],
        out_shape=(
            flat,
            flat,
            flat,
            jax.ShapeDtypeStruct((HEADS, 3 * walkers + 1, DH, ROWS), BF16),
            jax.ShapeDtypeStruct((2 * PAIRS + 1,), jnp.int32),
        ),
        scratch_shapes=[pltpu.VMEM((3, WIDTH, WIDTH), BF16)],
        compiler_params=pltpu.CompilerParams(vmem_limit_bytes=52 << 20),
        name="prepare",
    )(pair_list, pair_count, x, fc, weights, gain)


def turned(tile):
    return jnp.transpose(tile.astype(F32)).astype(BF16)


def head_tiles(tile, k_nat, q_all, v_all):
    for b in range(BLKS):
        k_nat[b] = turned(tile(1, b))
        q_all[b] = tile(0, b)
        v_all[b] = tile(2, b)


def slots(n, list_ref):
    a = [2 * n + c // MAXN for c in range(2 * MAXN)]
    return [(a[c], c % MAXN, list_ref[a[c], c % MAXN]) for c in range(2 * MAXN)]


def row_sums(list_ref, count_ref, k_nat, q_all, lse_ref):
    def body(n, carry):
        some = slots(n, list_ref)
        scores = [mm(k_nat[j], q_all[a]) for a, _, j in some]
        parts = [jnp.sum(jnp.exp(s).reshape(ROWS // 8, 8, ROWS), axis=0) for s in scores]
        parts = [
            jnp.where(c < count_ref[a], part, 0.0) for part, (a, c, _) in zip(parts, some)
        ]
        for u in range(2):
            row = parts[u * MAXN]
            for part in parts[u * MAXN + 1 : (u + 1) * MAXN]:
                row = row + part
            lse_ref[2 * n + u] = jnp.log(jnp.sum(row, axis=0, keepdims=True))
        return carry

    lax.fori_loop(0, BLKS // 2, body, 0)


def attend_rows(list_ref, count_ref, k_nat, q_all, v_all, lse_ref, att_ref):
    def body(n, carry):
        some = slots(n, list_ref)
        scores = [mm(k_nat[j], q_all[a]) for a, _, j in some]
        shifts = [lse_ref[a] + jnp.where(c < count_ref[a], 0.0, 1e30) for a, c, _ in some]
        probs = [jnp.exp(s - shift).astype(BF16) for s, shift in zip(scores, shifts)]
        parts = [mm(v_all[j], p) for p, (_, _, j) in zip(probs, some)]
        for u in range(2):
            row = parts[u * MAXN]
            for part in parts[u * MAXN + 1 : (u + 1) * MAXN]:
                row = row + part
            att_ref[2 * n + u] = row.astype(BF16)
        return carry

    lax.fori_loop(0, BLKS // 2, body, 0)


def forward_kernel(info_ref, qkv_ref, att_ref, lse_ref, k_nat, q_all, v_all, sums, lse, att):
    head_tiles(lambda t, b: qkv_ref[b, t], k_nat, q_all, v_all)
    q_all[DUMMY] = jnp.zeros((DH, ROWS), BF16)
    sums[...] = jnp.zeros_like(sums)
    att[...] = jnp.zeros_like(att)
    groups = info_ref[2 * PAIRS]

    def group(n):
        return [(info_ref[n * GROUP + u], info_ref[PAIRS + n * GROUP + u]) for u in range(GROUP)]

    def add_up(n, carry):
        pairs = group(n)
        scores = [mm(k_nat[j], q_all[a]) for a, j in pairs]
        parts = [jnp.sum(jnp.exp(s).reshape(ROWS // 8, 8, ROWS), axis=0) for s in scores]
        for (a, _), part in zip(pairs, parts):
            sums[a] += part
        return carry

    lax.fori_loop(0, groups, add_up, 0)
    for b in range(BLKS):
        lse[b] = jnp.log(jnp.sum(sums[b], axis=0, keepdims=True))
        lse_ref[b] = lse[b]
    lse[DUMMY] = jnp.full((1, ROWS), 1e30, F32)

    def attend(n, carry):
        pairs = group(n)
        scores = [mm(k_nat[j], q_all[a]) for a, j in pairs]
        probs = [jnp.exp(s - lse[a]).astype(BF16) for s, (a, _) in zip(scores, pairs)]
        parts = [mm(v_all[j], p) for p, (_, j) in zip(probs, pairs)]
        for (a, _), part in zip(pairs, parts):
            att[a] += part
        return carry

    lax.fori_loop(0, groups, attend, 0)
    for b in range(BLKS):
        att_ref[b] = att[b].astype(BF16)


def forward(info, qkv):
    return pl.pallas_call(
        forward_kernel,
        in_specs=[SMEM_SPEC, VMEM_SPEC],
        out_specs=[VMEM_SPEC] * 2,
        out_shape=(ATTENDED, LOG_SUMS),
        scratch_shapes=[
            pltpu.VMEM((BLKS, ROWS, DH), BF16),
            pltpu.VMEM((BLKS + 1, DH, ROWS), BF16),
            pltpu.VMEM((BLKS, DH, ROWS), BF16),
            pltpu.VMEM((BLKS + 1, 8, ROWS), F32),
            pltpu.VMEM((BLKS + 1, 1, ROWS), F32),
            pltpu.VMEM((BLKS + 1, DH, ROWS), F32),
        ],
        compiler_params=pltpu.CompilerParams(vmem_limit_bytes=52 << 20),
        name="forward",
    )(info, qkv)


def filing(slot, tiles, shelves, sems):
    return [
        pltpu.make_async_copy(tile, shelf.at[slot], sems.at[k])
        for k, (tile, shelf) in enumerate(zip(tiles, shelves))
    ]


def backward_kernel(mode, info_ref, picks_ref, qkv_ref, att_ref, lse_ref, dout_ref, *refs):
    tiles, refs = (refs[:3], refs[3:]) if mode else ((), refs)
    refs = refs[3:] if mode == 2 else refs
    out_ref, refs = refs[0], refs[1:]
    shelves, refs = (refs[:3], refs[3:]) if mode else ((), refs)
    kv_nat, q_dout, lse, delta, dq, dkv, sems = refs
    copies = filing(picks_ref[3], tiles, shelves, sems)
    for c in copies:
        c.start()
    base = 3 * picks_ref[0]
    nothing = jnp.zeros((DH, ROWS), BF16)
    for b in range(BLKS):
        kv_nat[b] = turned(jnp.concatenate([qkv_ref[b, base + 1], qkv_ref[b, base + 2]], axis=0))
        q_dout[b, 0:DH, 0:ROWS] = qkv_ref[b, base]
        q_dout[b, 0:DH, ROWS : 2 * ROWS] = nothing
        q_dout[b, DH : 2 * DH, 0:ROWS] = nothing
        q_dout[b, DH : 2 * DH, ROWS : 2 * ROWS] = dout_ref[b]
        lse[b] = lse_ref[b]
        delta[b] = jnp.sum(
            dout_ref[b].astype(F32) * att_ref[b].astype(F32), axis=0, keepdims=True
        )
    q_dout[DUMMY] = jnp.zeros((2 * DH, 2 * ROWS), BF16)
    lse[DUMMY] = jnp.full((1, ROWS), 1e30, F32)
    delta[DUMMY] = jnp.zeros((1, ROWS), F32)
    dq[...] = jnp.zeros_like(dq)
    dkv[...] = jnp.zeros_like(dkv)

    def body(n, carry):
        pairs = [(info_ref[n * GROUP + u], info_ref[PAIRS + n * GROUP + u]) for u in range(GROUP)]
        sides = [q_dout[a] for a, _ in pairs]
        boths = [mm(kv_nat[j], side) for (_, j), side in zip(pairs, sides)]
        probs = [jnp.exp(both[:, 0:ROWS] - lse[a]) for both, (a, _) in zip(boths, pairs)]
        score_grads = [
            (prob * (both[:, ROWS : 2 * ROWS] - delta[a])).astype(BF16)
            for prob, both, (a, _) in zip(probs, boths, pairs)
        ]
        kv_parts = [
            mm_nt(side, jnp.concatenate([score_grad, prob.astype(BF16)], axis=1))
            for side, score_grad, prob in zip(sides, score_grads, probs)
        ]
        q_parts = [
            mm(qkv_ref[j, base + 1], score_grad)
            for (_, j), score_grad in zip(pairs, score_grads)
        ]
        for (a, j), kv_part, q_part in zip(pairs, kv_parts, q_parts):
            dkv[j] += kv_part
            dq[a] += q_part
        return carry

    lax.fori_loop(0, info_ref[2 * PAIRS], body, 0)
    for b in range(BLKS):
        out_ref[b, 0] = (dq[b] * 0.25).astype(BF16)
        out_ref[b, 1] = dkv[b, 0:DH].astype(BF16)
        out_ref[b, 2] = dkv[b, DH : 2 * DH].astype(BF16)
        out_ref[b, 3] = att_ref[b]
    for c in copies:
        c.wait()


SHELF_SPEC = pl.BlockSpec(memory_space=pltpu.HBM)


def shelf_shapes(walkers):
    return tuple(
        jax.ShapeDtypeStruct((walkers + 1,) + t.shape, t.dtype) for t in (TILE, TILE, STASH)
    )


def backward(info, picks, qkv, att, lse, dout, walkers, tiles=None, shelves=None):
    mode = 0 if tiles is None else 1 if shelves is None else 2
    outs = shelf_shapes(walkers) if mode else ()
    result = pl.pallas_call(
        partial(backward_kernel, mode),
        in_specs=[SMEM_SPEC] * 2
        + [VMEM_SPEC] * (7 if mode else 4)
        + [SHELF_SPEC] * (3 if mode == 2 else 0),
        out_specs=(VMEM_SPEC,) + (SHELF_SPEC,) * len(outs),
        out_shape=(STASH,) + outs,
        input_output_aliases={9: 1, 10: 2, 11: 3} if mode == 2 else {},
        scratch_shapes=[
            pltpu.VMEM((BLKS, ROWS, 2 * DH), BF16),
            pltpu.VMEM((BLKS + 1, 2 * DH, 2 * ROWS), BF16),
            pltpu.VMEM((BLKS + 1, 1, ROWS), F32),
            pltpu.VMEM((BLKS + 1, 1, ROWS), F32),
            pltpu.VMEM((BLKS + 1, DH, ROWS), F32),
            pltpu.VMEM((BLKS, 2 * DH, ROWS), F32),
            pltpu.SemaphoreType.DMA((3,)),
        ],
        compiler_params=pltpu.CompilerParams(vmem_limit_bytes=52 << 20),
        name="backward",
    )(info, picks, qkv, att, lse, dout, *(tiles or ()), *(shelves or ()))
    return result[0], result[1:]


def per_device(layer_inputs, final_cot, attn_weights, norm_gain, pair_list, pair_count):
    seg = lax.axis_index("segment")
    walkers = layer_inputs.shape[1]
    weights = attn_weights[0]
    gain_col = norm_gain[0][:, None]
    x_t, fc_t, normed, qkv, info = prepare(
        layer_inputs[0], final_cot, weights, norm_gain, pair_list, pair_count
    )
    qkv, w_below = swap(qkv, weights[3])
    dout = qkv[:, 3 * walkers]
    g = fc_t[0]
    att, lse = forward(info, qkv)

    ticks = walkers + SEGS - 1
    tiles = shelves = None
    for tick in range(ticks):
        first = tick - (SEGS - 1 - seg)
        picks = jnp.stack([first, jnp.int32(tick + 1), first + 1, first - 1])
        most = jnp.array([walkers - 1] * 3 + [walkers], jnp.int32)
        picks = jnp.minimum(jnp.maximum(picks, 0), most).astype(jnp.int32)
        parts, shelves = backward(info, picks, qkv, att, lse, dout, walkers, tiles, shelves or None)
        if tick < ticks - 1:
            cot, stash, gnext, dout, att, lse = step(
                picks, pair_list, pair_count, parts, x_t, gain_col, g, fc_t, weights, w_below, qkv
            )
        else:
            cot, stash = last_step(picks, parts, x_t, gain_col, g, weights)
        tiles = (cot, g, stash)
        g = gnext
    cot_all, summed, gain_sum = close(normed, x_t, weights, tiles, shelves)
    grad_total = summed.reshape(4, WIDTH, WIDTH).astype(F32)
    return (cot_all[None], grad_total[None], gain_sum[:1])


def solution(mesh):
    return jax.shard_map(
        per_device,
        mesh=mesh,
        in_specs=(
            P("segment", None, "blk", None),
            P(None, "blk", None),
            P("segment", None, None, None),
            P("segment", None),
            P(),
            P(),
        ),
        out_specs=(
            P("segment", None, "blk", None),
            P("segment", None, None, None),
            P("segment", None),
        ),
        check_vma=False,
    )
```

```python
from functools import partial

import jax
import jax.numpy as jnp
from jax import lax
from jax.experimental import pallas as pl
from jax.experimental.pallas import tpu as pltpu
from jax.sharding import PartitionSpec as P

HEADS = 16
DH = 16
BLKS = 16
SEGS = 8
ROWS = 128
WIDTH = 256
GROUP = 16
MAXN = 8
PAIRS = BLKS * MAXN + GROUP
DUMMY = BLKS
eps = 1e-05
F32, BF16 = jnp.float32, jnp.bfloat16
VMEM_SPEC = pl.BlockSpec(memory_space=pltpu.VMEM)
SMEM_SPEC = pl.BlockSpec(memory_space=pltpu.SMEM)


def mm(a, b):
    return jnp.dot(a, b, preferred_element_type=F32)


def mm_nt(a, b):
    return lax.dot_general(a, b, (((1,), (1,)), ((), ())), preferred_element_type=F32)


SIDE = 4
SHIFTS = sorted(
    [(dx, dy) for dx in range(SIDE) for dy in range(SIDE)],
    key=lambda s: -min(s[0], SIDE - s[0]) - min(s[1], SIDE - s[1]),
)


def blocks_from(me):
    x, y = me // SIDE, lax.rem(me, SIDE)
    return [lax.rem(x + dx, SIDE) * SIDE + lax.rem(y + dy, SIDE) for dx, dy in SHIFTS]


def peers(me):
    return blocks_from(me)[: BLKS - 1]


def signal(semaphore, where):
    pl.semaphore_signal(semaphore, inc=1, device_id=where, device_id_type=pl.DeviceIdType.MESH)


def greet(me, more=()):
    barrier = pltpu.get_barrier_semaphore()
    for peer in peers(me):
        signal(barrier, {"blk": peer})
    for seg in more:
        signal(barrier, {"segment": seg})


def all_in(more=()):
    pl.semaphore_wait(pltpu.get_barrier_semaphore(), BLKS - 1 + len(more))


def copy_to(src, dst, send, recv, where):
    return pltpu.make_async_remote_copy(
        src_ref=src,
        dst_ref=dst,
        send_sem=send,
        recv_sem=recv,
        device_id=where,
        device_id_type=pl.DeviceIdType.MESH,
    )


def swap_kernel(in_ref, w_ref, out_ref, below_ref, send, recv, w_send, w_recv):
    me = lax.axis_index("blk")
    seg = lax.axis_index("segment")
    above, below = lax.rem(seg + 1, SEGS), lax.rem(seg + SEGS - 1, SEGS)
    greet(me, (below,))
    all_in((above,))
    copies = [
        copy_to(in_ref.at[peer], out_ref.at[me], send.at[k], recv.at[k], {"blk": peer})
        for k, peer in enumerate(peers(me))
    ]
    copies.append(copy_to(w_ref, below_ref, w_send, w_recv, {"segment": above}))
    for c in copies:
        c.start()
    out_ref[me] = in_ref[me]
    for c in copies:
        c.wait()


def swap(values, w_out):
    sems = pltpu.SemaphoreType.DMA((BLKS - 1,))
    return pl.pallas_call(
        swap_kernel,
        out_shape=(
            jax.ShapeDtypeStruct(values.shape, values.dtype),
            jax.ShapeDtypeStruct(w_out.shape, w_out.dtype),
        ),
        in_specs=[VMEM_SPEC] * 2,
        out_specs=[VMEM_SPEC] * 2,
        scratch_shapes=[sems, sems, pltpu.SemaphoreType.DMA, pltpu.SemaphoreType.DMA],
        compiler_params=pltpu.CompilerParams(
            collective_id=0, has_side_effects=True, vmem_limit_bytes=16 << 20
        ),
        name="swap",
    )(values, w_out)


def close_kernel(
    normed_ref, x_ref, w_ref, cot_last, g_last, stash_last, cot_ref, g_ref, stash_ref,
    cots_ref, out_ref, gain_out,
    mine, parts, got, own, gain_own, got_gain, send1, recv1, send2, recv2, send3, recv3,
):
    me = lax.axis_index("blk")
    seg = lax.axis_index("segment")
    walkers = normed_ref.shape[0]
    greet(me)

    def newest(last_ref, shelf_ref):
        old = shelf_ref[walkers - 1].astype(F32)
        return jnp.where(seg == 0, last_ref[...].astype(F32), old).astype(BF16)

    mine[...] = newest(stash_last, stash_ref)
    g_new = newest(g_last, g_ref)

    def grads(w, t):
        tile = mine[:, t] if w == walkers - 1 else stash_ref[w, :, t]
        return tile.reshape(WIDTH, ROWS)

    for t in range(4):
        product = jnp.zeros((WIDTH, WIDTH), F32)
        for w in range(walkers):
            if t < 3:
                product += mm_nt(normed_ref[w], grads(w, t))
            else:
                product += mm_nt(grads(w, 3), g_new if w == walkers - 1 else g_ref[w])
        rows = WIDTH * 4 // BLKS
        parts[4 * t : 4 * t + 4] = product.astype(BF16).reshape(4, rows, WIDTH)
    gain = jnp.zeros((WIDTH, ROWS), F32)
    for w in range(walkers):
        x = x_ref[w].astype(F32)
        unit = x * lax.rsqrt(jnp.mean(x * x, axis=0, keepdims=True) + eps)
        normed_grad = mm(w_ref[0], grads(w, 0)) + mm(w_ref[1], grads(w, 1)) + mm(w_ref[2], grads(w, 2))
        gain += normed_grad * unit
    row = jnp.sum(jnp.transpose(gain), axis=0, keepdims=True)
    gain_own[...] = jnp.broadcast_to(row, gain_own.shape)

    all_in()
    first = [
        copy_to(parts.at[peer], got.at[me], send1.at[k], recv1.at[k], {"blk": peer})
        for k, peer in enumerate(peers(me))
    ]
    gains = [
        copy_to(gain_own, got_gain.at[me], send3.at[k], recv3.at[k], {"blk": peer})
        for k, peer in enumerate(peers(me))
    ]
    for c in first:
        c.start()
    for c in gains:
        c.start()
    got[me] = parts[me]
    got_gain[me] = gain_own[...]
    for w in range(walkers - 1):
        cots_ref[w] = turned(cot_ref[w])
    cots_ref[walkers - 1] = turned(newest(cot_last, cot_ref))
    for c in first:
        c.wait_recv()
    acc = got[0].astype(F32)
    for b in range(1, BLKS):
        acc = acc + got[b].astype(F32)
    own[...] = acc.astype(BF16)
    second = [
        copy_to(own, out_ref.at[me], send2.at[k], recv2.at[k], {"blk": peer})
        for k, peer in enumerate(peers(me))
    ]
    for c in second:
        c.start()
    out_ref[me] = own[...]
    for c in gains:
        c.wait()
    gain_out[...] = jnp.sum(got_gain[...], axis=0)
    for c in first:
        c.wait_send()
    for c in second:
        c.wait()


def close(normed, x_t, weights, tiles, shelves):
    sems = pltpu.SemaphoreType.DMA((BLKS - 1,))
    walkers = normed.shape[0]
    chunks = (BLKS, 4 * WIDTH // BLKS, WIDTH)
    return pl.pallas_call(
        close_kernel,
        out_shape=(
            jax.ShapeDtypeStruct((walkers, ROWS, WIDTH), BF16),
            jax.ShapeDtypeStruct(chunks, BF16),
            jax.ShapeDtypeStruct((8, WIDTH), F32),
        ),
        in_specs=[VMEM_SPEC] * 9,
        out_specs=[VMEM_SPEC] * 3,
        scratch_shapes=[
            pltpu.VMEM((HEADS, 4, DH, ROWS), BF16),
            pltpu.VMEM(chunks, BF16),
            pltpu.VMEM(chunks, BF16),
            pltpu.VMEM(chunks[1:], BF16),
            pltpu.VMEM((8, WIDTH), F32),
            pltpu.VMEM((BLKS, 8, WIDTH), F32),
        ]
        + [sems] * 6,
        compiler_params=pltpu.CompilerParams(
            collective_id=3, has_side_effects=True, vmem_limit_bytes=24 << 20
        ),
        name="close",
    )(normed, x_t, weights, *tiles, *shelves)


def local_grads(walker_ref, x_ref, gain_ref, g_ref, w_ref):
    x = x_ref[walker_ref[0]].astype(F32)
    inv = lax.rsqrt(jnp.mean(x * x, axis=0, keepdims=True) + eps)
    unit = x * inv
    g = g_ref[...].astype(F32)

    def finish(stash_ref):
        normed_grad = mm(w_ref[0], stash_ref[:, 0].reshape(WIDTH, ROWS))
        for t in range(1, 3):
            normed_grad += mm(w_ref[t], stash_ref[:, t].reshape(WIDTH, ROWS))
        unit_grad = normed_grad * gain_ref[...]
        centre = jnp.mean(unit_grad * unit, axis=0, keepdims=True)
        return (g + inv * (unit_grad - unit * centre)).astype(BF16)

    return finish


def send_parts(me, parts_ref, stash_ref, send, recv):
    copies = [
        copy_to(parts_ref.at[peer], stash_ref.at[me], send.at[k], recv.at[k], {"blk": peer})
        for k, peer in enumerate(peers(me))
    ]
    for c in copies:
        c.start()
    stash_ref[me] = parts_ref[me]
    return copies


def step_kernel(
    walker_ref, list_ref, count_ref, parts_ref, x_ref, gain_ref, g_ref, fc_ref, w_ref, w_below_ref, qkv_ref,
    cot_ref, stash_ref, gnext_ref, dout_ref, att_ref, lse_ref,
    k_nat, q_all, v_all, g_own, dout_own, ready, send1, recv1, hop_send, hop_recv, send2, recv2,
):
    me = lax.axis_index("blk")
    seg = lax.axis_index("segment")
    above, below = lax.rem(seg + 1, SEGS), lax.rem(seg + SEGS - 1, SEGS)
    near = (above, below)
    greet(me, near)
    grads = local_grads(walker_ref, x_ref, gain_ref, g_ref, w_ref)
    head_tiles(lambda t, b: qkv_ref[b, 3 * walker_ref[2] + t], k_nat, q_all, v_all)
    all_in(near)
    first = send_parts(me, parts_ref, stash_ref, send1, recv1)
    row_sums(list_ref, count_ref, k_nat, q_all, lse_ref)
    for c in first:
        c.wait_recv()
    signal(ready, {"segment": above})
    cot = grads(stash_ref)
    cot_ref[...] = cot
    last_g = fc_ref[walker_ref[1]].astype(F32)
    g_below = jnp.where(seg == 0, last_g, cot.astype(F32)).astype(BF16)
    g_own[...] = g_below
    dout_own[...] = mm(w_below_ref[...], g_below).astype(BF16).reshape(HEADS, DH, ROWS)
    pl.semaphore_wait(ready, 1)
    second = [
        copy_to(
            dout_own.at[peer], dout_ref.at[me], send2.at[k], recv2.at[k],
            {"segment": below, "blk": peer},
        )
        for k, peer in enumerate(blocks_from(me))
    ]
    second.append(copy_to(g_own, gnext_ref, hop_send, hop_recv, {"segment": below}))
    for c in second:
        c.start()
    attend_rows(list_ref, count_ref, k_nat, q_all, v_all, lse_ref, att_ref)
    for c in second:
        c.wait()
    for c in first:
        c.wait_send()


def last_step_kernel(
    walker_ref, parts_ref, x_ref, gain_ref, g_ref, w_ref, cot_ref, stash_ref, send1, recv1
):
    me = lax.axis_index("blk")
    greet(me)
    grads = local_grads(walker_ref, x_ref, gain_ref, g_ref, w_ref)
    all_in()
    first = send_parts(me, parts_ref, stash_ref, send1, recv1)
    for c in first:
        c.wait()
    cot_ref[...] = grads(stash_ref)


TILE = jax.ShapeDtypeStruct((WIDTH, ROWS), BF16)
STASH = jax.ShapeDtypeStruct((HEADS, 4, DH, ROWS), BF16)
ATTENDED = jax.ShapeDtypeStruct((BLKS, DH, ROWS), BF16)
LOG_SUMS = jax.ShapeDtypeStruct((BLKS, 1, ROWS), F32)
HEAD_TILES = [
    pltpu.VMEM((BLKS, ROWS, DH), BF16),
    pltpu.VMEM((BLKS, DH, ROWS), BF16),
    pltpu.VMEM((BLKS, DH, ROWS), BF16),
]


def step(picks, pair_list, pair_count, parts, x_t, gain_col, g, fc_t, weights, w_below, qkv):
    sems = pltpu.SemaphoreType.DMA((BLKS - 1,))
    more = pltpu.SemaphoreType.DMA((BLKS,))
    return pl.pallas_call(
        step_kernel,
        out_shape=(TILE, STASH, TILE, ATTENDED, ATTENDED, LOG_SUMS),
        in_specs=[SMEM_SPEC] * 3 + [VMEM_SPEC] * 8,
        out_specs=[VMEM_SPEC] * 6,
        scratch_shapes=HEAD_TILES
        + [
            pltpu.VMEM((WIDTH, ROWS), BF16),
            pltpu.VMEM((HEADS, DH, ROWS), BF16),
            pltpu.SemaphoreType.REGULAR,
            sems,
            sems,
            pltpu.SemaphoreType.DMA,
            pltpu.SemaphoreType.DMA,
            more,
            more,
        ],
        compiler_params=pltpu.CompilerParams(
            collective_id=2, has_side_effects=True, vmem_limit_bytes=24 << 20
        ),
        name="step",
    )(picks, pair_list, pair_count, parts, x_t, gain_col, g, fc_t, weights, w_below, qkv)


def last_step(picks, parts, x_t, gain_col, g, weights):
    sems = pltpu.SemaphoreType.DMA((BLKS - 1,))
    return pl.pallas_call(
        last_step_kernel,
        out_shape=(TILE, STASH),
        in_specs=[SMEM_SPEC] + [VMEM_SPEC] * 5,
        out_specs=[VMEM_SPEC] * 2,
        scratch_shapes=[sems, sems],
        compiler_params=pltpu.CompilerParams(
            collective_id=1, has_side_effects=True, vmem_limit_bytes=16 << 20
        ),
        name="last_step",
    )(picks, parts, x_t, gain_col, g, weights)


def prepare_kernel(x_ref, fc_ref, w_ref, gain_ref, x_out, fc_out, normed_out, qkv_out, turned_w):
    walker = pl.program_id(0)

    @pl.when(walker == 0)
    def _():
        for t in range(3):
            turned_w[t] = turned(w_ref[t])

    x = x_ref[0].astype(F32)
    inv = lax.rsqrt(jnp.mean(x * x, axis=1, keepdims=True) + eps)
    normed = jnp.transpose(x * inv * gain_ref[...]).astype(BF16)
    x_out[0] = jnp.transpose(x).astype(BF16)
    fc = turned(fc_ref[0])
    fc_out[0] = fc
    normed_out[0] = normed

    @pl.when(walker < pl.num_programs(0) - 1)
    def _():
        query = mm(turned_w[0], normed).astype(BF16) * jnp.asarray(0.25, BF16)
        qkv_out[:, 0] = query.reshape(HEADS, DH, ROWS)
        for t in range(1, 3):
            qkv_out[:, t] = mm(turned_w[t], normed).astype(BF16).reshape(HEADS, DH, ROWS)

    @pl.when(walker == pl.num_programs(0) - 1)
    def _():
        first_g = turned(fc_ref[0])
        qkv_out[:, 0] = mm(w_ref[3], first_g).astype(BF16).reshape(HEADS, DH, ROWS)


def prepare(x, fc, weights, gain):
    walkers = x.shape[0]

    def own(w):
        return (lax.rem(w, walkers), 0, 0)

    def tile():
        return pl.BlockSpec((1, WIDTH, ROWS), own)

    flat = jax.ShapeDtypeStruct((walkers, WIDTH, ROWS), BF16)
    return pl.pallas_call(
        prepare_kernel,
        grid=(walkers + 1,),
        in_specs=[
            pl.BlockSpec((1, ROWS, WIDTH), own),
            pl.BlockSpec((1, ROWS, WIDTH), own),
            pl.BlockSpec((4, WIDTH, WIDTH), lambda w: (0, 0, 0)),
            pl.BlockSpec((1, WIDTH), lambda w: (0, 0)),
        ],
        out_specs=[
            tile(),
            tile(),
            tile(),
            pl.BlockSpec((HEADS, 3, DH, ROWS), lambda w: (0, w, 0, 0)),
        ],
        out_shape=(
            flat,
            flat,
            flat,
            jax.ShapeDtypeStruct((HEADS, 3 * walkers + 1, DH, ROWS), BF16),
        ),
        scratch_shapes=[pltpu.VMEM((3, WIDTH, WIDTH), BF16)],
        compiler_params=pltpu.CompilerParams(vmem_limit_bytes=48 << 20),
        name="prepare",
    )(x, fc, weights, gain)


def turned(tile):
    return jnp.transpose(tile.astype(F32)).astype(BF16)


def head_tiles(tile, k_nat, q_all, v_all):
    for b in range(BLKS):
        k_nat[b] = turned(tile(1, b))
        q_all[b] = tile(0, b)
        v_all[b] = tile(2, b)


def slots(n, list_ref):
    a = [2 * n + c // MAXN for c in range(2 * MAXN)]
    return [(a[c], c % MAXN, list_ref[a[c], c % MAXN]) for c in range(2 * MAXN)]


def row_sums(list_ref, count_ref, k_nat, q_all, lse_ref):
    def body(n, carry):
        some = slots(n, list_ref)
        scores = [mm(k_nat[j], q_all[a]) for a, _, j in some]
        parts = [jnp.sum(jnp.exp(s).reshape(ROWS // 8, 8, ROWS), axis=0) for s in scores]
        parts = [
            jnp.where(c < count_ref[a], part, 0.0) for part, (a, c, _) in zip(parts, some)
        ]
        for u in range(2):
            row = parts[u * MAXN]
            for part in parts[u * MAXN + 1 : (u + 1) * MAXN]:
                row = row + part
            lse_ref[2 * n + u] = jnp.log(jnp.sum(row, axis=0, keepdims=True))
        return carry

    lax.fori_loop(0, BLKS // 2, body, 0)


def attend_rows(list_ref, count_ref, k_nat, q_all, v_all, lse_ref, att_ref):
    def body(n, carry):
        some = slots(n, list_ref)
        scores = [mm(k_nat[j], q_all[a]) for a, _, j in some]
        shifts = [lse_ref[a] + jnp.where(c < count_ref[a], 0.0, 1e30) for a, c, _ in some]
        probs = [jnp.exp(s - shift).astype(BF16) for s, shift in zip(scores, shifts)]
        parts = [mm(v_all[j], p) for p, (_, _, j) in zip(probs, some)]
        for u in range(2):
            row = parts[u * MAXN]
            for part in parts[u * MAXN + 1 : (u + 1) * MAXN]:
                row = row + part
            att_ref[2 * n + u] = row.astype(BF16)
        return carry

    lax.fori_loop(0, BLKS // 2, body, 0)


def forward_kernel(list_ref, count_ref, qkv_ref, att_ref, lse_ref, info_ref, k_nat, q_all, v_all):
    def note(n, place):
        c, a = n // BLKS, lax.rem(n, BLKS)
        info_ref[place] = a
        info_ref[PAIRS + place] = list_ref[a, c]
        return place + jnp.where(c < count_ref[a], 1, 0)

    used = lax.fori_loop(0, BLKS * MAXN, note, 0)
    for k in range(GROUP):
        info_ref[used + k] = DUMMY
        info_ref[PAIRS + used + k] = 0
    info_ref[2 * PAIRS] = (used + GROUP - 1) // GROUP
    head_tiles(lambda t, b: qkv_ref[b, t], k_nat, q_all, v_all)
    row_sums(list_ref, count_ref, k_nat, q_all, lse_ref)
    attend_rows(list_ref, count_ref, k_nat, q_all, v_all, lse_ref, att_ref)


def forward(pair_list, pair_count, qkv):
    return pl.pallas_call(
        forward_kernel,
        grid=(1,),
        in_specs=[
            SMEM_SPEC,
            SMEM_SPEC,
            pl.BlockSpec((BLKS, 3, DH, ROWS), lambda i: (0, 0, 0, 0)),
        ],
        out_specs=[
            pl.BlockSpec((BLKS, DH, ROWS), lambda i: (0, 0, 0)),
            pl.BlockSpec((BLKS, 1, ROWS), lambda i: (0, 0, 0)),
            SMEM_SPEC,
        ],
        out_shape=(ATTENDED, LOG_SUMS, jax.ShapeDtypeStruct((2 * PAIRS + 1,), jnp.int32)),
        scratch_shapes=HEAD_TILES,
        compiler_params=pltpu.CompilerParams(vmem_limit_bytes=24 << 20),
        name="forward",
    )(pair_list, pair_count, qkv)


def filing(slot, tiles, shelves, sems):
    return [
        pltpu.make_async_copy(tile, shelf.at[slot], sems.at[k])
        for k, (tile, shelf) in enumerate(zip(tiles, shelves))
    ]


def backward_kernel(mode, info_ref, picks_ref, qkv_ref, att_ref, lse_ref, dout_ref, *refs):
    tiles, refs = (refs[:3], refs[3:]) if mode else ((), refs)
    refs = refs[3:] if mode == 2 else refs
    out_ref, refs = refs[0], refs[1:]
    shelves, refs = (refs[:3], refs[3:]) if mode else ((), refs)
    kv_nat, q_dout, lse, delta, dq, dkv, sems = refs
    copies = filing(picks_ref[3], tiles, shelves, sems)
    for c in copies:
        c.start()
    base = 3 * picks_ref[0]
    nothing = jnp.zeros((DH, ROWS), BF16)
    for b in range(BLKS):
        kv_nat[b] = turned(jnp.concatenate([qkv_ref[b, base + 1], qkv_ref[b, base + 2]], axis=0))
        q_dout[b, 0:DH, 0:ROWS] = qkv_ref[b, base]
        q_dout[b, 0:DH, ROWS : 2 * ROWS] = nothing
        q_dout[b, DH : 2 * DH, 0:ROWS] = nothing
        q_dout[b, DH : 2 * DH, ROWS : 2 * ROWS] = dout_ref[b]
        lse[b] = lse_ref[b]
        delta[b] = jnp.sum(
            dout_ref[b].astype(F32) * att_ref[b].astype(F32), axis=0, keepdims=True
        )
    q_dout[DUMMY] = jnp.zeros((2 * DH, 2 * ROWS), BF16)
    lse[DUMMY] = jnp.full((1, ROWS), 1e30, F32)
    delta[DUMMY] = jnp.zeros((1, ROWS), F32)
    dq[...] = jnp.zeros_like(dq)
    dkv[...] = jnp.zeros_like(dkv)

    def body(n, carry):
        pairs = [(info_ref[n * GROUP + u], info_ref[PAIRS + n * GROUP + u]) for u in range(GROUP)]
        sides = [q_dout[a] for a, _ in pairs]
        boths = [mm(kv_nat[j], side) for (_, j), side in zip(pairs, sides)]
        probs = [jnp.exp(both[:, 0:ROWS] - lse[a]) for both, (a, _) in zip(boths, pairs)]
        score_grads = [
            (prob * (both[:, ROWS : 2 * ROWS] - delta[a])).astype(BF16)
            for prob, both, (a, _) in zip(probs, boths, pairs)
        ]
        kv_parts = [
            mm_nt(side, jnp.concatenate([score_grad, prob.astype(BF16)], axis=1))
            for side, score_grad, prob in zip(sides, score_grads, probs)
        ]
        q_parts = [
            mm(qkv_ref[j, base + 1], score_grad)
            for (_, j), score_grad in zip(pairs, score_grads)
        ]
        for (a, j), kv_part, q_part in zip(pairs, kv_parts, q_parts):
            dkv[j] += kv_part
            dq[a] += q_part
        return carry

    lax.fori_loop(0, info_ref[2 * PAIRS], body, 0)
    for b in range(BLKS):
        out_ref[b, 0] = (dq[b] * 0.25).astype(BF16)
        out_ref[b, 1] = dkv[b, 0:DH].astype(BF16)
        out_ref[b, 2] = dkv[b, DH : 2 * DH].astype(BF16)
        out_ref[b, 3] = att_ref[b]
    for c in copies:
        c.wait()


SHELF_SPEC = pl.BlockSpec(memory_space=pl.ANY)


def shelf_shapes(walkers):
    return tuple(
        jax.ShapeDtypeStruct((walkers + 1,) + t.shape, t.dtype) for t in (TILE, TILE, STASH)
    )


def backward(info, picks, qkv, att, lse, dout, walkers, tiles=None, shelves=None):
    mode = 0 if tiles is None else 1 if shelves is None else 2
    outs = shelf_shapes(walkers) if mode else ()
    result = pl.pallas_call(
        partial(backward_kernel, mode),
        in_specs=[SMEM_SPEC] * 2
        + [VMEM_SPEC] * (7 if mode else 4)
        + [SHELF_SPEC] * (3 if mode == 2 else 0),
        out_specs=(VMEM_SPEC,) + (SHELF_SPEC,) * len(outs),
        out_shape=(STASH,) + outs,
        input_output_aliases={9: 1, 10: 2, 11: 3} if mode == 2 else {},
        scratch_shapes=[
            pltpu.VMEM((BLKS, ROWS, 2 * DH), BF16),
            pltpu.VMEM((BLKS + 1, 2 * DH, 2 * ROWS), BF16),
            pltpu.VMEM((BLKS + 1, 1, ROWS), F32),
            pltpu.VMEM((BLKS + 1, 1, ROWS), F32),
            pltpu.VMEM((BLKS + 1, DH, ROWS), F32),
            pltpu.VMEM((BLKS, 2 * DH, ROWS), F32),
            pltpu.SemaphoreType.DMA((3,)),
        ],
        compiler_params=pltpu.CompilerParams(vmem_limit_bytes=16 << 20),
        name="backward",
    )(info, picks, qkv, att, lse, dout, *(tiles or ()), *(shelves or ()))
    return result[0], result[1:]


def file_kernel(picks_ref, *refs):
    copies = filing(picks_ref[4], refs[:3], refs[6:9], refs[9])
    for c in copies:
        c.start()
    for c in copies:
        c.wait()


def file_last(picks, tiles, shelves, walkers):
    return pl.pallas_call(
        file_kernel,
        in_specs=[SMEM_SPEC] + [VMEM_SPEC] * 3 + [SHELF_SPEC] * 3,
        out_specs=(SHELF_SPEC,) * 3,
        out_shape=shelf_shapes(walkers),
        input_output_aliases={4: 0, 5: 1, 6: 2},
        scratch_shapes=[pltpu.SemaphoreType.DMA((3,))],
        name="file_last",
    )(picks, *tiles, *shelves)


def per_device(layer_inputs, final_cot, attn_weights, norm_gain, pair_list, pair_count):
    seg = lax.axis_index("segment")
    walkers = layer_inputs.shape[1]
    weights = attn_weights[0]
    gain_col = norm_gain[0][:, None]
    x_t, fc_t, normed, qkv = prepare(layer_inputs[0], final_cot, weights, norm_gain)
    qkv, w_below = swap(qkv, weights[3])
    dout = qkv[:, 3 * walkers]
    g = fc_t[0]
    att, lse, info = forward(pair_list, pair_count, qkv)

    ticks = walkers + SEGS - 1
    tiles = shelves = None
    for tick in range(ticks):
        first = tick - (SEGS - 1 - seg)
        picks = jnp.stack([first, jnp.int32(tick + 1), first + 1, first - 1, first])
        most = jnp.array([walkers - 1] * 3 + [walkers] * 2, jnp.int32)
        picks = jnp.minimum(jnp.maximum(picks, 0), most).astype(jnp.int32)
        parts, shelves = backward(info, picks, qkv, att, lse, dout, walkers, tiles, shelves or None)
        if tick < ticks - 1:
            cot, stash, gnext, dout, att, lse = step(
                picks, pair_list, pair_count, parts, x_t, gain_col, g, fc_t, weights, w_below, qkv
            )
        else:
            cot, stash = last_step(picks, parts, x_t, gain_col, g, weights)
        tiles = (cot, g, stash)
        g = gnext
    filed = [shelf[:walkers] for shelf in file_last(picks, tiles, shelves, walkers)]
    cot_all, summed, gain_sum = close(normed, x_t, weights, tiles, filed)
    grad_total = summed.reshape(4, WIDTH, WIDTH).astype(F32)
    return (cot_all[None], grad_total[None], gain_sum[:1])


def solution(mesh):
    return jax.shard_map(
        per_device,
        mesh=mesh,
        in_specs=(
            P("segment", None, "blk", None),
            P(None, "blk", None),
            P("segment", None, None, None),
            P("segment", None),
            P(),
            P(),
        ),
        out_specs=(
            P("segment", None, "blk", None),
            P("segment", None, None, None),
            P("segment", None),
        ),
        check_vma=False,
    )
```

```python
from functools import partial

import jax
import jax.numpy as jnp
from jax import lax
from jax.experimental import pallas as pl
from jax.experimental.pallas import tpu as pltpu
from jax.sharding import PartitionSpec as P

HEADS = 16
DH = 16
BLKS = 16
SEGS = 8
ROWS = 128
WIDTH = 256
GROUP = 16
MAXN = 8
PAIRS = BLKS * MAXN + GROUP
DUMMY = BLKS
eps = 1e-05
F32, BF16 = jnp.float32, jnp.bfloat16
VMEM_SPEC = pl.BlockSpec(memory_space=pltpu.VMEM)
SMEM_SPEC = pl.BlockSpec(memory_space=pltpu.SMEM)


def mm(a, b):
    return jnp.dot(a, b, preferred_element_type=F32)


def mm_nt(a, b):
    return lax.dot_general(a, b, (((1,), (1,)), ((), ())), preferred_element_type=F32)


SIDE = 4
SHIFTS = sorted(
    [(dx, dy) for dx in range(SIDE) for dy in range(SIDE)],
    key=lambda s: -min(s[0], SIDE - s[0]) - min(s[1], SIDE - s[1]),
)


def blocks_from(me):
    x, y = me // SIDE, lax.rem(me, SIDE)
    return [lax.rem(x + dx, SIDE) * SIDE + lax.rem(y + dy, SIDE) for dx, dy in SHIFTS]


def peers(me):
    return blocks_from(me)[: BLKS - 1]


def signal(semaphore, where):
    pl.semaphore_signal(semaphore, inc=1, device_id=where, device_id_type=pl.DeviceIdType.MESH)


def greet(me, more=()):
    barrier = pltpu.get_barrier_semaphore()
    for peer in peers(me):
        signal(barrier, {"blk": peer})
    for seg in more:
        signal(barrier, {"segment": seg})


def all_in(more=()):
    pl.semaphore_wait(pltpu.get_barrier_semaphore(), BLKS - 1 + len(more))


def copy_to(src, dst, send, recv, where):
    return pltpu.make_async_remote_copy(
        src_ref=src,
        dst_ref=dst,
        send_sem=send,
        recv_sem=recv,
        device_id=where,
        device_id_type=pl.DeviceIdType.MESH,
    )


def swap_kernel(in_ref, w_ref, out_ref, below_ref, send, recv, w_send, w_recv):
    me = lax.axis_index("blk")
    seg = lax.axis_index("segment")
    above, below = lax.rem(seg + 1, SEGS), lax.rem(seg + SEGS - 1, SEGS)
    greet(me, (below,))
    all_in((above,))
    copies = [
        copy_to(in_ref.at[peer], out_ref.at[me], send.at[k], recv.at[k], {"blk": peer})
        for k, peer in enumerate(peers(me))
    ]
    copies.append(copy_to(w_ref, below_ref, w_send, w_recv, {"segment": above}))
    for c in copies:
        c.start()
    out_ref[me] = in_ref[me]
    for c in copies:
        c.wait()


def swap(values, w_out):
    sems = pltpu.SemaphoreType.DMA((BLKS - 1,))
    return pl.pallas_call(
        swap_kernel,
        out_shape=(
            jax.ShapeDtypeStruct(values.shape, values.dtype),
            jax.ShapeDtypeStruct(w_out.shape, w_out.dtype),
        ),
        in_specs=[VMEM_SPEC] * 2,
        out_specs=[VMEM_SPEC] * 2,
        scratch_shapes=[sems, sems, pltpu.SemaphoreType.DMA, pltpu.SemaphoreType.DMA],
        compiler_params=pltpu.CompilerParams(
            collective_id=0, has_side_effects=True, vmem_limit_bytes=16 << 20
        ),
        name="swap",
    )(values, w_out)


def close_kernel(
    normed_ref, x_ref, w_ref, cot_last, g_last, stash_last, cot_ref, g_ref, stash_ref,
    cots_ref, out_ref, gain_out,
    mine, parts, got, own, gain_own, got_gain, send1, recv1, send2, recv2, send3, recv3,
):
    me = lax.axis_index("blk")
    seg = lax.axis_index("segment")
    walkers = normed_ref.shape[0]
    greet(me)

    def newest(last_ref, shelf_ref):
        old = shelf_ref[walkers - 1].astype(F32)
        return jnp.where(seg == 0, last_ref[...].astype(F32), old).astype(BF16)

    mine[...] = newest(stash_last, stash_ref)
    g_new = newest(g_last, g_ref)

    def grads(w, t):
        tile = mine[:, t] if w == walkers - 1 else stash_ref[w, :, t]
        return tile.reshape(WIDTH, ROWS)

    for t in range(4):
        product = jnp.zeros((WIDTH, WIDTH), F32)
        for w in range(walkers):
            if t < 3:
                product += mm_nt(normed_ref[w], grads(w, t))
            else:
                product += mm_nt(grads(w, 3), g_new if w == walkers - 1 else g_ref[w])
        rows = WIDTH * 4 // BLKS
        parts[4 * t : 4 * t + 4] = product.astype(BF16).reshape(4, rows, WIDTH)
    gain = jnp.zeros((WIDTH, ROWS), F32)
    for w in range(walkers):
        x = x_ref[w].astype(F32)
        unit = x * lax.rsqrt(jnp.mean(x * x, axis=0, keepdims=True) + eps)
        normed_grad = mm(w_ref[0], grads(w, 0)) + mm(w_ref[1], grads(w, 1)) + mm(w_ref[2], grads(w, 2))
        gain += normed_grad * unit
    row = jnp.sum(jnp.transpose(gain), axis=0, keepdims=True)
    gain_own[...] = jnp.broadcast_to(row, gain_own.shape)

    all_in()
    first = [
        copy_to(parts.at[peer], got.at[me], send1.at[k], recv1.at[k], {"blk": peer})
        for k, peer in enumerate(peers(me))
    ]
    gains = [
        copy_to(gain_own, got_gain.at[me], send3.at[k], recv3.at[k], {"blk": peer})
        for k, peer in enumerate(peers(me))
    ]
    for c in first:
        c.start()
    for c in gains:
        c.start()
    got[me] = parts[me]
    got_gain[me] = gain_own[...]
    for w in range(walkers - 1):
        cots_ref[w] = turned(cot_ref[w])
    cots_ref[walkers - 1] = turned(newest(cot_last, cot_ref))
    for c in first:
        c.wait_recv()
    acc = got[0].astype(F32)
    for b in range(1, BLKS):
        acc = acc + got[b].astype(F32)
    own[...] = acc.astype(BF16)
    second = [
        copy_to(own, out_ref.at[me], send2.at[k], recv2.at[k], {"blk": peer})
        for k, peer in enumerate(peers(me))
    ]
    for c in second:
        c.start()
    out_ref[me] = own[...]
    for c in gains:
        c.wait()
    gain_out[...] = jnp.sum(got_gain[...], axis=0)
    for c in first:
        c.wait_send()
    for c in second:
        c.wait()


def close(normed, x_t, weights, tiles, shelves):
    sems = pltpu.SemaphoreType.DMA((BLKS - 1,))
    walkers = normed.shape[0]
    chunks = (BLKS, 4 * WIDTH // BLKS, WIDTH)
    return pl.pallas_call(
        close_kernel,
        out_shape=(
            jax.ShapeDtypeStruct((walkers, ROWS, WIDTH), BF16),
            jax.ShapeDtypeStruct(chunks, BF16),
            jax.ShapeDtypeStruct((8, WIDTH), F32),
        ),
        in_specs=[VMEM_SPEC] * 9,
        out_specs=[VMEM_SPEC] * 3,
        scratch_shapes=[
            pltpu.VMEM((HEADS, 4, DH, ROWS), BF16),
            pltpu.VMEM(chunks, BF16),
            pltpu.VMEM(chunks, BF16),
            pltpu.VMEM(chunks[1:], BF16),
            pltpu.VMEM((8, WIDTH), F32),
            pltpu.VMEM((BLKS, 8, WIDTH), F32),
        ]
        + [sems] * 6,
        compiler_params=pltpu.CompilerParams(
            collective_id=3, has_side_effects=True, vmem_limit_bytes=24 << 20
        ),
        name="close",
    )(normed, x_t, weights, *tiles, *shelves)


def local_grads(walker_ref, x_ref, gain_ref, g_ref, w_ref):
    x = x_ref[walker_ref[0]].astype(F32)
    inv = lax.rsqrt(jnp.mean(x * x, axis=0, keepdims=True) + eps)
    unit = x * inv
    g = g_ref[...].astype(F32)

    def finish(stash_ref):
        normed_grad = mm(w_ref[0], stash_ref[:, 0].reshape(WIDTH, ROWS))
        for t in range(1, 3):
            normed_grad += mm(w_ref[t], stash_ref[:, t].reshape(WIDTH, ROWS))
        unit_grad = normed_grad * gain_ref[...]
        centre = jnp.mean(unit_grad * unit, axis=0, keepdims=True)
        return (g + inv * (unit_grad - unit * centre)).astype(BF16)

    return finish


def send_parts(me, parts_ref, stash_ref, send, recv):
    copies = [
        copy_to(parts_ref.at[peer], stash_ref.at[me], send.at[k], recv.at[k], {"blk": peer})
        for k, peer in enumerate(peers(me))
    ]
    for c in copies:
        c.start()
    stash_ref[me] = parts_ref[me]
    return copies


def step_kernel(
    walker_ref, list_ref, count_ref, parts_ref, x_ref, gain_ref, g_ref, fc_ref, w_ref, w_below_ref, qkv_ref,
    cot_ref, stash_ref, gnext_ref, dout_ref, att_ref, lse_ref,
    k_nat, q_all, v_all, g_own, dout_own, ready, send1, recv1, hop_send, hop_recv, send2, recv2,
):
    me = lax.axis_index("blk")
    seg = lax.axis_index("segment")
    above, below = lax.rem(seg + 1, SEGS), lax.rem(seg + SEGS - 1, SEGS)
    near = (above, below)
    greet(me, near)
    grads = local_grads(walker_ref, x_ref, gain_ref, g_ref, w_ref)
    head_tiles(lambda t, b: qkv_ref[b, 3 * walker_ref[2] + t], k_nat, q_all, v_all)
    all_in(near)
    first = send_parts(me, parts_ref, stash_ref, send1, recv1)
    row_sums(list_ref, count_ref, k_nat, q_all, lse_ref)
    for c in first:
        c.wait_recv()
    signal(ready, {"segment": above})
    cot = grads(stash_ref)
    cot_ref[...] = cot
    last_g = fc_ref[walker_ref[1]].astype(F32)
    g_below = jnp.where(seg == 0, last_g, cot.astype(F32)).astype(BF16)
    g_own[...] = g_below
    hop = copy_to(g_own, gnext_ref, hop_send, hop_recv, {"segment": below})
    hop.start()
    dout_own[...] = mm(w_below_ref[...], g_below).astype(BF16).reshape(HEADS, DH, ROWS)
    pl.semaphore_wait(ready, 1)
    second = [
        copy_to(
            dout_own.at[peer], dout_ref.at[me], send2.at[k], recv2.at[k],
            {"segment": below, "blk": peer},
        )
        for k, peer in enumerate(blocks_from(me))
    ]
    for c in second:
        c.start()
    attend_rows(list_ref, count_ref, k_nat, q_all, v_all, lse_ref, att_ref)
    for c in second:
        c.wait()
    hop.wait()
    for c in first:
        c.wait_send()


def last_step_kernel(
    walker_ref, parts_ref, x_ref, gain_ref, g_ref, w_ref, cot_ref, stash_ref, send1, recv1
):
    me = lax.axis_index("blk")
    greet(me)
    grads = local_grads(walker_ref, x_ref, gain_ref, g_ref, w_ref)
    all_in()
    first = send_parts(me, parts_ref, stash_ref, send1, recv1)
    for c in first:
        c.wait()
    cot_ref[...] = grads(stash_ref)


TILE = jax.ShapeDtypeStruct((WIDTH, ROWS), BF16)
STASH = jax.ShapeDtypeStruct((HEADS, 4, DH, ROWS), BF16)
ATTENDED = jax.ShapeDtypeStruct((BLKS, DH, ROWS), BF16)
LOG_SUMS = jax.ShapeDtypeStruct((BLKS, 1, ROWS), F32)
HEAD_TILES = [
    pltpu.VMEM((BLKS, ROWS, DH), BF16),
    pltpu.VMEM((BLKS, DH, ROWS), BF16),
    pltpu.VMEM((BLKS, DH, ROWS), BF16),
]


def step(picks, pair_list, pair_count, parts, x_t, gain_col, g, fc_t, weights, w_below, qkv):
    sems = pltpu.SemaphoreType.DMA((BLKS - 1,))
    more = pltpu.SemaphoreType.DMA((BLKS,))
    return pl.pallas_call(
        step_kernel,
        out_shape=(TILE, STASH, TILE, ATTENDED, ATTENDED, LOG_SUMS),
        in_specs=[SMEM_SPEC] * 3 + [VMEM_SPEC] * 8,
        out_specs=[VMEM_SPEC] * 6,
        scratch_shapes=HEAD_TILES
        + [
            pltpu.VMEM((WIDTH, ROWS), BF16),
            pltpu.VMEM((HEADS, DH, ROWS), BF16),
            pltpu.SemaphoreType.REGULAR,
            sems,
            sems,
            pltpu.SemaphoreType.DMA,
            pltpu.SemaphoreType.DMA,
            more,
            more,
        ],
        compiler_params=pltpu.CompilerParams(
            collective_id=2, has_side_effects=True, vmem_limit_bytes=24 << 20
        ),
        name="step",
    )(picks, pair_list, pair_count, parts, x_t, gain_col, g, fc_t, weights, w_below, qkv)


def last_step(picks, parts, x_t, gain_col, g, weights):
    sems = pltpu.SemaphoreType.DMA((BLKS - 1,))
    return pl.pallas_call(
        last_step_kernel,
        out_shape=(TILE, STASH),
        in_specs=[SMEM_SPEC] + [VMEM_SPEC] * 5,
        out_specs=[VMEM_SPEC] * 2,
        scratch_shapes=[sems, sems],
        compiler_params=pltpu.CompilerParams(
            collective_id=1, has_side_effects=True, vmem_limit_bytes=16 << 20
        ),
        name="last_step",
    )(picks, parts, x_t, gain_col, g, weights)


def prepare_kernel(x_ref, fc_ref, w_ref, gain_ref, x_out, fc_out, normed_out, qkv_out, turned_w):
    walker = pl.program_id(0)

    @pl.when(walker == 0)
    def _():
        for t in range(3):
            turned_w[t] = turned(w_ref[t])

    x = x_ref[0].astype(F32)
    inv = lax.rsqrt(jnp.mean(x * x, axis=1, keepdims=True) + eps)
    normed = jnp.transpose(x * inv * gain_ref[...]).astype(BF16)
    x_out[0] = jnp.transpose(x).astype(BF16)
    fc = turned(fc_ref[0])
    fc_out[0] = fc
    normed_out[0] = normed

    @pl.when(walker < pl.num_programs(0) - 1)
    def _():
        query = mm(turned_w[0], normed).astype(BF16) * jnp.asarray(0.25, BF16)
        qkv_out[:, 0] = query.reshape(HEADS, DH, ROWS)
        for t in range(1, 3):
            qkv_out[:, t] = mm(turned_w[t], normed).astype(BF16).reshape(HEADS, DH, ROWS)

    @pl.when(walker == pl.num_programs(0) - 1)
    def _():
        first_g = turned(fc_ref[0])
        qkv_out[:, 0] = mm(w_ref[3], first_g).astype(BF16).reshape(HEADS, DH, ROWS)


def prepare(x, fc, weights, gain):
    walkers = x.shape[0]

    def own(w):
        return (lax.rem(w, walkers), 0, 0)

    def tile():
        return pl.BlockSpec((1, WIDTH, ROWS), own)

    flat = jax.ShapeDtypeStruct((walkers, WIDTH, ROWS), BF16)
    return pl.pallas_call(
        prepare_kernel,
        grid=(walkers + 1,),
        in_specs=[
            pl.BlockSpec((1, ROWS, WIDTH), own),
            pl.BlockSpec((1, ROWS, WIDTH), own),
            pl.BlockSpec((4, WIDTH, WIDTH), lambda w: (0, 0, 0)),
            pl.BlockSpec((1, WIDTH), lambda w: (0, 0)),
        ],
        out_specs=[
            tile(),
            tile(),
            tile(),
            pl.BlockSpec((HEADS, 3, DH, ROWS), lambda w: (0, w, 0, 0)),
        ],
        out_shape=(
            flat,
            flat,
            flat,
            jax.ShapeDtypeStruct((HEADS, 3 * walkers + 1, DH, ROWS), BF16),
        ),
        scratch_shapes=[pltpu.VMEM((3, WIDTH, WIDTH), BF16)],
        compiler_params=pltpu.CompilerParams(vmem_limit_bytes=48 << 20),
        name="prepare",
    )(x, fc, weights, gain)


def turned(tile):
    return jnp.transpose(tile.astype(F32)).astype(BF16)


def head_tiles(tile, k_nat, q_all, v_all):
    for b in range(BLKS):
        k_nat[b] = turned(tile(1, b))
        q_all[b] = tile(0, b)
        v_all[b] = tile(2, b)


def slots(n, list_ref):
    a = [2 * n + c // MAXN for c in range(2 * MAXN)]
    return [(a[c], c % MAXN, list_ref[a[c], c % MAXN]) for c in range(2 * MAXN)]


def row_sums(list_ref, count_ref, k_nat, q_all, lse_ref):
    def body(n, carry):
        some = slots(n, list_ref)
        scores = [mm(k_nat[j], q_all[a]) for a, _, j in some]
        parts = [jnp.sum(jnp.exp(s).reshape(ROWS // 8, 8, ROWS), axis=0) for s in scores]
        parts = [
            jnp.where(c < count_ref[a], part, 0.0) for part, (a, c, _) in zip(parts, some)
        ]
        for u in range(2):
            row = parts[u * MAXN]
            for part in parts[u * MAXN + 1 : (u + 1) * MAXN]:
                row = row + part
            lse_ref[2 * n + u] = jnp.log(jnp.sum(row, axis=0, keepdims=True))
        return carry

    lax.fori_loop(0, BLKS // 2, body, 0)


def attend_rows(list_ref, count_ref, k_nat, q_all, v_all, lse_ref, att_ref):
    def body(n, carry):
        some = slots(n, list_ref)
        scores = [mm(k_nat[j], q_all[a]) for a, _, j in some]
        shifts = [lse_ref[a] + jnp.where(c < count_ref[a], 0.0, 1e30) for a, c, _ in some]
        probs = [jnp.exp(s - shift).astype(BF16) for s, shift in zip(scores, shifts)]
        parts = [mm(v_all[j], p) for p, (_, _, j) in zip(probs, some)]
        for u in range(2):
            row = parts[u * MAXN]
            for part in parts[u * MAXN + 1 : (u + 1) * MAXN]:
                row = row + part
            att_ref[2 * n + u] = row.astype(BF16)
        return carry

    lax.fori_loop(0, BLKS // 2, body, 0)


def forward_kernel(list_ref, count_ref, qkv_ref, att_ref, lse_ref, info_ref, k_nat, q_all, v_all):
    def note(n, place):
        c, a = n // BLKS, lax.rem(n, BLKS)
        info_ref[place] = a
        info_ref[PAIRS + place] = list_ref[a, c]
        return place + jnp.where(c < count_ref[a], 1, 0)

    used = lax.fori_loop(0, BLKS * MAXN, note, 0)
    for k in range(GROUP):
        info_ref[used + k] = DUMMY
        info_ref[PAIRS + used + k] = 0
    info_ref[2 * PAIRS] = (used + GROUP - 1) // GROUP
    head_tiles(lambda t, b: qkv_ref[b, t], k_nat, q_all, v_all)
    row_sums(list_ref, count_ref, k_nat, q_all, lse_ref)
    attend_rows(list_ref, count_ref, k_nat, q_all, v_all, lse_ref, att_ref)


def forward(pair_list, pair_count, qkv):
    return pl.pallas_call(
        forward_kernel,
        grid=(1,),
        in_specs=[
            SMEM_SPEC,
            SMEM_SPEC,
            pl.BlockSpec((BLKS, 3, DH, ROWS), lambda i: (0, 0, 0, 0)),
        ],
        out_specs=[
            pl.BlockSpec((BLKS, DH, ROWS), lambda i: (0, 0, 0)),
            pl.BlockSpec((BLKS, 1, ROWS), lambda i: (0, 0, 0)),
            SMEM_SPEC,
        ],
        out_shape=(ATTENDED, LOG_SUMS, jax.ShapeDtypeStruct((2 * PAIRS + 1,), jnp.int32)),
        scratch_shapes=HEAD_TILES,
        compiler_params=pltpu.CompilerParams(vmem_limit_bytes=24 << 20),
        name="forward",
    )(pair_list, pair_count, qkv)


def filing(slot, tiles, shelves, sems):
    return [
        pltpu.make_async_copy(tile, shelf.at[slot], sems.at[k])
        for k, (tile, shelf) in enumerate(zip(tiles, shelves))
    ]


def backward_kernel(mode, info_ref, picks_ref, qkv_ref, att_ref, lse_ref, dout_ref, *refs):
    tiles, refs = (refs[:3], refs[3:]) if mode else ((), refs)
    refs = refs[3:] if mode == 2 else refs
    out_ref, refs = refs[0], refs[1:]
    shelves, refs = (refs[:3], refs[3:]) if mode else ((), refs)
    kv_nat, q_dout, lse, delta, dq, dkv, sems = refs
    copies = filing(picks_ref[3], tiles, shelves, sems)
    for c in copies:
        c.start()
    base = 3 * picks_ref[0]
    nothing = jnp.zeros((DH, ROWS), BF16)
    for b in range(BLKS):
        kv_nat[b] = turned(jnp.concatenate([qkv_ref[b, base + 1], qkv_ref[b, base + 2]], axis=0))
        q_dout[b, 0:DH, 0:ROWS] = qkv_ref[b, base]
        q_dout[b, 0:DH, ROWS : 2 * ROWS] = nothing
        q_dout[b, DH : 2 * DH, 0:ROWS] = nothing
        q_dout[b, DH : 2 * DH, ROWS : 2 * ROWS] = dout_ref[b]
        lse[b] = lse_ref[b]
        delta[b] = jnp.sum(
            dout_ref[b].astype(F32) * att_ref[b].astype(F32), axis=0, keepdims=True
        )
    q_dout[DUMMY] = jnp.zeros((2 * DH, 2 * ROWS), BF16)
    lse[DUMMY] = jnp.full((1, ROWS), 1e30, F32)
    delta[DUMMY] = jnp.zeros((1, ROWS), F32)
    dq[...] = jnp.zeros_like(dq)
    dkv[...] = jnp.zeros_like(dkv)

    def body(n, carry):
        pairs = [(info_ref[n * GROUP + u], info_ref[PAIRS + n * GROUP + u]) for u in range(GROUP)]
        sides = [q_dout[a] for a, _ in pairs]
        boths = [mm(kv_nat[j], side) for (_, j), side in zip(pairs, sides)]
        probs = [jnp.exp(both[:, 0:ROWS] - lse[a]) for both, (a, _) in zip(boths, pairs)]
        score_grads = [
            (prob * (both[:, ROWS : 2 * ROWS] - delta[a])).astype(BF16)
            for prob, both, (a, _) in zip(probs, boths, pairs)
        ]
        kv_parts = [
            mm_nt(side, jnp.concatenate([score_grad, prob.astype(BF16)], axis=1))
            for side, score_grad, prob in zip(sides, score_grads, probs)
        ]
        q_parts = [
            mm(qkv_ref[j, base + 1], score_grad)
            for (_, j), score_grad in zip(pairs, score_grads)
        ]
        for (a, j), kv_part, q_part in zip(pairs, kv_parts, q_parts):
            dkv[j] += kv_part
            dq[a] += q_part
        return carry

    lax.fori_loop(0, info_ref[2 * PAIRS], body, 0)
    for b in range(BLKS):
        out_ref[b, 0] = (dq[b] * 0.25).astype(BF16)
        out_ref[b, 1] = dkv[b, 0:DH].astype(BF16)
        out_ref[b, 2] = dkv[b, DH : 2 * DH].astype(BF16)
        out_ref[b, 3] = att_ref[b]
    for c in copies:
        c.wait()


SHELF_SPEC = pl.BlockSpec(memory_space=pl.ANY)


def shelf_shapes(walkers):
    return tuple(
        jax.ShapeDtypeStruct((walkers + 1,) + t.shape, t.dtype) for t in (TILE, TILE, STASH)
    )


def backward(info, picks, qkv, att, lse, dout, walkers, tiles=None, shelves=None):
    mode = 0 if tiles is None else 1 if shelves is None else 2
    outs = shelf_shapes(walkers) if mode else ()
    result = pl.pallas_call(
        partial(backward_kernel, mode),
        in_specs=[SMEM_SPEC] * 2
        + [VMEM_SPEC] * (7 if mode else 4)
        + [SHELF_SPEC] * (3 if mode == 2 else 0),
        out_specs=(VMEM_SPEC,) + (SHELF_SPEC,) * len(outs),
        out_shape=(STASH,) + outs,
        input_output_aliases={9: 1, 10: 2, 11: 3} if mode == 2 else {},
        scratch_shapes=[
            pltpu.VMEM((BLKS, ROWS, 2 * DH), BF16),
            pltpu.VMEM((BLKS + 1, 2 * DH, 2 * ROWS), BF16),
            pltpu.VMEM((BLKS + 1, 1, ROWS), F32),
            pltpu.VMEM((BLKS + 1, 1, ROWS), F32),
            pltpu.VMEM((BLKS + 1, DH, ROWS), F32),
            pltpu.VMEM((BLKS, 2 * DH, ROWS), F32),
            pltpu.SemaphoreType.DMA((3,)),
        ],
        compiler_params=pltpu.CompilerParams(vmem_limit_bytes=16 << 20),
        name="backward",
    )(info, picks, qkv, att, lse, dout, *(tiles or ()), *(shelves or ()))
    return result[0], result[1:]


def file_kernel(picks_ref, *refs):
    copies = filing(picks_ref[4], refs[:3], refs[6:9], refs[9])
    for c in copies:
        c.start()
    for c in copies:
        c.wait()


def file_last(picks, tiles, shelves, walkers):
    return pl.pallas_call(
        file_kernel,
        in_specs=[SMEM_SPEC] + [VMEM_SPEC] * 3 + [SHELF_SPEC] * 3,
        out_specs=(SHELF_SPEC,) * 3,
        out_shape=shelf_shapes(walkers),
        input_output_aliases={4: 0, 5: 1, 6: 2},
        scratch_shapes=[pltpu.SemaphoreType.DMA((3,))],
        name="file_last",
    )(picks, *tiles, *shelves)


def per_device(layer_inputs, final_cot, attn_weights, norm_gain, pair_list, pair_count):
    seg = lax.axis_index("segment")
    walkers = layer_inputs.shape[1]
    weights = attn_weights[0]
    gain_col = norm_gain[0][:, None]
    x_t, fc_t, normed, qkv = prepare(layer_inputs[0], final_cot, weights, norm_gain)
    qkv, w_below = swap(qkv, weights[3])
    dout = qkv[:, 3 * walkers]
    g = fc_t[0]
    att, lse, info = forward(pair_list, pair_count, qkv)

    ticks = walkers + SEGS - 1
    tiles = shelves = None
    for tick in range(ticks):
        first = tick - (SEGS - 1 - seg)
        picks = jnp.stack([first, jnp.int32(tick + 1), first + 1, first - 1, first])
        most = jnp.array([walkers - 1] * 3 + [walkers] * 2, jnp.int32)
        picks = jnp.minimum(jnp.maximum(picks, 0), most).astype(jnp.int32)
        parts, shelves = backward(info, picks, qkv, att, lse, dout, walkers, tiles, shelves or None)
        if tick < ticks - 1:
            cot, stash, gnext, dout, att, lse = step(
                picks, pair_list, pair_count, parts, x_t, gain_col, g, fc_t, weights, w_below, qkv
            )
        else:
            cot, stash = last_step(picks, parts, x_t, gain_col, g, weights)
        tiles = (cot, g, stash)
        g = gnext
    filed = [shelf[:walkers] for shelf in file_last(picks, tiles, shelves, walkers)]
    cot_all, summed, gain_sum = close(normed, x_t, weights, tiles, filed)
    grad_total = summed.reshape(4, WIDTH, WIDTH).astype(F32)
    return (cot_all[None], grad_total[None], gain_sum[:1])


def solution(mesh):
    return jax.shard_map(
        per_device,
        mesh=mesh,
        in_specs=(
            P("segment", None, "blk", None),
            P(None, "blk", None),
            P("segment", None, None, None),
            P("segment", None),
            P(),
            P(),
        ),
        out_specs=(
            P("segment", None, "blk", None),
            P("segment", None, None, None),
            P("segment", None),
        ),
        check_vma=False,
    )
```
